256 devices in a mesh: dp: 16 (over x_lo, y, core), mp: 8 (over z), side: 2 (over x_hi).
Axes of the slice: x: 4 (x_hi: 2, x_lo: 2; x = x_hi * 2 + x_lo), y: 4, z: 8, core: 2. Of those that a mesh axis runs over, the one named last changes fastest.
Arguments:
- tokens: bfloat16 [4096, 3072], P('dp', 'mp'), may hold values from -6 to 6
- up_weight: bfloat16 [2, 3072, 6144], P('side', 'dp', 'mp'), may hold values from -0.109375 to 0.109375
- down_weight: bfloat16 [2, 6144, 3072], P('side', 'mp', 'dp'), may hold values from -0.078125 to 0.078125
- mod_table: float32 [2, 50, 3, 3072], P('side'), may hold values from -3 to 3
- timesteps: int32 [16], P('dp'), may hold values from 0 to 49
- valid_counts: int32 [16], replicated, may hold values from 64 to 256, as said below
Outputs:
- block_out: bfloat16 [2, 4096, 3072], P('side', 'dp', 'mp')
- up_grads: float32 [3072, 6144], P(('dp', 'side'), 'mp')
- down_grads: float32 [6144, 3072], P('mp', ('dp', 'side'))
The draws below stay inside these ranges and needn't reach their ends.
Inputs may be any that keep to these rules, and one draw needn't show every extreme that they name: `valid_counts`: every image has at least 64 valid tokens, and in every draw some image has all 256 valid.
All inputs are finite; a program needn't handle non-finite values.
Results may differ from the reference program's by a relative error of at most 0.018.
Values may be sent and summed in bfloat16 or wider, within the bound.
A program may use at most 64 MiB of HBM per device.

```python
import jax
import jax.numpy as jnp
from jax import lax

D = 3072
FFW = 6144
STEPS = 50
SEQ = 256
SAMPLES = 16
TOKENS = 4096
N_DP = 16


def draw_valid_counts(key, part):
    draw_key = jax.random.fold_in(key, 11)
    pick_key = jax.random.fold_in(key, 23)
    counts = jax.random.randint(draw_key, (SAMPLES,), SEQ // 4, SEQ + 1)
    chosen = jax.random.randint(pick_key, (), 0, SAMPLES)
    return jnp.where(jnp.arange(SAMPLES) == chosen, SEQ, counts).astype(jnp.int32)


def set_ends(array, own_key, low, largest):
    place = [jax.random.randint(jax.random.fold_in(own_key, axis), (), 0, length) for axis, length in enumerate(array.shape)]
    widest = array.shape.index(max(array.shape))
    next_to = place[:widest] + [(place[widest] + 1) % array.shape[widest]] + place[widest + 1:]
    return array.at[tuple(place)].set(low).at[tuple(next_to)].set(largest)


def strengthened(entries, own_key, source, target, parts, factor):
    def block_of(dim):
        return (jnp.arange(entries.shape[dim]) // (entries.shape[dim] // parts)).reshape((-1,) + (1,) * (entries.ndim - 1 - dim))

    one_side = jax.random.permutation(own_key, parts)[block_of(target)]
    far = (block_of(target) + parts // 2) % parts
    return jnp.where((block_of(source) == one_side) | (block_of(source) == far), factor * entries, entries)


def level_of(key, shape, pieces, least, high):
    gain = 1.0
    for position, shards_of in pieces:
        steps = jax.random.uniform(jax.random.fold_in(jax.random.fold_in(key, 6), position), (shards_of,), jnp.float32, least / len(pieces), high / len(pieces))
        gain = gain * jnp.repeat(jnp.exp(steps), shape[position] // shards_of).reshape((-1,) + (1,) * (len(shape) - 1 - position))
    return gain


def bell_draw(key, extent, spread, limit, shards=(), kind=jnp.bfloat16):
    level = level_of(key, extent, shards, -0.22, 0.18) if shards else 1.0
    entries = jax.random.normal(key, extent, jnp.float32) * spread * level
    return jnp.minimum(jnp.maximum(entries, -limit), limit).astype(kind)


def bell_draw_with(own_key, dims, width, bound, split, heavy, kind=jnp.bfloat16):
    values = width * jax.random.normal(own_key, dims, jnp.float32)
    if split:
        values = values * level_of(own_key, dims, split, -0.22, 0.18)
    return jnp.clip(strengthened(values, jax.random.fold_in(own_key, 3), *heavy), -bound, bound).astype(kind)


def setup_inputs(seed: int = 0) -> dict:
    key_list = jax.random.split(jax.random.key(seed), 7)
    return {
        "tokens": bell_draw_with(key_list[0], (TOKENS, D), 1.0, 6.0, ((0, 16), (1, 8)), (0, 1, 16, 2.0)),
        "up_weight": bell_draw(key_list[1], (2, D, FFW), D ** -0.5, 0.109375, ((0, 2), (1, 16), (2, 8))),
        "down_weight": bell_draw(key_list[2], (2, FFW, D), FFW ** -0.5, 0.078125, ((0, 2), (1, 8), (2, 16))),
        "mod_table": bell_draw(key_list[3], (2, STEPS, 3, D), 0.5, 3.0, ((0, 2),), jnp.float32),
        "timesteps": set_ends(jax.random.randint(key_list[4], (SAMPLES,), 0, STEPS), jax.random.fold_in(key_list[4], 1), 0, STEPS - 1).astype(jnp.int32),
        "valid_counts": draw_valid_counts(jax.random.fold_in(key_list[6], 71), 0),
    }


def gelu_tanh(values):
    return jax.nn.gelu(values, approximate=True)

def block_forward(tokens, up_matrix, down_matrix, table, timesteps):
    wide = tokens.astype(jnp.float32).reshape(N_DP, SEQ, D)
    average = lax.optimization_barrier(jnp.mean(wide, axis=-1, keepdims=True))
    centred = wide - average
    variance = lax.optimization_barrier(jnp.mean(centred * centred, axis=-1, keepdims=True))
    scaled = centred * lax.rsqrt(variance + 1e-06)
    modulation = table[timesteps]
    normed = (scaled * (1.0 + modulation[:, 1:2]) + modulation[:, 0:1]).astype(jnp.bfloat16).reshape(TOKENS, D)
    hidden_pre = jnp.dot(normed, up_matrix, preferred_element_type=jnp.float32)
    hidden_act = gelu_tanh(hidden_pre).astype(jnp.bfloat16)
    mixed = jnp.dot(hidden_act, down_matrix, preferred_element_type=jnp.float32).reshape(N_DP, SEQ, D)
    gate_rows = modulation[:, 2:3]
    output = (wide + gate_rows * mixed).astype(jnp.bfloat16).reshape(TOKENS, D)
    return (normed, hidden_pre, hidden_act, gate_rows, output)

def rounded_sum(left, right):

    def accumulate(running, index):
        left_rows = lax.dynamic_slice_in_dim(left, (index * SEQ).astype(jnp.int32), SEQ, 0)
        right_rows = lax.dynamic_slice_in_dim(right, (index * SEQ).astype(jnp.int32), SEQ, 0)
        term = lax.dot_general(left_rows, right_rows, (((0,), (0,)), ((), ())), preferred_element_type=jnp.float32)
        term = lax.optimization_barrier(term.astype(jnp.bfloat16))
        return (running + term.astype(jnp.float32), None)
    start_value = jnp.zeros((left.shape[1], right.shape[1]), jnp.float32)
    result, unused = lax.scan(accumulate, start_value, jnp.arange(N_DP, dtype=jnp.int32))
    return result

def block_grads(normed, hidden_pre, hidden_act, gate_rows, own, other, down_matrix, valid_counts):
    positions = jnp.arange(SEQ, dtype=jnp.int32)
    valid_rows = (positions[None, :] < valid_counts[:, None]).astype(jnp.float32)[:, :, None]
    valid_total = jnp.sum(valid_counts).astype(jnp.float32)
    differ = (own.astype(jnp.float32) - other.astype(jnp.float32)).reshape(N_DP, SEQ, D)
    grad_out = (gate_rows * differ * valid_rows / jnp.sqrt(valid_total)).astype(jnp.bfloat16).reshape(TOKENS, D)
    grad_act = lax.dot_general(grad_out, down_matrix, (((1,), (1,)), ((), ())), preferred_element_type=jnp.float32)
    unused, pullback = jax.vjp(gelu_tanh, hidden_pre)
    grad_pre = pullback(grad_act)[0].astype(jnp.bfloat16)
    return (rounded_sum(normed, grad_pre), rounded_sum(hidden_act, grad_out))

def reference(tokens, up_weight, down_weight, mod_table, timesteps, valid_counts):
    teacher = block_forward(tokens, up_weight[0], down_weight[0], mod_table[0], timesteps)
    student = block_forward(tokens, up_weight[1], down_weight[1], mod_table[1], timesteps)
    student_up, student_down = block_grads(student[0], student[1], student[2], student[3], student[4], teacher[4], down_weight[1], valid_counts)
    block_out = jnp.stack([teacher[4], student[4]])
    return (block_out, student_up, student_down)
```

```python
import functools

import jax
import jax.numpy as jnp
from jax import lax
from jax.experimental import pallas as pl
from jax.experimental.pallas import tpu as pltpu
from jax.sharding import PartitionSpec as P

BF = jnp.bfloat16
F32 = jnp.float32
R = 4
ROWS = 192 // R
RA = 32
NZ = 8
SEQ = 256
BLK = 384
N_SEM = 300


def gelu_pair(v):
    k = 0.7978845608028654
    v2 = v * v
    t = jnp.tanh(k * v * (1.0 + 0.044715 * v2))
    half = 0.5 * (1.0 + t)
    act = v * half
    slope = half + 0.5 * v * (1.0 - t * t) * (k * (1.0 + 3.0 * 0.044715 * v2))
    return act, slope


def nn(a, b):
    return lax.dot_general(a, b, (((1,), (0,)), ((), ())), preferred_element_type=F32)


def nt(a, b):
    return lax.dot_general(a, b, (((1,), (1,)), ((), ())), preferred_element_type=F32)


def tn(a, b):
    return lax.dot_general(a, b, (((0,), (0,)), ((), ())), preferred_element_type=F32)


def kernel(
    axes,
    tok_ref, up_ref, downt_ref, mod_ref, gate_ref, valid_ref,
    out_ref, ug_ref, dg_ref,
    T, U, D, N, NTR, HP, SL, ACT, PO, PS, PR, ZS, ZR, GATE, TOKT, OTA, OTB, GT, GA, GP,
    QV, XBS, XBR, A2S, A2R, A1S, A1R, B2S, B2R, B1S, B1R, AXS, AXR, FS, FO, FR, HS, HR,
    send, recv, local,
):
    dp, z, s = lax.axis_index("dp"), lax.axis_index("mp"), lax.axis_index("side")
    c = lax.rem(dp, 2)
    y = lax.rem(lax.div(dp, 2), 4)
    xl = lax.div(dp, 8)
    xo = 1 - xl
    yp, ym, y2 = lax.rem(y + 1, 4), lax.rem(y + 3, 4), lax.rem(y + 2, 4)
    oc = 1 - c

    def zz(k):
        return lax.rem(z + (k + NZ), NZ)

    def where(dp_=None, mp_=None, side_=None):
        at = {"dp": dp if dp_ is None else dp_, "mp": z if mp_ is None else mp_, "side": s if side_ is None else side_}
        return tuple(at[a] for a in axes)

    def jj(a, b):
        return a * 4 + b

    X = where(dp_=xo * 8 + y * 2 + c)
    YP = where(dp_=xl * 8 + yp * 2 + c)
    YM = where(dp_=xl * 8 + ym * 2 + c)
    ZP = where(mp_=zz(1))
    ZM = where(mp_=zz(-1))
    C = where(dp_=dp + 1 - 2 * c)
    S = where(side_=1 - s)

    barrier = pltpu.get_barrier_semaphore()
    peers = (X, YP, YM, ZP, ZM, C, S)
    for peer in peers:
        pl.semaphore_signal(barrier, inc=1, device_id=peer, device_id_type=pl.DeviceIdType.MESH)
    pl.semaphore_wait(barrier, len(peers))

    used = [0]
    started = {None: [], 0: [], 1: []}

    class Copy:
        def __init__(self, refs, dev, side):
            self.refs, self.dev, self.i = refs, dev, used[0]
            used[0] += 1
            self.made().start()
            started[side].append(self)

        def made(self):
            src, dst = self.refs()
            return pltpu.make_async_remote_copy(
                src_ref=src, dst_ref=dst, send_sem=send.at[self.i], recv_sem=recv.at[self.i],
                device_id=self.dev, device_id_type=pl.DeviceIdType.MESH,
            )

        def wait_recv(self):
            self.made().wait_recv()

        def wait_send(self):
            self.made().wait_send()

    def copy(src, dst, dev, side=None):
        return Copy(lambda: (src(), dst()), dev, side)

    def copy_same(at, dev, side=None):
        return Copy(lambda: (at(),) * 2, dev, side)

    student = s == 1

    class Gather:
        def __init__(self, buf, ra):
            self.buf, self.ra = buf, ra

        def g0(self):
            self.xa = copy_same(lambda: self.apart(xl, y), X)
            self.yp = copy_same(lambda: self.buf(own), YP)
            self.ym = copy_same(lambda: self.buf(own), YM)
            self.xb = copy_same(lambda: self.bpart(xl, y), X)

        def g1(self):
            self.xa.wait_recv()
            self.xap = copy_same(lambda: self.apart(xo, y), YP)
            self.xam = copy_same(lambda: self.apart(xo, y), YM)

        def apart(self, xx, yy):
            return self.buf(jj(xx, yy)).at[:, pl.ds(0, self.ra)]

        def bpart(self, xx, yy):
            b = self.buf(jj(xx, yy))
            return b.at[:, pl.ds(self.ra, b.shape[1] - self.ra)]

        def g2(self):
            self.yp.wait_recv()
            self.rp = copy_same(lambda: self.buf(jj(xl, ym)).at[0], YP)
            self.bxm = copy_same(lambda: self.bpart(xl, ym), X)
            self.ym.wait_recv()
            self.rm = copy_same(lambda: self.buf(jj(xl, yp)).at[1], YM)
            self.bxp = copy_same(lambda: self.bpart(xl, yp), X)

        def g3(self):
            self.xap.wait_recv()
            self.rxp = copy_same(lambda: self.buf(jj(xo, ym)).at[0, pl.ds(0, self.ra)], YP)
            self.xam.wait_recv()
            self.rxm = copy_same(lambda: self.buf(jj(xo, yp)).at[1, pl.ds(0, self.ra)], YM)

        def g4(self):
            self.rp.wait_recv()
            self.rm.wait_recv()
            self.bx2 = copy_same(lambda: self.bpart(xl, y2), X)

        def g5(self):
            for d in (self.xb, self.bxm, self.bxp, self.rxp, self.rxm, self.bx2):
                d.wait_recv()

    own = jj(xl, y)
    u_out = copy(lambda: up_ref.at[:, pl.ds(pl.multiple_of(oc * BLK, 128), BLK)], lambda: U.at[own, c], C)
    d_out = copy(lambda: downt_ref.at[oc], lambda: D.at[:, own, c], C)
    tok_in = pltpu.make_async_copy(tok_ref, T.at[z], local.at[0])
    tok_in.start()
    u_in = pltpu.make_async_copy(up_ref.at[:, pl.ds(pl.multiple_of(c * BLK, 128), BLK)], U.at[own, c], local.at[1])
    u_in.start()
    d_in = pltpu.make_async_copy(downt_ref.at[c], D.at[:, own, c], local.at[2])
    d_in.start()

    tk = {}

    def tok_send(hop):
        for p in range(2):
            rows = pl.ds(128 * p, 128)
            if hop:
                if ("+", hop - 1, p) in tk:
                    tk["+", hop - 1, p].wait_recv()
            at = functools.partial(lambda k, rows: tok_ref.at[rows] if k is None else T.at[zz(k), rows], rows=rows)
            src = functools.partial(at, None if hop == 0 else -hop)
            if hop < 3 or p == 0:
                tk["+", hop, p] = copy(src, functools.partial(at, -hop), ZP)
            if hop:
                if ("-", hop - 1, p) in tk:
                    tk["-", hop - 1, p].wait_recv()
            src = functools.partial(at, None if hop == 0 else hop)
            if hop < 3 or p == 1:
                tk["-", hop, p] = copy(src, functools.partial(at, hop), ZM)

    gu = Gather(lambda j: U.at[j], 128)
    gd = [Gather(functools.partial(lambda r, j: D.at[r, j], r), RA) for r in range(R)]

    tok_send(0)
    u_in.wait()
    u_out.wait_recv()
    gu.g0()
    tok_in.wait()
    gate = jnp.transpose(jnp.broadcast_to(gate_ref[0:1, :], (128, BLK)))
    GATE[:, 0:128] = gate
    GATE[:, 128:256] = gate
    tt = jnp.transpose(T[z].astype(F32))
    TOKT[...] = tt
    tok_send(1)
    gu.g1()
    tok_send(2)
    gu.g2()
    gu.g3()
    tok_send(3)
    gu.g4()
    d_in.wait()
    d_out.wait_recv()
    gd[0].g0()
    tk["+", 3, 0].wait_recv()
    tk["-", 3, 1].wait_recv()

    def norm_rows(i, carry):
        rows = pl.ds(pl.multiple_of(i * 16, 16), 16)
        x = [T[b, rows].astype(F32) for b in range(NZ)]
        total = x[0]
        for b in range(1, NZ):
            total = total + x[b]
        mean = jnp.sum(total, axis=-1, keepdims=True) * (1.0 / (NZ * BLK))
        x = [v - mean for v in x]
        sq = x[0] * x[0]
        for b in range(1, NZ):
            sq = sq + x[b] * x[b]
        var = jnp.sum(sq, axis=-1, keepdims=True) * (1.0 / (NZ * BLK))
        rs = lax.rsqrt(var + 1e-06)
        for b in range(NZ):
            cols = slice(b * BLK, (b + 1) * BLK)
            n = x[b] * rs * (1.0 + mod_ref[1:2, cols]) + mod_ref[0:1, cols]
            N[c, b, rows] = n.astype(BF)
        return carry

    n_out = []
    for p in range(2):
        lax.fori_loop(8 * p, 8 * p + 8, norm_rows, 0)
        rows = pl.ds(128 * p, 128)
        n_out.append(copy_same(functools.partial(lambda rows: N.at[c, :, rows], rows), C))

    gu.g5()

    def hidden(img):
        h = nn(N[img, 0], U[0].reshape(BLK, BLK))
        for b in range(1, NZ):
            h = h + nn(N[img, b], U[b].reshape(BLK, BLK))
        HP[...] = h

        def act_rows(i, carry):
            rows = pl.ds(pl.multiple_of(i * 32, 32), 32)
            a, g = gelu_pair(HP[rows])
            ACT[img, rows] = a.astype(BF)
            SL[img, rows] = g
            return carry

        lax.fori_loop(0, SEQ // 32, act_rows, 0)

    def hidden_loop(i, carry):
        @pl.when(i == 1)
        def _():
            for d in n_out:
                d.wait_recv()

        hidden(lax.rem(c + i, 2))
        return carry

    gd[0].g1()
    lax.fori_loop(0, 2, hidden_loop, 0)

    m_out, zs = {}, {}

    def mixed(r):
        w = D[r].reshape(NZ * 2 * ROWS, BLK)
        PS[r] = nt(w, ACT[oc]).astype(BF)
        m_out[r] = copy(lambda: PS.at[r], lambda: PR.at[r], C)
        PO[r] = nt(w, ACT[c])

    def val(r, b):
        rows = pl.ds(pl.multiple_of(b * 2 * ROWS, 32), 2 * ROWS)
        return PO[r, rows] + PR[r, rows].astype(F32)

    def zstage(r, k):
        h0, h1 = pl.ds(0, ROWS), pl.ds(ROWS, ROWS)
        if k == 0:
            m_out[r].wait_recv()
            v = val(r, zz(4)).astype(BF)
            ZS[r, 0, 0] = v
            zs[r, 0, 0] = copy(lambda: ZS.at[r, 0, 0, h0], lambda: ZR.at[r, 0, 0, h0], ZP)
            zs[r, 1, 0] = copy(lambda: ZS.at[r, 0, 0, h1], lambda: ZR.at[r, 1, 0, h1], ZM)
            return
        for q in range(2):
            zs[r, q, k - 1].wait_recv()
            v = val(r, zz((4 - k) if q == 0 else (k - 4)))
            if k == 1:
                h = slice(0, ROWS) if q == 0 else slice(ROWS, 2 * ROWS)
                g = slice(ROWS, 2 * ROWS) if q == 0 else slice(0, ROWS)
                ZS[r, q, k, h] = (v[h] + ZR[r, q, 0, h].astype(F32)).astype(BF)
                ZS[r, q, k, g] = v[g].astype(BF)
            else:
                ZS[r, q, k] = (v + ZR[r, q, k - 1].astype(F32)).astype(BF)
            at = functools.partial(lambda ref, q: ref.at[r, q, k], q=q)
            zs[r, q, k] = copy(functools.partial(at, ZS), functools.partial(at, ZR), ZP if q == 0 else ZM)

    sw = {}

    def rows_of(r, h):
        return slice(192 * h + ROWS * r, 192 * h + ROWS * (r + 1))

    def output(r):
        zs[r, 0, 3].wait_recv()
        zs[r, 1, 3].wait_recv()
        m = val(r, z) + ZR[r, 0, 3].astype(F32) + ZR[r, 1, 3].astype(F32)
        for h in range(2):
            w = rows_of(r, h)
            o = (TOKT[w] + GATE[w] * m[ROWS * h:ROWS * (h + 1)]).astype(BF)
            OTA[r, h] = o
            TOKT[w] = o.astype(F32)

        @pl.when(s == 0)
        def _():
            sw[r] = copy(lambda: OTA.at[r], lambda: OTB.at[r], S, 0)

    ag, fw = {}, {}

    def gslice(r, img, b, h):
        n = ROWS if h is not None else 2 * ROWS
        return GT.at[r, img, pl.ds(pl.multiple_of(b * 2 * ROWS + (h or 0) * ROWS, 16), n)]

    def astage(r, k):
        @pl.when(student)
        def _():
            def push(kk, dev, h=None):
                return copy_same(lambda: gslice(r, c, zz(kk), h), dev, 1)

            if k == 0:
                sw[r].wait_recv()
                vrow = valid_ref[0:1, :]
                for h in range(2):
                    w = rows_of(r, h)
                    diff = OTA[r, h].astype(F32) - OTB[r, h].astype(F32)
                    rows = pl.ds(pl.multiple_of(z * 2 * ROWS + h * ROWS, 16), ROWS)
                    GT[r, c, rows] = (GATE[w] * diff * vrow).astype(BF)
                ag[r, 0, 0] = push(0, ZP)
                ag[r, 1, 0] = push(0, ZM)
                fw[r, 0] = [push(0, C)]
                return
            ag[r, 0, k - 1].wait_recv()
            h = 0 if k > 2 else None
            if k < 4:
                ag[r, 0, k] = push(-k, ZP, h)
            fw[r, k] = [push(-k, C, None if k < 4 else 0)]
            ag[r, 1, k - 1].wait_recv()
            h = 1 if k > 2 else None
            if k < 4:
                ag[r, 1, k] = push(k, ZM, h)
            fw[r, k].append(push(k, C, None if k < 4 else 1))

    class Reduce:
        def __init__(self, kind, r):
            self.i = kind * R + r
            self.r, self.kind = r, kind

        def both(self, src, dst):
            def one(h):
                return copy(lambda: src.at[self.i, h], lambda: dst.at[self.i, h], (YP, YM)[h], 1)

            return [one(0), one(1)]

        def q(self, j, rows):
            return QV[self.kind, j, :, rows]

        def r0(self):
            i, a, b = self.i, slice(0, RA), slice(RA, ROWS)
            for h in range(2):
                for x in range(2):
                    A2S[i, h, x] = QV[self.kind, jj(x, y2), h, a].astype(BF)
            self.a2 = self.both(A2S, A2R)
            for k in range(4):
                XBS[i, k] = QV[self.kind, jj(xo, k), :, b].astype(BF)
            self.xb = copy(lambda: XBS.at[i], lambda: XBR.at[i], X, 1)

        def r1(self):
            i, a = self.i, slice(0, RA)
            for h in range(2):
                self.a2[h].wait_recv()
                for x in range(2):
                    v = self.q(jj(x, (yp, ym)[h]), a)
                    A1S[i, h, x, h] = (v[h] + A2R[i, h, x].astype(F32)).astype(BF)
                    A1S[i, h, x, 1 - h] = v[1 - h].astype(BF)
            self.a1 = self.both(A1S, A1R)

        def r2(self):
            i, b = self.i, slice(RA, ROWS)
            self.xb.wait_recv()
            v = self.q(jj(xl, y2), b) + XBR[i, y2].astype(F32)
            B2S[i] = v.astype(BF)
            self.b2 = self.both(B2S, B2R)

        def r3(self):
            i, b = self.i, slice(RA, ROWS)
            for h in range(2):
                self.b2[h].wait_recv()
                yy = (yp, ym)[h]
                v = self.q(jj(xl, yy), b) + XBR[i, yy].astype(F32)
                B1S[i, h, h] = (v[h] + B2R[i, h].astype(F32)).astype(BF)
                B1S[i, h, 1 - h] = v[1 - h].astype(BF)
            self.b1 = self.both(B1S, B1R)

        def r4(self):
            i, a = self.i, slice(0, RA)
            for h in range(2):
                self.a1[h].wait_recv()
            v = self.q(jj(xo, y), a) + A1R[i, 0, xo].astype(F32) + A1R[i, 1, xo].astype(F32)
            AXS[i] = v.astype(BF)
            self.ax = copy(lambda: AXS.at[i], lambda: AXR.at[i], X, 1)

        def r5(self):
            i, a, b = self.i, slice(0, RA), slice(RA, ROWS)
            for d in (self.ax, *self.b1):
                d.wait_recv()
            va = self.q(own, a) + A1R[i, 0, xl].astype(F32) + A1R[i, 1, xl].astype(F32) + AXR[i].astype(F32)
            vb = self.q(own, b) + XBR[i, y].astype(F32) + B1R[i, 0].astype(F32) + B1R[i, 1].astype(F32)
            FO[i, :, a] = va
            FO[i, :, b] = vb
            FS[i] = FO[i, oc].astype(BF)
            self.f = copy(lambda: FS.at[i], lambda: FR.at[i], C, 1)

        def r6(self):
            i = self.i
            self.f.wait_recv()
            if self.r < R // 2:
                HS[i, c] = FO[i, c].astype(BF)
                HS[i, oc] = FR[i]
                self.h = copy(lambda: HS.at[i], lambda: HR.at[i], S, 1)
            else:
                o = (ug_ref, dg_ref)[self.kind]
                rows = slice(ROWS * (self.r - R // 2), ROWS * (self.r - R // 2 + 1))

                @pl.when(c == 0)
                def _():
                    o[rows, 0:BLK] = FO[i, 0]
                    o[rows, BLK:2 * BLK] = FR[i].astype(F32)

                @pl.when(c == 1)
                def _():
                    o[rows, 0:BLK] = FR[i].astype(F32)
                    o[rows, BLK:2 * BLK] = FO[i, 1]

    red = {(k, r): Reduce(k, r) for k in range(2) for r in range(R)}

    def down_grads(r):
        g = [GT[r, 0], GT[r, 1]]
        q = nn(g[0], ACT[0]) + nn(g[1], ACT[1])
        QV[1] = q.reshape(NZ, 2, ROWS, BLK)

    def grad_act(r):
        w = D[r].reshape(NZ * 2 * ROWS, BLK)
        for img in range(2):
            v = tn(GT[r, img], w)
            if r == 0:
                GA[img] = v
            else:
                GA[img] += v

    def arrived(r):
        for k in range(5):
            for d in fw[r, k]:
                d.wait_recv()

    def transposed():
        @pl.when(student)
        def _():
            def one(i, carry):
                img, j = lax.div(i, 8), lax.rem(i, 8)
                t = jnp.transpose(N[img, j].astype(F32)).astype(BF)
                for r in range(R):
                    for h in range(2):
                        NTR[r, img, pl.ds(pl.multiple_of(j * 2 * ROWS + h * ROWS, 16), ROWS)] = t[rows_of(r, h)]
                return carry

            lax.fori_loop(0, 16, one, 0)

    for r in range(R):
        if r:
            gd[r].g1()
        if r > 1:
            zstage(r - 2, 3)
        if r + 1 < R:
            gd[r + 1].g0()
        if r > 0:
            zstage(r - 1, 1)
        if r == 1:
            transposed()
        gd[r].g2()
        if r > 2:
            output(r - 3)
        gd[r].g3()
        if r > 0:
            zstage(r - 1, 2)
        if r > 2:
            astage(r - 3, 0)
        gd[r].g4()
        gd[r].g5()
        mixed(r)
        zstage(r, 0)
    zstage(R - 2, 3)
    zstage(R - 1, 1)
    output(R - 3)
    zstage(R - 1, 2)
    output(R - 2)
    astage(R - 3, 0)
    zstage(R - 1, 3)
    astage(0, 1)
    output(R - 1)
    astage(R - 2, 0)
    astage(1, 1)
    astage(0, 2)
    astage(R - 1, 0)
    astage(2, 1)
    astage(1, 2)
    astage(0, 3)
    astage(3, 1)
    astage(2, 2)
    astage(1, 3)
    astage(0, 4)
    astage(3, 2)
    astage(2, 3)

    out_ref[...] = jnp.transpose(TOKT[...]).astype(BF)

    @pl.when(student)
    def _():
        arrived(0)
        down_grads(0)
        red[1, 0].r0()

    astage(1, 4)
    astage(3, 3)
    astage(2, 4)

    @pl.when(student)
    def _():
        grad_act(0)
        red[1, 0].r1()
        red[1, 0].r2()

    astage(3, 4)

    @pl.when(student)
    def _():
        red[1, 0].r3()
        red[1, 0].r4()
        order = [(1, r) for r in range(R)] + [(0, r) for r in range(R)]

        def first(k, r):
            if k == 1:
                arrived(r)
                down_grads(r)
            else:
                if r == 0:
                    for img in range(2):
                        GP[img] = (GA[img] * SL[img]).astype(BF)
                q = nn(NTR[r, 0], GP[0]) + nn(NTR[r, 1], GP[1])
                QV[0] = q.reshape(NZ, 2, ROWS, BLK)
            red[k, r].r0()

        for n in range(1, 2 * R):
            k, r = order[n]
            prev = red[order[n - 1]]
            if n > 1:
                prev.r3()
                prev.r4()
            prev.r5()
            first(k, r)
            if k == 1:
                grad_act(r)
            prev.r6()
            red[k, r].r1()
            red[k, r].r2()
        last = red[order[-1]]
        last.r3()
        last.r4()
        last.r5()
        last.r6()

    @pl.when(s == 0)
    def _():
        for k in (1, 0):
            o = (ug_ref, dg_ref)[k]
            for r in range(R // 2):
                red[k, r].h.wait_recv()
                for h in range(2):
                    o[ROWS * r:ROWS * (r + 1), BLK * h:BLK * (h + 1)] = HR[k * R + r, h].astype(F32)

    for d in started[None]:
        d.wait_send()

    @pl.when(s == 0)
    def _():
        for d in started[0]:
            d.wait_send()

    @pl.when(student)
    def _():
        for d in started[1]:
            d.wait_send()


def shards(axes, tokens, up_weight, down_weight, mod_table, timesteps, valid_counts):
    mp, dp = lax.axis_index("mp"), lax.axis_index("dp")
    mod = lax.dynamic_index_in_dim(mod_table[0], timesteps[0], 0, keepdims=False)
    gate = jnp.broadcast_to(lax.dynamic_slice_in_dim(mod[2], mp * BLK, BLK)[None], (8, BLK))
    count = lax.dynamic_index_in_dim(valid_counts, dp, 0, keepdims=False)
    total = jnp.sum(valid_counts).astype(F32)
    valid = (jnp.arange(SEQ, dtype=jnp.int32) < count).astype(F32) / jnp.sqrt(total)
    valid = jnp.broadcast_to(valid[None], (8, SEQ))
    downt = down_weight[0].reshape(2, BLK, R, ROWS).transpose(0, 2, 3, 1)

    v = pltpu.VMEM
    nred = 2 * R
    scratch = [
        v((NZ, SEQ, BLK), BF),
        v((NZ, 2, 192, BLK), BF),
        v((R, NZ, 2, ROWS, BLK), BF),
        v((2, NZ, SEQ, BLK), BF),
        v((R, 2, NZ * 2 * ROWS, SEQ), BF),
        v((SEQ, BLK), F32),
        v((2, SEQ, BLK), F32),
        v((2, SEQ, BLK), BF),
        v((R, NZ * 2 * ROWS, SEQ), F32),
        v((R, NZ * 2 * ROWS, SEQ), BF),
        v((R, NZ * 2 * ROWS, SEQ), BF),
        v((R, 2, 4, 2 * ROWS, SEQ), BF),
        v((R, 2, 4, 2 * ROWS, SEQ), BF),
        v((BLK, SEQ), F32),
        v((BLK, SEQ), F32),
        v((R, 2, ROWS, SEQ), BF),
        v((R, 2, ROWS, SEQ), BF),
        v((R, 2, NZ * 2 * ROWS, SEQ), BF),
        v((2, SEQ, BLK), F32),
        v((2, SEQ, BLK), BF),
        v((2, NZ, 2, ROWS, BLK), F32),
        v((nred, 4, 2, ROWS - RA, BLK), BF),
        v((nred, 4, 2, ROWS - RA, BLK), BF),
        v((nred, 2, 2, RA, BLK), BF),
        v((nred, 2, 2, RA, BLK), BF),
        v((nred, 2, 2, 2, RA, BLK), BF),
        v((nred, 2, 2, 2, RA, BLK), BF),
        v((nred, 2, ROWS - RA, BLK), BF),
        v((nred, 2, ROWS - RA, BLK), BF),
        v((nred, 2, 2, ROWS - RA, BLK), BF),
        v((nred, 2, 2, ROWS - RA, BLK), BF),
        v((nred, 2, RA, BLK), BF),
        v((nred, 2, RA, BLK), BF),
        v((nred, ROWS, BLK), BF),
        v((nred, 2, ROWS, BLK), F32),
        v((nred, ROWS, BLK), BF),
        v((nred, 2, ROWS, BLK), BF),
        v((nred, 2, ROWS, BLK), BF),
        pltpu.SemaphoreType.DMA((N_SEM,)),
        pltpu.SemaphoreType.DMA((N_SEM,)),
        pltpu.SemaphoreType.DMA((3,)),
    ]
    hbm = pl.BlockSpec(memory_space=pl.ANY)
    vm = pl.BlockSpec(memory_space=pltpu.VMEM)
    out, up, down = pl.pallas_call(
        functools.partial(kernel, axes),
        out_shape=(
            jax.ShapeDtypeStruct((SEQ, BLK), BF),
            jax.ShapeDtypeStruct((96, 2 * BLK), F32),
            jax.ShapeDtypeStruct((96, 2 * BLK), F32),
        ),
        in_specs=[hbm, hbm, hbm, vm, vm, vm],
        out_specs=(vm, vm, vm),
        scratch_shapes=scratch,
        compiler_params=pltpu.CompilerParams(
            collective_id=0, has_side_effects=True, vmem_limit_bytes=67043328
        ),
    )(tokens, up_weight[0], downt, mod, gate, valid)
    return out[None], up, down.T


def solution(mesh):
    placed = (
        P("dp", "mp"),
        P("side", "dp", "mp"),
        P("side", "mp", "dp"),
        P("side", None, None, None),
        P("dp"),
        P(),
    )
    return jax.shard_map(
        functools.partial(shards, mesh.axis_names),
        mesh=mesh,
        in_specs=placed,
        out_specs=(P("side", "dp", "mp"), P(("dp", "side"), "mp"), P("mp", ("dp", "side"))),
        check_vma=False,
    )
```

```python
import functools

import jax
import jax.numpy as jnp
from jax import lax
from jax.experimental import pallas as pl
from jax.experimental.pallas import tpu as pltpu
from jax.sharding import PartitionSpec as P

BF = jnp.bfloat16
F32 = jnp.float32
R = 4
ROWS = 192 // R
RA = 32
NZ = 8
SEQ = 256
BLK = 384
N_RECV = 290
N_SEND = {None: 32, 0: 4, 1: 32}


def gelu_pair(v):
    k = 0.7978845608028654
    v2 = v * v
    t = jnp.tanh(k * v * (1.0 + 0.044715 * v2))
    half = 0.5 * (1.0 + t)
    act = v * half
    slope = half + 0.5 * v * (1.0 - t * t) * (k * (1.0 + 3.0 * 0.044715 * v2))
    return act, slope


def nn(a, b):
    return lax.dot_general(a, b, (((1,), (0,)), ((), ())), preferred_element_type=F32)


def nt(a, b):
    return lax.dot_general(a, b, (((1,), (1,)), ((), ())), preferred_element_type=F32)


def tn(a, b):
    return lax.dot_general(a, b, (((0,), (0,)), ((), ())), preferred_element_type=F32)


def kernel(
    axes,
    tok_ref, up_ref, downt_ref, mod_ref, counts_ref,
    out_ref, ug_ref, dg_ref,
    T, U, D, N, NTR, HP, SL, ACT, PO, PS, PR, ZS, ZR, GATE, TOKT, OTA, OTB, GT, GA, GP,
    QV, XBS, XBR, A2S, A2R, A1S, A1R, B2S, B2R, B1S, B1R, AXS, AXR, FS, FO, FR, HS, HR,
    send, recv, local,
):
    dp, z, s = lax.axis_index("dp"), lax.axis_index("mp"), lax.axis_index("side")
    c = lax.rem(dp, 2)
    y = lax.rem(lax.div(dp, 2), 4)
    xl = lax.div(dp, 8)
    xo = 1 - xl
    yp, ym, y2 = lax.rem(y + 1, 4), lax.rem(y + 3, 4), lax.rem(y + 2, 4)
    oc = 1 - c

    def zz(k):
        return lax.rem(z + (k + NZ), NZ)

    def where(dp_=None, mp_=None, side_=None):
        at = {"dp": dp if dp_ is None else dp_, "mp": z if mp_ is None else mp_, "side": s if side_ is None else side_}
        return tuple(at[a] for a in axes)

    def jj(a, b):
        return a * 4 + b

    X = where(dp_=xo * 8 + y * 2 + c)
    YP = where(dp_=xl * 8 + yp * 2 + c)
    YM = where(dp_=xl * 8 + ym * 2 + c)
    ZP = where(mp_=zz(1))
    ZM = where(mp_=zz(-1))
    C = where(dp_=dp + 1 - 2 * c)
    S = where(side_=1 - s)

    barrier = pltpu.get_barrier_semaphore()
    peers = (X, YP, YM, ZP, ZM, C, S)
    for peer in peers:
        pl.semaphore_signal(barrier, inc=1, device_id=peer, device_id_type=pl.DeviceIdType.MESH)
    pl.semaphore_wait(barrier, len(peers))

    used = [0]
    started = {None: [], 0: [], 1: []}

    class Copy:
        def __init__(self, refs, dev, side):
            self.refs, self.dev, self.i = refs, dev, used[0]
            used[0] += 1
            mine = started[side]
            pool = N_SEND[side]
            self.j = len(mine) % pool + {None: 0, 0: N_SEND[None], 1: N_SEND[None] + N_SEND[0]}[side]
            if len(mine) >= pool:
                mine[-pool].wait_send()
            self.made().start()
            mine.append(self)

        def made(self):
            src, dst = self.refs()
            return pltpu.make_async_remote_copy(
                src_ref=src, dst_ref=dst, send_sem=send.at[self.j], recv_sem=recv.at[self.i],
                device_id=self.dev, device_id_type=pl.DeviceIdType.MESH,
            )

        def wait_recv(self):
            self.made().wait_recv()

        def wait_send(self):
            self.made().wait_send()

    def copy(src, dst, dev, side=None):
        return Copy(lambda: (src(), dst()), dev, side)

    def copy_same(at, dev, side=None):
        return Copy(lambda: (at(),) * 2, dev, side)

    student = s == 1

    class Gather:
        def __init__(self, buf, ra):
            self.buf, self.ra = buf, ra

        def g0(self):
            self.xa = copy_same(lambda: self.apart(xl, y), X)
            self.yp = copy_same(lambda: self.buf(own), YP)
            self.ym = copy_same(lambda: self.buf(own), YM)
            self.xb = copy_same(lambda: self.bpart(xl, y), X)

        def g1(self):
            self.xa.wait_recv()
            self.xap = copy_same(lambda: self.apart(xo, y), YP)
            self.xam = copy_same(lambda: self.apart(xo, y), YM)

        def apart(self, xx, yy):
            return self.buf(jj(xx, yy)).at[:, pl.ds(0, self.ra)]

        def bpart(self, xx, yy):
            b = self.buf(jj(xx, yy))
            return b.at[:, pl.ds(self.ra, b.shape[1] - self.ra)]

        def g2(self):
            self.yp.wait_recv()
            self.rp = copy_same(lambda: self.buf(jj(xl, ym)).at[0], YP)
            self.bxm = copy_same(lambda: self.bpart(xl, ym), X)
            self.ym.wait_recv()
            self.rm = copy_same(lambda: self.buf(jj(xl, yp)).at[1], YM)
            self.bxp = copy_same(lambda: self.bpart(xl, yp), X)

        def g3(self):
            self.xap.wait_recv()
            self.rxp = copy_same(lambda: self.buf(jj(xo, ym)).at[0, pl.ds(0, self.ra)], YP)
            self.xam.wait_recv()
            self.rxm = copy_same(lambda: self.buf(jj(xo, yp)).at[1, pl.ds(0, self.ra)], YM)

        def g4(self):
            self.rp.wait_recv()
            self.rm.wait_recv()
            self.bx2 = copy_same(lambda: self.bpart(xl, y2), X)

        def g5(self):
            for d in (self.xb, self.bxm, self.bxp, self.rxp, self.rxm, self.bx2):
                d.wait_recv()

    own = jj(xl, y)
    u_out = copy(lambda: up_ref.at[:, pl.ds(pl.multiple_of(oc * BLK, 128), BLK)], lambda: U.at[own, c], C)
    d_out = copy(lambda: downt_ref.at[:, :, pl.ds(pl.multiple_of(oc * BLK, 128), BLK)], lambda: D.at[:, own, c], C)
    tok_in = pltpu.make_async_copy(tok_ref, T.at[z], local.at[0])
    tok_in.start()
    u_in = pltpu.make_async_copy(up_ref.at[:, pl.ds(pl.multiple_of(c * BLK, 128), BLK)], U.at[own, c], local.at[1])
    u_in.start()
    d_in = pltpu.make_async_copy(
        downt_ref.at[:, :, pl.ds(pl.multiple_of(c * BLK, 128), BLK)], D.at[:, own, c], local.at[2]
    )
    d_in.start()

    tk = {}

    def tok_send(hop):
        for p in range(2):
            rows = pl.ds(128 * p, 128)
            if hop:
                if ("+", hop - 1, p) in tk:
                    tk["+", hop - 1, p].wait_recv()
            at = functools.partial(lambda k, rows: tok_ref.at[rows] if k is None else T.at[zz(k), rows], rows=rows)
            src = functools.partial(at, None if hop == 0 else -hop)
            if hop < 3 or p == 0:
                tk["+", hop, p] = copy(src, functools.partial(at, -hop), ZP)
            if hop:
                if ("-", hop - 1, p) in tk:
                    tk["-", hop - 1, p].wait_recv()
            src = functools.partial(at, None if hop == 0 else hop)
            if hop < 3 or p == 1:
                tk["-", hop, p] = copy(src, functools.partial(at, hop), ZM)

    gu = Gather(lambda j: U.at[j], 128)
    gd = [Gather(functools.partial(lambda r, j: D.at[r, j], r), RA) for r in range(R)]

    tok_send(0)
    u_in.wait()
    u_out.wait_recv()
    gu.g0()
    tok_in.wait()
    gate = mod_ref[2:3, pl.ds(pl.multiple_of(z * BLK, 128), BLK)]
    gate = jnp.transpose(jnp.broadcast_to(gate, (128, BLK)))
    GATE[:, 0:128] = gate
    GATE[:, 128:256] = gate
    tt = jnp.transpose(T[z].astype(F32))
    TOKT[...] = tt
    tok_send(1)
    gu.g1()
    tok_send(2)
    gu.g2()
    gu.g3()
    d_in.wait()
    d_out.wait_recv()
    gd[0].g0()
    tok_send(3)
    gu.g4()
    gd[1].g0()
    tk["+", 3, 0].wait_recv()
    tk["-", 3, 1].wait_recv()

    def norm_rows(i, carry):
        rows = pl.ds(pl.multiple_of(i * 16, 16), 16)
        x = [T[b, rows].astype(F32) for b in range(NZ)]
        total = x[0]
        for b in range(1, NZ):
            total = total + x[b]
        mean = jnp.sum(total, axis=-1, keepdims=True) * (1.0 / (NZ * BLK))
        x = [v - mean for v in x]
        sq = x[0] * x[0]
        for b in range(1, NZ):
            sq = sq + x[b] * x[b]
        var = jnp.sum(sq, axis=-1, keepdims=True) * (1.0 / (NZ * BLK))
        rs = lax.rsqrt(var + 1e-06)
        for b in range(NZ):
            cols = slice(b * BLK, (b + 1) * BLK)
            n = x[b] * rs * (1.0 + mod_ref[1:2, cols]) + mod_ref[0:1, cols]
            N[c, b, rows] = n.astype(BF)
        return carry

    n_out = []

    def norm_half(p):
        lax.fori_loop(8 * p, 8 * p + 8, norm_rows, 0)
        n_out.append(copy_same(lambda: N.at[c, :, pl.ds(128 * p, 128)], C))

    def hidden(img):
        h = nn(N[img, 0], U[0].reshape(BLK, BLK))
        for b in range(1, NZ):
            h = h + nn(N[img, b], U[b].reshape(BLK, BLK))
        HP[...] = h

        def act_rows(i, carry):
            rows = pl.ds(pl.multiple_of(i * 32, 32), 32)
            a, g = gelu_pair(HP[rows])
            ACT[img, rows] = a.astype(BF)
            SL[img, rows] = g
            return carry

        lax.fori_loop(0, SEQ // 32, act_rows, 0)

    norm_half(0)
    gd[0].g1()
    gd[0].g2()
    norm_half(1)
    gd[2].g0()
    gu.g5()
    gd[0].g3()
    gd[1].g1()
    gd[1].g2()
    hidden(c)
    gd[0].g4()
    gd[3].g0()
    gd[1].g3()
    gd[2].g1()
    gd[2].g2()
    for d in n_out:
        d.wait_recv()

    m_out, zs = {}, {}

    def mixed(r):
        w = D[r].reshape(NZ * 2 * ROWS, BLK)
        PS[r] = nt(w, ACT[oc]).astype(BF)
        m_out[r] = copy(lambda: PS.at[r], lambda: PR.at[r], C)
        PO[r] = nt(w, ACT[c])

    def val(r, b):
        rows = pl.ds(pl.multiple_of(b * 2 * ROWS, 32), 2 * ROWS)
        return PO[r, rows] + PR[r, rows].astype(F32)

    def zstage(r, k):
        h0, h1 = pl.ds(0, ROWS), pl.ds(ROWS, ROWS)
        if k == 0:
            m_out[r].wait_recv()
            v = val(r, zz(4)).astype(BF)
            ZS[r, 0, 0] = v
            zs[r, 0, 0] = copy(lambda: ZS.at[r, 0, 0, h0], lambda: ZR.at[r, 0, 0, h0], ZP)
            zs[r, 1, 0] = copy(lambda: ZS.at[r, 0, 0, h1], lambda: ZR.at[r, 1, 0, h1], ZM)
            return
        for q in range(2):
            zs[r, q, k - 1].wait_recv()
            v = val(r, zz((4 - k) if q == 0 else (k - 4)))
            if k == 1:
                h = slice(0, ROWS) if q == 0 else slice(ROWS, 2 * ROWS)
                g = slice(ROWS, 2 * ROWS) if q == 0 else slice(0, ROWS)
                ZS[r, q, k, h] = (v[h] + ZR[r, q, 0, h].astype(F32)).astype(BF)
                ZS[r, q, k, g] = v[g].astype(BF)
            else:
                ZS[r, q, k] = (v + ZR[r, q, k - 1].astype(F32)).astype(BF)
            at = functools.partial(lambda ref, q: ref.at[r, q, k], q=q)
            zs[r, q, k] = copy(functools.partial(at, ZS), functools.partial(at, ZR), ZP if q == 0 else ZM)

    sw = {}

    def rows_of(r, h):
        return slice(192 * h + ROWS * r, 192 * h + ROWS * (r + 1))

    def output(r):
        zs[r, 0, 3].wait_recv()
        zs[r, 1, 3].wait_recv()
        m = val(r, z) + ZR[r, 0, 3].astype(F32) + ZR[r, 1, 3].astype(F32)
        for h in range(2):
            w = rows_of(r, h)
            o = (TOKT[w] + GATE[w] * m[ROWS * h:ROWS * (h + 1)]).astype(BF)
            OTA[r, h] = o
            TOKT[w] = o.astype(F32)

        @pl.when(s == 0)
        def _():
            sw[r] = copy(lambda: OTA.at[r], lambda: OTB.at[r], S, 0)

    ag, fw = {}, {}

    def gslice(r, img, b, h):
        n = ROWS if h is not None else 2 * ROWS
        return GT.at[r, img, pl.ds(pl.multiple_of(b * 2 * ROWS + (h or 0) * ROWS, 16), n)]

    def astage(r, k):
        @pl.when(student)
        def _():
            def push(kk, dev, h=None):
                return copy_same(lambda: gslice(r, c, zz(kk), h), dev, 1)

            if k == 0:
                sw[r].wait_recv()
                total = counts_ref[0]
                for k_ in range(1, 16):
                    total = total + counts_ref[k_]
                norm = jnp.sqrt(jnp.full((1, SEQ), total, jnp.int32).astype(F32))
                at = lax.broadcasted_iota(jnp.int32, (1, SEQ), 1)
                vrow = jnp.where(at < counts_ref[dp], 1.0, 0.0) / norm
                for h in range(2):
                    w = rows_of(r, h)
                    diff = OTA[r, h].astype(F32) - OTB[r, h].astype(F32)
                    rows = pl.ds(pl.multiple_of(z * 2 * ROWS + h * ROWS, 16), ROWS)
                    GT[r, c, rows] = (GATE[w] * diff * vrow).astype(BF)
                ag[r, 0, 0] = push(0, ZP)
                ag[r, 1, 0] = push(0, ZM)
                fw[r, 0] = [push(0, C)]
                return
            ag[r, 0, k - 1].wait_recv()
            h = 0 if k > 2 else None
            if k < 4:
                ag[r, 0, k] = push(-k, ZP, h)
            fw[r, k] = [push(-k, C, None if k < 4 else 0)]
            ag[r, 1, k - 1].wait_recv()
            h = 1 if k > 2 else None
            if k < 4:
                ag[r, 1, k] = push(k, ZM, h)
            fw[r, k].append(push(k, C, None if k < 4 else 1))

    class Reduce:
        def __init__(self, kind, r):
            self.i = kind * R + r
            self.r, self.kind = r, kind

        def both(self, src, dst):
            def one(h):
                return copy(lambda: src.at[self.i, h], lambda: dst.at[self.i, h], (YP, YM)[h], 1)

            return [one(0), one(1)]

        def q(self, j, rows):
            return QV[self.i, j, :, rows]

        def r0(self):
            i, a, b = self.i, slice(0, RA), slice(RA, ROWS)
            for h in range(2):
                for x in range(2):
                    A2S[i, h, x] = QV[self.i, jj(x, y2), h, a].astype(BF)
            self.a2 = self.both(A2S, A2R)
            for k in range(4):
                XBS[i, k] = QV[self.i, jj(xo, k), :, b].astype(BF)
            self.xb = copy(lambda: XBS.at[i], lambda: XBR.at[i], X, 1)

        def r1(self):
            i, a = self.i, slice(0, RA)
            for h in range(2):
                self.a2[h].wait_recv()
                for x in range(2):
                    v = self.q(jj(x, (yp, ym)[h]), a)
                    A1S[i, h, x, h] = (v[h] + A2R[i, h, x].astype(F32)).astype(BF)
                    A1S[i, h, x, 1 - h] = v[1 - h].astype(BF)
            self.a1 = self.both(A1S, A1R)

        def r2(self):
            i, b = self.i, slice(RA, ROWS)
            self.xb.wait_recv()
            v = self.q(jj(xl, y2), b) + XBR[i, y2].astype(F32)
            B2S[i] = v.astype(BF)
            self.b2 = self.both(B2S, B2R)

        def r3(self):
            i, b = self.i, slice(RA, ROWS)
            for h in range(2):
                self.b2[h].wait_recv()
                yy = (yp, ym)[h]
                v = self.q(jj(xl, yy), b) + XBR[i, yy].astype(F32)
                B1S[i, h, h] = (v[h] + B2R[i, h].astype(F32)).astype(BF)
                B1S[i, h, 1 - h] = v[1 - h].astype(BF)
            self.b1 = self.both(B1S, B1R)

        def r4(self):
            i, a = self.i, slice(0, RA)
            for h in range(2):
                self.a1[h].wait_recv()
            v = self.q(jj(xo, y), a) + A1R[i, 0, xo].astype(F32) + A1R[i, 1, xo].astype(F32)
            AXS[i] = v.astype(BF)
            self.ax = copy(lambda: AXS.at[i], lambda: AXR.at[i], X, 1)

        def r5(self):
            i, a, b = self.i, slice(0, RA), slice(RA, ROWS)
            for d in (self.ax, *self.b1):
                d.wait_recv()
            va = self.q(own, a) + A1R[i, 0, xl].astype(F32) + A1R[i, 1, xl].astype(F32) + AXR[i].astype(F32)
            vb = self.q(own, b) + XBR[i, y].astype(F32) + B1R[i, 0].astype(F32) + B1R[i, 1].astype(F32)
            FO[i, :, a] = va
            FO[i, :, b] = vb
            FS[i] = FO[i, oc].astype(BF)
            self.f = copy(lambda: FS.at[i], lambda: FR.at[i], C, 1)

        def r6(self):
            i = self.i
            self.f.wait_recv()
            if self.r < R // 2:
                HS[i, c] = FO[i, c].astype(BF)
                HS[i, oc] = FR[i]
                self.h = copy(lambda: HS.at[i], lambda: HR.at[i], S, 1)
            else:
                o = (ug_ref, dg_ref)[self.kind]
                rows = slice(ROWS * (self.r - R // 2), ROWS * (self.r - R // 2 + 1))

                @pl.when(c == 0)
                def _():
                    o[rows, 0:BLK] = FO[i, 0]
                    o[rows, BLK:2 * BLK] = FR[i].astype(F32)

                @pl.when(c == 1)
                def _():
                    o[rows, 0:BLK] = FR[i].astype(F32)
                    o[rows, BLK:2 * BLK] = FO[i, 1]

    red = {(k, r): Reduce(k, r) for k in range(2) for r in range(R)}

    def down_grads(r):
        g = [GT[r, 0], GT[r, 1]]
        q = nn(g[0], ACT[0]) + nn(g[1], ACT[1])
        QV[R + r] = q.reshape(NZ, 2, ROWS, BLK)

    def grad_act(r):
        w = D[r].reshape(NZ * 2 * ROWS, BLK)
        for img in range(2):
            v = tn(GT[r, img], w)
            if r == 0:
                GA[img] = v
            else:
                GA[img] += v

    def arrived(r):
        for k in range(5):
            for d in fw[r, k]:
                d.wait_recv()

    def transposed(part):
        def one(i, carry):
            img, j = lax.div(i, 8), lax.rem(i, 8)
            t = jnp.transpose(N[img, j].astype(F32)).astype(BF)
            for r in range(R):
                for h in range(2):
                    NTR[r, img, pl.ds(pl.multiple_of(j * 2 * ROWS + h * ROWS, 16), ROWS)] = t[rows_of(r, h)]
            return carry

        lax.fori_loop(4 * part, 4 * part + 4, one, 0)

    def up_grads(r):
        if r == 0:
            for img in range(2):
                GP[img] = (GA[img] * SL[img]).astype(BF)
        q = nn(NTR[r, 0], GP[0]) + nn(NTR[r, 1], GP[1])
        QV[r] = q.reshape(NZ, 2, ROWS, BLK)

    def stage(n, k):
        if k < 4:
            zstage(n, k)
        elif k == 4:
            output(n)
        elif k < 10:
            astage(n, k - 5)
        else:
            e = red[(1, n) if n < R else (0, n - R)]
            if k == 10:
                if n < R:
                    arrived(n)
                    down_grads(n)
                    e.r0()
                    grad_act(n)
                else:
                    up_grads(n - R)
                    e.r0()
            elif k == 11:
                e.r1()
                e.r2()
            elif k == 12:
                e.r3()
                e.r4()
            elif k == 13:
                e.r5()
            else:
                e.r6()

    def diagonal(d):
        for n in range(2 * R):
            k = d - n
            if 0 <= k < 15 and (n < R or k >= 10):
                stage(n, k)

    hidden(oc)
    gd[0].g5()
    mixed(0)
    gd[1].g4()
    gd[2].g3()
    gd[3].g1()
    gd[3].g2()
    zstage(0, 0)
    gd[1].g5()
    mixed(1)
    gd[2].g4()
    gd[3].g3()
    zstage(0, 1)
    zstage(1, 0)
    gd[2].g5()
    mixed(2)
    gd[3].g4()
    zstage(0, 2)
    zstage(1, 1)
    zstage(2, 0)
    gd[3].g5()
    mixed(3)
    for d in range(3, R + 4):
        diagonal(d)
    out_ref[...] = jnp.transpose(TOKT[...]).astype(BF)

    @pl.when(student)
    def _():
        for d in range(R + 4, 15 + 2 * R - 1):
            diagonal(d)
            if d < R + 8:
                transposed(d - R - 4)

    @pl.when(s == 0)
    def _():
        for k in (1, 0):
            o = (ug_ref, dg_ref)[k]
            for r in range(R // 2):
                red[k, r].h.wait_recv()
                for h in range(2):
                    o[ROWS * r:ROWS * (r + 1), BLK * h:BLK * (h + 1)] = HR[k * R + r, h].astype(F32)

    for d in started[None][-N_SEND[None]:]:
        d.wait_send()

    @pl.when(s == 0)
    def _():
        for d in started[0][-N_SEND[0]:]:
            d.wait_send()

    @pl.when(student)
    def _():
        for d in started[1][-N_SEND[1]:]:
            d.wait_send()


def shards(axes, tokens, up_weight, down_weight, mod_table, timesteps, valid_counts):
    mod = lax.dynamic_index_in_dim(mod_table[0], timesteps[0], 0, keepdims=False)
    downt = down_weight[0].T.reshape(R, ROWS, 2 * BLK)

    v = pltpu.VMEM
    nred = 2 * R
    scratch = [
        v((NZ, SEQ, BLK), BF),
        v((NZ, 2, 192, BLK), BF),
        v((R, NZ, 2, ROWS, BLK), BF),
        v((2, NZ, SEQ, BLK), BF),
        v((R, 2, NZ * 2 * ROWS, SEQ), BF),
        v((SEQ, BLK), F32),
        v((2, SEQ, BLK), F32),
        v((2, SEQ, BLK), BF),
        v((R, NZ * 2 * ROWS, SEQ), F32),
        v((R, NZ * 2 * ROWS, SEQ), BF),
        v((R, NZ * 2 * ROWS, SEQ), BF),
        v((R, 2, 4, 2 * ROWS, SEQ), BF),
        v((R, 2, 4, 2 * ROWS, SEQ), BF),
        v((BLK, SEQ), F32),
        v((BLK, SEQ), F32),
        v((R, 2, ROWS, SEQ), BF),
        v((R, 2, ROWS, SEQ), BF),
        v((R, 2, NZ * 2 * ROWS, SEQ), BF),
        v((2, SEQ, BLK), F32),
        v((2, SEQ, BLK), BF),
        v((nred, NZ, 2, ROWS, BLK), F32),
        v((nred, 4, 2, ROWS - RA, BLK), BF),
        v((nred, 4, 2, ROWS - RA, BLK), BF),
        v((nred, 2, 2, RA, BLK), BF),
        v((nred, 2, 2, RA, BLK), BF),
        v((nred, 2, 2, 2, RA, BLK), BF),
        v((nred, 2, 2, 2, RA, BLK), BF),
        v((nred, 2, ROWS - RA, BLK), BF),
        v((nred, 2, ROWS - RA, BLK), BF),
        v((nred, 2, 2, ROWS - RA, BLK), BF),
        v((nred, 2, 2, ROWS - RA, BLK), BF),
        v((nred, 2, RA, BLK), BF),
        v((nred, 2, RA, BLK), BF),
        v((nred, ROWS, BLK), BF),
        v((nred, 2, ROWS, BLK), F32),
        v((nred, ROWS, BLK), BF),
        v((nred, 2, ROWS, BLK), BF),
        v((nred, 2, ROWS, BLK), BF),
        pltpu.SemaphoreType.DMA((sum(N_SEND.values()),)),
        pltpu.SemaphoreType.DMA((N_RECV,)),
        pltpu.SemaphoreType.DMA((3,)),
    ]
    hbm = pl.BlockSpec(memory_space=pl.ANY)
    vm = pl.BlockSpec(memory_space=pltpu.VMEM)
    out, up, down = pl.pallas_call(
        functools.partial(kernel, axes),
        out_shape=(
            jax.ShapeDtypeStruct((SEQ, BLK), BF),
            jax.ShapeDtypeStruct((96, 2 * BLK), F32),
            jax.ShapeDtypeStruct((96, 2 * BLK), F32),
        ),
        in_specs=[hbm, hbm, hbm, vm, pl.BlockSpec(memory_space=pltpu.SMEM)],
        out_specs=(vm, vm, vm),
        scratch_shapes=scratch,
        compiler_params=pltpu.CompilerParams(
            collective_id=0, has_side_effects=True, vmem_limit_bytes=67043328
        ),
    )(tokens, up_weight[0], downt, mod, valid_counts)
    return out[None], up, down.T


def solution(mesh):
    placed = (
        P("dp", "mp"),
        P("side", "dp", "mp"),
        P("side", "mp", "dp"),
        P("side", None, None, None),
        P("dp"),
        P(),
    )
    return jax.shard_map(
        functools.partial(shards, mesh.axis_names),
        mesh=mesh,
        in_specs=placed,
        out_specs=(P("side", "dp", "mp"), P(("dp", "side"), "mp"), P("mp", ("dp", "side"))),
        check_vma=False,
    )
```

```python
import functools

import jax
import jax.numpy as jnp
from jax import lax
from jax.experimental import pallas as pl
from jax.experimental.pallas import tpu as pltpu
from jax.sharding import PartitionSpec as P

BF = jnp.bfloat16
F32 = jnp.float32
R = 4
ROWS = 192 // R
RA = 32
NZ = 8
SEQ = 256
BLK = 384
N_RECV = 192
N_SEND = {None: 32, 0: 4, 1: 32}


def gelu_pair(v):
    k = 0.7978845608028654
    v2 = v * v
    t = jnp.tanh(k * v * (1.0 + 0.044715 * v2))
    half = 0.5 * (1.0 + t)
    act = v * half
    slope = half + 0.5 * v * (1.0 - t * t) * (k * (1.0 + 3.0 * 0.044715 * v2))
    return act, slope


def nn(a, b):
    return lax.dot_general(a, b, (((1,), (0,)), ((), ())), preferred_element_type=F32)


def nt(a, b):
    return lax.dot_general(a, b, (((1,), (1,)), ((), ())), preferred_element_type=F32)


def tn(a, b):
    return lax.dot_general(a, b, (((0,), (0,)), ((), ())), preferred_element_type=F32)


def kernel(
    axes,
    tok_ref, up_ref, downt_ref, mod_ref, counts_ref,
    out_ref, ug_ref, dg_ref,
    T, U, D, N, NTR, HP, SL, ACT, PO, PS, PR, ZS, ZR, GATE, TOKT, OTA, OTB, GT, GA, GP,
    QV, XBS, XBR, A2S, A2R, A1S, A1R, B2S, B2R, B1S, B1R, AXS, AXR, FS, FO, FR, HS, HR,
    send, recv, local,
):
    dp, z, s = lax.axis_index("dp"), lax.axis_index("mp"), lax.axis_index("side")
    c = lax.rem(dp, 2)
    y = lax.rem(lax.div(dp, 2), 4)
    xl = lax.div(dp, 8)
    xo = 1 - xl
    yp, ym, y2 = lax.rem(y + 1, 4), lax.rem(y + 3, 4), lax.rem(y + 2, 4)
    oc = 1 - c

    def zz(k):
        return lax.rem(z + (k + NZ), NZ)

    def where(dp_=None, mp_=None, side_=None):
        at = {"dp": dp if dp_ is None else dp_, "mp": z if mp_ is None else mp_, "side": s if side_ is None else side_}
        return tuple(at[a] for a in axes)

    def jj(a, b):
        return a * 4 + b

    X = where(dp_=xo * 8 + y * 2 + c)
    YP = where(dp_=xl * 8 + yp * 2 + c)
    YM = where(dp_=xl * 8 + ym * 2 + c)
    ZP = where(mp_=zz(1))
    ZM = where(mp_=zz(-1))
    C = where(dp_=dp + 1 - 2 * c)
    S = where(side_=1 - s)

    barrier = pltpu.get_barrier_semaphore()
    peers = (X, YP, YM, ZP, ZM, C, S)
    for peer in peers:
        pl.semaphore_signal(barrier, inc=1, device_id=peer, device_id_type=pl.DeviceIdType.MESH)
    pl.semaphore_wait(barrier, len(peers))

    used = [0]
    started = {None: [], 0: [], 1: []}

    class Copy:
        def __init__(self, refs, dev, side, at=None):
            self.refs, self.dev = refs, dev
            if at is None:
                at = used[0]
                used[0] += 1
            self.i = at
            mine = started[side]
            pool = N_SEND[side]
            self.j = len(mine) % pool + {None: 0, 0: N_SEND[None], 1: N_SEND[None] + N_SEND[0]}[side]
            if len(mine) >= pool:
                mine[-pool].wait_send()
            self.made().start()
            mine.append(self)

        def made(self):
            src, dst = self.refs()
            return pltpu.make_async_remote_copy(
                src_ref=src, dst_ref=dst, send_sem=send.at[self.j], recv_sem=recv.at[self.i],
                device_id=self.dev, device_id_type=pl.DeviceIdType.MESH,
            )

        def wait_recv(self):
            self.made().wait_recv()

        def wait_send(self):
            self.made().wait_send()

    def copy(src, dst, dev, side=None, at=None):
        return Copy(lambda: (src(), dst()), dev, side, at)

    def copy_same(ref, dev, side=None, at=None):
        return Copy(lambda: (ref(),) * 2, dev, side, at)

    def wait_bytes(i, ref):
        pltpu.make_async_copy(ref, ref, recv.at[i]).wait()

    student = s == 1

    class Gather:
        def __init__(self, buf, ra, four):
            self.buf, self.ra, self.four = buf, ra, four

        def g0(self):
            self.bx = used[0]
            used[0] += 1
            self.xa = copy_same(lambda: self.apart(xl, y), X)
            self.yp = copy_same(lambda: self.buf(own), YP)
            self.ym = copy_same(lambda: self.buf(own), YM)
            self.xb = copy_same(lambda: self.bpart(xl, y), X, at=self.bx)

        def g1(self):
            self.xa.wait_recv()
            self.xap = copy_same(lambda: self.apart(xo, y), YP)
            self.xam = copy_same(lambda: self.apart(xo, y), YM)

        def apart(self, xx, yy):
            return self.buf(jj(xx, yy)).at[:, pl.ds(0, self.ra)]

        def bpart(self, xx, yy):
            b = self.buf(jj(xx, yy))
            return b.at[:, pl.ds(self.ra, b.shape[1] - self.ra)]

        def g2(self):
            self.yp.wait_recv()
            self.rp = copy_same(lambda: self.buf(jj(xl, ym)).at[0], YP)
            self.bxm = copy_same(lambda: self.bpart(xl, ym), X, at=self.bx)
            self.ym.wait_recv()
            self.rm = copy_same(lambda: self.buf(jj(xl, yp)).at[1], YM)
            self.bxp = copy_same(lambda: self.bpart(xl, yp), X, at=self.bx)

        def g3(self):
            self.xap.wait_recv()
            self.rxp = copy_same(lambda: self.buf(jj(xo, ym)).at[0, pl.ds(0, self.ra)], YP)
            self.xam.wait_recv()
            self.rxm = copy_same(lambda: self.buf(jj(xo, yp)).at[1, pl.ds(0, self.ra)], YM)

        def g4(self):
            self.rp.wait_recv()
            self.rm.wait_recv()
            self.bx2 = copy_same(lambda: self.bpart(xl, y2), X, at=self.bx)

        def g5(self):
            self.rxp.wait_recv()
            self.rxm.wait_recv()
            wait_bytes(self.bx, self.four())

    own = jj(xl, y)
    u_out = copy(lambda: up_ref.at[:, pl.ds(pl.multiple_of(oc * BLK, 128), BLK)], lambda: U.at[own, c], C)
    d_out = copy(lambda: downt_ref.at[:, :, pl.ds(pl.multiple_of(oc * BLK, 128), BLK)], lambda: D.at[:, own, c], C)
    tok_in = pltpu.make_async_copy(tok_ref, T.at[z], local.at[0])
    tok_in.start()
    u_in = pltpu.make_async_copy(up_ref.at[:, pl.ds(pl.multiple_of(c * BLK, 128), BLK)], U.at[own, c], local.at[1])
    u_in.start()
    d_in = pltpu.make_async_copy(
        downt_ref.at[:, :, pl.ds(pl.multiple_of(c * BLK, 128), BLK)], D.at[:, own, c], local.at[2]
    )
    d_in.start()

    tk = {}

    def tok_send(hop):
        for p in range(2):
            rows = pl.ds(128 * p, 128)
            if hop:
                if ("+", hop - 1, p) in tk:
                    tk["+", hop - 1, p].wait_recv()
            at = functools.partial(lambda k, rows: tok_ref.at[rows] if k is None else T.at[zz(k), rows], rows=rows)
            src = functools.partial(at, None if hop == 0 else -hop)
            if hop < 3 or p == 0:
                tk["+", hop, p] = copy(src, functools.partial(at, -hop), ZP)
            if hop:
                if ("-", hop - 1, p) in tk:
                    tk["-", hop - 1, p].wait_recv()
            src = functools.partial(at, None if hop == 0 else hop)
            if hop < 3 or p == 1:
                tk["-", hop, p] = copy(src, functools.partial(at, hop), ZM)

    gu = Gather(lambda j: U.at[j], 128, lambda: U.at[0:4, :, 128:192])
    gd = [
        Gather(functools.partial(lambda r, j: D.at[r, j], r), RA, functools.partial(lambda r: D.at[r, 0:4, :, RA:ROWS], r))
        for r in range(R)
    ]

    tok_send(0)
    u_in.wait()
    u_out.wait_recv()
    gu.g0()
    tok_in.wait()
    gate = mod_ref[2:3, pl.ds(pl.multiple_of(z * BLK, 128), BLK)]
    gate = jnp.transpose(jnp.broadcast_to(gate, (128, BLK)))
    GATE[:, 0:128] = gate
    GATE[:, 128:256] = gate
    tt = jnp.transpose(T[z].astype(F32))
    TOKT[...] = tt
    tok_send(1)
    gu.g1()
    tok_send(2)
    gu.g2()
    d_in.wait()
    d_out.wait_recv()
    gu.g3()
    gd[0].g0()
    gd[1].g0()
    tok_send(3)
    gu.g4()
    gd[2].g0()
    gd[3].g0()
    tk["+", 3, 0].wait_recv()
    tk["-", 3, 1].wait_recv()

    def norm_rows(i, carry):
        rows = pl.ds(pl.multiple_of(i * 16, 16), 16)
        x = [T[b, rows].astype(F32) for b in range(NZ)]
        total = x[0]
        for b in range(1, NZ):
            total = total + x[b]
        mean = jnp.sum(total, axis=-1, keepdims=True) * (1.0 / (NZ * BLK))
        x = [v - mean for v in x]
        sq = x[0] * x[0]
        for b in range(1, NZ):
            sq = sq + x[b] * x[b]
        var = jnp.sum(sq, axis=-1, keepdims=True) * (1.0 / (NZ * BLK))
        rs = lax.rsqrt(var + 1e-06)
        for b in range(NZ):
            cols = slice(b * BLK, (b + 1) * BLK)
            n = x[b] * rs * (1.0 + mod_ref[1:2, cols]) + mod_ref[0:1, cols]
            N[c, b, rows] = n.astype(BF)
        return carry

    n_out = []

    def norm_half(p):
        lax.fori_loop(8 * p, 8 * p + 8, norm_rows, 0)
        n_out.append(copy_same(lambda: N.at[c, :, pl.ds(128 * p, 128)], C))

    def hidden(img):
        h = nn(N[img, 0], U[0].reshape(BLK, BLK))
        for b in range(1, NZ):
            h = h + nn(N[img, b], U[b].reshape(BLK, BLK))
        HP[...] = h

        def act_rows(i, carry):
            rows = pl.ds(pl.multiple_of(i * 32, 32), 32)
            a, g = gelu_pair(HP[rows])
            ACT[img, rows] = a.astype(BF)
            SL[img, rows] = g
            return carry

        lax.fori_loop(0, SEQ // 32, act_rows, 0)

    norm_half(0)
    gd[0].g1()
    gd[0].g2()
    gd[1].g1()
    gd[1].g2()
    norm_half(1)
    gu.g5()
    gd[2].g1()
    gd[2].g2()
    gd[0].g3()
    hidden(c)
    gd[3].g1()
    gd[3].g2()
    gd[0].g4()
    gd[1].g3()
    gd[1].g4()
    for d in n_out:
        d.wait_recv()

    m_out, zs = {}, {}

    def mixed(r):
        w = D[r].reshape(NZ * 2 * ROWS, BLK)
        PS[r] = nt(w, ACT[oc]).astype(BF)
        m_out[r] = copy(lambda: PS.at[r], lambda: PR.at[r], C)
        PO[r] = nt(w, ACT[c])

    def val(r, b):
        rows = pl.ds(pl.multiple_of(b * 2 * ROWS, 32), 2 * ROWS)
        return PO[r, rows] + PR[r, rows].astype(F32)

    def zstage(r, k):
        h0, h1 = pl.ds(0, ROWS), pl.ds(ROWS, ROWS)
        if k == 0:
            m_out[r].wait_recv()
            v = val(r, zz(4)).astype(BF)
            ZS[r, 0, 0] = v
            zs[r, 0, 0] = copy(lambda: ZS.at[r, 0, 0, h0], lambda: ZR.at[r, 0, 0, h0], ZP)
            zs[r, 1, 0] = copy(lambda: ZS.at[r, 0, 0, h1], lambda: ZR.at[r, 1, 0, h1], ZM)
            return
        for q in range(2):
            zs[r, q, k - 1].wait_recv()
            v = val(r, zz((4 - k) if q == 0 else (k - 4)))
            if k == 1:
                h = slice(0, ROWS) if q == 0 else slice(ROWS, 2 * ROWS)
                g = slice(ROWS, 2 * ROWS) if q == 0 else slice(0, ROWS)
                ZS[r, q, k, h] = (v[h] + ZR[r, q, 0, h].astype(F32)).astype(BF)
                ZS[r, q, k, g] = v[g].astype(BF)
            else:
                ZS[r, q, k] = (v + ZR[r, q, k - 1].astype(F32)).astype(BF)
            at = functools.partial(lambda ref, q: ref.at[r, q, k], q=q)
            zs[r, q, k] = copy(functools.partial(at, ZS), functools.partial(at, ZR), ZP if q == 0 else ZM)

    sw = {}

    def rows_of(r, h):
        return slice(192 * h + ROWS * r, 192 * h + ROWS * (r + 1))

    def output(r):
        zs[r, 0, 3].wait_recv()
        zs[r, 1, 3].wait_recv()
        m = val(r, z) + ZR[r, 0, 3].astype(F32) + ZR[r, 1, 3].astype(F32)
        for h in range(2):
            w = rows_of(r, h)
            o = (TOKT[w] + GATE[w] * m[ROWS * h:ROWS * (h + 1)]).astype(BF)
            OTA[r, h] = o
            TOKT[w] = o.astype(F32)

        @pl.when(s == 0)
        def _():
            sw[r] = copy(lambda: OTA.at[r], lambda: OTB.at[r], S, 0)

    ag, fw = {}, {}
    for r in range(R):
        fw[r] = used[0]
        used[0] += 1

    def gslice(r, img, b, h):
        n = ROWS if h is not None else 2 * ROWS
        return GT.at[r, img, pl.ds(pl.multiple_of(b * 2 * ROWS + (h or 0) * ROWS, 16), n)]

    def astage(r, k):
        @pl.when(student)
        def _():
            def push(kk, dev, h=None):
                return copy_same(lambda: gslice(r, c, zz(kk), h), dev, 1, fw[r] if dev is C else None)

            if k == 0:
                sw[r].wait_recv()
                total = counts_ref[0]
                for k_ in range(1, 16):
                    total = total + counts_ref[k_]
                norm = jnp.sqrt(jnp.full((1, SEQ), total, jnp.int32).astype(F32))
                at = lax.broadcasted_iota(jnp.int32, (1, SEQ), 1)
                vrow = jnp.where(at < counts_ref[dp], 1.0, 0.0) / norm
                for h in range(2):
                    w = rows_of(r, h)
                    diff = OTA[r, h].astype(F32) - OTB[r, h].astype(F32)
                    rows = pl.ds(pl.multiple_of(z * 2 * ROWS + h * ROWS, 16), ROWS)
                    GT[r, c, rows] = (GATE[w] * diff * vrow).astype(BF)
                ag[r, 0, 0] = push(0, ZP)
                ag[r, 1, 0] = push(0, ZM)
                push(0, C)
                return
            ag[r, 0, k - 1].wait_recv()
            h = 0 if k > 2 else None
            if k < 4:
                ag[r, 0, k] = push(-k, ZP, h)
            push(-k, C, None if k < 4 else 0)
            ag[r, 1, k - 1].wait_recv()
            h = 1 if k > 2 else None
            if k < 4:
                ag[r, 1, k] = push(k, ZM, h)
            push(k, C, None if k < 4 else 1)

    red_sems = [[used[0] + 11 * i + j for j in range(11)] for i in range(R)]
    used[0] += 11 * R

    class Reduce:
        def __init__(self, kind, r):
            self.i = kind * R + r
            self.r, self.kind = r, kind

        def sem(self, name):
            return red_sems[self.r][self.names.index(name)]

        names = ("a20", "a21", "a10", "a11", "b20", "b21", "b10", "b11", "xb", "ax", "f")

        def both(self, name, src, dst):
            def one(h):
                at = self.sem(name + str(h))
                return copy(lambda: src.at[self.i, h], lambda: dst.at[self.i, h], (YP, YM)[h], 1, at)

            return [one(0), one(1)]

        def q(self, j, rows):
            return QV[self.i, j, :, rows]

        def r0(self):
            i, a, b = self.i, slice(0, RA), slice(RA, ROWS)
            for h in range(2):
                for x in range(2):
                    A2S[i, h, x] = QV[self.i, jj(x, y2), h, a].astype(BF)
            self.a2 = self.both("a2", A2S, A2R)
            for k in range(4):
                XBS[i, k] = QV[self.i, jj(xo, k), :, b].astype(BF)
            self.xb = copy(lambda: XBS.at[i], lambda: XBR.at[i], X, 1, self.sem("xb"))

        def r1(self):
            i, a = self.i, slice(0, RA)
            for h in range(2):
                self.a2[h].wait_recv()
                for x in range(2):
                    v = self.q(jj(x, (yp, ym)[h]), a)
                    A1S[i, h, x, h] = (v[h] + A2R[i, h, x].astype(F32)).astype(BF)
                    A1S[i, h, x, 1 - h] = v[1 - h].astype(BF)
            self.a1 = self.both("a1", A1S, A1R)

        def r2(self):
            i, b = self.i, slice(RA, ROWS)
            self.xb.wait_recv()
            v = self.q(jj(xl, y2), b) + XBR[i, y2].astype(F32)
            B2S[i] = v.astype(BF)
            self.b2 = self.both("b2", B2S, B2R)

        def r3(self):
            i, b = self.i, slice(RA, ROWS)
            for h in range(2):
                self.a1[h].wait_recv()
            for h in range(2):
                self.b2[h].wait_recv()
                yy = (yp, ym)[h]
                v = self.q(jj(xl, yy), b) + XBR[i, yy].astype(F32)
                B1S[i, h, h] = (v[h] + B2R[i, h].astype(F32)).astype(BF)
                B1S[i, h, 1 - h] = v[1 - h].astype(BF)
            self.b1 = self.both("b1", B1S, B1R)

        def r4(self):
            i, a = self.i, slice(0, RA)
            v = self.q(jj(xo, y), a) + A1R[i, 0, xo].astype(F32) + A1R[i, 1, xo].astype(F32)
            AXS[i] = v.astype(BF)
            self.ax = copy(lambda: AXS.at[i], lambda: AXR.at[i], X, 1, self.sem("ax"))

        def r5(self):
            i, a, b = self.i, slice(0, RA), slice(RA, ROWS)
            for d in (self.ax, *self.b1):
                d.wait_recv()
            va = self.q(own, a) + A1R[i, 0, xl].astype(F32) + A1R[i, 1, xl].astype(F32) + AXR[i].astype(F32)
            vb = self.q(own, b) + XBR[i, y].astype(F32) + B1R[i, 0].astype(F32) + B1R[i, 1].astype(F32)
            FO[i, :, a] = va
            FO[i, :, b] = vb
            FS[i] = FO[i, oc].astype(BF)
            self.f = copy(lambda: FS.at[i], lambda: FR.at[i], C, 1, self.sem("f"))

        def r6(self):
            i = self.i
            self.f.wait_recv()
            if self.r < R // 2:
                HS[i, c] = FO[i, c].astype(BF)
                HS[i, oc] = FR[i]
                self.h = copy(lambda: HS.at[i], lambda: HR.at[i], S, 1)
            else:
                o = (ug_ref, dg_ref)[self.kind]
                rows = slice(ROWS * (self.r - R // 2), ROWS * (self.r - R // 2 + 1))

                @pl.when(c == 0)
                def _():
                    o[rows, 0:BLK] = FO[i, 0]
                    o[rows, BLK:2 * BLK] = FR[i].astype(F32)

                @pl.when(c == 1)
                def _():
                    o[rows, 0:BLK] = FR[i].astype(F32)
                    o[rows, BLK:2 * BLK] = FO[i, 1]

    red = {(k, r): Reduce(k, r) for k in range(2) for r in range(R)}

    def down_grads(r):
        g = [GT[r, 0], GT[r, 1]]
        q = nn(g[0], ACT[0]) + nn(g[1], ACT[1])
        QV[R + r] = q.reshape(NZ, 2, ROWS, BLK)

    def grad_act(r):
        w = D[r].reshape(NZ * 2 * ROWS, BLK)
        for img in range(2):
            v = tn(GT[r, img], w)
            if r == 0:
                GA[img] = v
            else:
                GA[img] += v

    def arrived(r):
        wait_bytes(fw[r], GT.at[r, 0])

    def transposed(part):
        def one(i, carry):
            img, j = lax.div(i, 8), lax.rem(i, 8)
            t = jnp.transpose(N[img, j].astype(F32)).astype(BF)
            for r in range(R):
                for h in range(2):
                    NTR[r, img, pl.ds(pl.multiple_of(j * 2 * ROWS + h * ROWS, 16), ROWS)] = t[rows_of(r, h)]
            return carry

        lax.fori_loop(4 * part, 4 * part + 4, one, 0)

    def up_grads(r):
        if r == 0:
            for img in range(2):
                GP[img] = (GA[img] * SL[img]).astype(BF)
        q = nn(NTR[r, 0], GP[0]) + nn(NTR[r, 1], GP[1])
        QV[r] = q.reshape(NZ, 2, ROWS, BLK)

    def stage(n, k):
        if k < 4:
            zstage(n, k)
        elif k == 4:
            output(n)
        elif k < 10:
            astage(n, k - 5)
        else:
            e = red[(1, n) if n < R else (0, n - R)]
            if k == 10:
                if n < R:
                    arrived(n)
                    down_grads(n)
                    e.r0()
                    grad_act(n)
                else:
                    up_grads(n - R)
                    e.r0()
            elif k == 11:
                e.r1()
                e.r2()
            elif k == 12:
                e.r3()
                e.r4()
            elif k == 13:
                e.r5()
            else:
                e.r6()

    def diagonal(d):
        for n in reversed(range(2 * R)):
            k = d - n
            if 0 <= k < 15 and (n < R or k >= 10):
                stage(n, k)

    hidden(oc)
    gd[2].g3()
    gd[2].g4()
    gd[0].g5()
    mixed(0)
    gd[3].g3()
    gd[3].g4()
    gd[1].g5()
    mixed(1)
    zstage(0, 0)
    gd[2].g5()
    mixed(2)
    zstage(1, 0)
    zstage(0, 1)
    gd[3].g5()
    mixed(3)
    diagonal(2)
    for d in range(3, R + 4):
        diagonal(d)
    out_ref[...] = jnp.transpose(TOKT[...]).astype(BF)

    @pl.when(student)
    def _():
        for d in range(R + 4, 15 + 2 * R - 1):
            diagonal(d)
            if d < R + 8:
                transposed(d - R - 4)

    @pl.when(s == 0)
    def _():
        for k in (1, 0):
            o = (ug_ref, dg_ref)[k]
            for r in range(R // 2):
                red[k, r].h.wait_recv()
                for h in range(2):
                    o[ROWS * r:ROWS * (r + 1), BLK * h:BLK * (h + 1)] = HR[k * R + r, h].astype(F32)

    for d in started[None][-N_SEND[None]:]:
        d.wait_send()

    @pl.when(s == 0)
    def _():
        for d in started[0][-N_SEND[0]:]:
            d.wait_send()

    @pl.when(student)
    def _():
        for d in started[1][-N_SEND[1]:]:
            d.wait_send()


def shards(axes, tokens, up_weight, down_weight, mod_table, timesteps, valid_counts):
    mod = lax.dynamic_index_in_dim(mod_table[0], timesteps[0], 0, keepdims=False)
    downt = down_weight[0].T.reshape(R, ROWS, 2 * BLK)

    v = pltpu.VMEM
    nred = 2 * R
    scratch = [
        v((NZ, SEQ, BLK), BF),
        v((NZ, 2, 192, BLK), BF),
        v((R, NZ, 2, ROWS, BLK), BF),
        v((2, NZ, SEQ, BLK), BF),
        v((R, 2, NZ * 2 * ROWS, SEQ), BF),
        v((SEQ, BLK), F32),
        v((2, SEQ, BLK), F32),
        v((2, SEQ, BLK), BF),
        v((R, NZ * 2 * ROWS, SEQ), F32),
        v((R, NZ * 2 * ROWS, SEQ), BF),
        v((R, NZ * 2 * ROWS, SEQ), BF),
        v((R, 2, 4, 2 * ROWS, SEQ), BF),
        v((R, 2, 4, 2 * ROWS, SEQ), BF),
        v((BLK, SEQ), F32),
        v((BLK, SEQ), F32),
        v((R, 2, ROWS, SEQ), BF),
        v((R, 2, ROWS, SEQ), BF),
        v((R, 2, NZ * 2 * ROWS, SEQ), BF),
        v((2, SEQ, BLK), F32),
        v((2, SEQ, BLK), BF),
        v((nred, NZ, 2, ROWS, BLK), F32),
        v((nred, 4, 2, ROWS - RA, BLK), BF),
        v((nred, 4, 2, ROWS - RA, BLK), BF),
        v((nred, 2, 2, RA, BLK), BF),
        v((nred, 2, 2, RA, BLK), BF),
        v((nred, 2, 2, 2, RA, BLK), BF),
        v((nred, 2, 2, 2, RA, BLK), BF),
        v((nred, 2, ROWS - RA, BLK), BF),
        v((nred, 2, ROWS - RA, BLK), BF),
        v((nred, 2, 2, ROWS - RA, BLK), BF),
        v((nred, 2, 2, ROWS - RA, BLK), BF),
        v((nred, 2, RA, BLK), BF),
        v((nred, 2, RA, BLK), BF),
        v((nred, ROWS, BLK), BF),
        v((nred, 2, ROWS, BLK), F32),
        v((nred, ROWS, BLK), BF),
        v((nred, 2, ROWS, BLK), BF),
        v((nred, 2, ROWS, BLK), BF),
        pltpu.SemaphoreType.DMA((sum(N_SEND.values()),)),
        pltpu.SemaphoreType.DMA((N_RECV,)),
        pltpu.SemaphoreType.DMA((3,)),
    ]
    hbm = pl.BlockSpec(memory_space=pl.ANY)
    vm = pl.BlockSpec(memory_space=pltpu.VMEM)
    out, up, down = pl.pallas_call(
        functools.partial(kernel, axes),
        out_shape=(
            jax.ShapeDtypeStruct((SEQ, BLK), BF),
            jax.ShapeDtypeStruct((96, 2 * BLK), F32),
            jax.ShapeDtypeStruct((96, 2 * BLK), F32),
        ),
        in_specs=[hbm, hbm, hbm, vm, pl.BlockSpec(memory_space=pltpu.SMEM)],
        out_specs=(vm, vm, vm),
        scratch_shapes=scratch,
        compiler_params=pltpu.CompilerParams(
            collective_id=0, has_side_effects=True, vmem_limit_bytes=67043328
        ),
    )(tokens, up_weight[0], downt, mod, valid_counts)
    def settle(out_in, up_in, down_in, out_to, up_to, down_to):
        out_to[...] = out_in[...]
        up_to[...] = up_in[...]
        down_to[...] = down_in[...]

    out, up, down = pl.pallas_call(
        settle,
        out_shape=(
            jax.ShapeDtypeStruct((SEQ, BLK), BF),
            jax.ShapeDtypeStruct((96, 2 * BLK), F32),
            jax.ShapeDtypeStruct((96, 2 * BLK), F32),
        ),
        in_specs=[vm] * 3,
        out_specs=(vm,) * 3,
    )(out, up, down)
    return out[None], up, down.T


def solution(mesh):
    placed = (
        P("dp", "mp"),
        P("side", "dp", "mp"),
        P("side", "mp", "dp"),
        P("side", None, None, None),
        P("dp"),
        P(),
    )
    return jax.shard_map(
        functools.partial(shards, mesh.axis_names),
        mesh=mesh,
        in_specs=placed,
        out_specs=(P("side", "dp", "mp"), P(("dp", "side"), "mp"), P("mp", ("dp", "side"))),
        check_vma=False,
    )
```

```python
import functools

import jax
import jax.numpy as jnp
from jax import lax
from jax.experimental import pallas as pl
from jax.experimental.pallas import tpu as pltpu
from jax.sharding import PartitionSpec as P

BF = jnp.bfloat16
F32 = jnp.float32
R = 4
ROWS = 192 // R
RA = (32, 32, 32, 16)
RU = 112
NZ = 8
SEQ = 256
BLK = 384
N_RECV = 145
N_SEND = {None: 40, 1: 2}


def gelu_pair(v):
    k = 0.7978845608028654
    v2 = v * v
    t = jnp.tanh(k * v * (1.0 + 0.044715 * v2))
    half = 0.5 * (1.0 + t)
    act = v * half
    slope = half + 0.5 * v * (1.0 - t * t) * (k * (1.0 + 3.0 * 0.044715 * v2))
    return act, slope


def nn(a, b):
    return lax.dot_general(a, b, (((1,), (0,)), ((), ())), preferred_element_type=F32)


def nt(a, b):
    return lax.dot_general(a, b, (((1,), (1,)), ((), ())), preferred_element_type=F32)


def tn(a, b):
    return lax.dot_general(a, b, (((0,), (0,)), ((), ())), preferred_element_type=F32)


def kernel(
    axes,
    tok_ref, up_ref, downt_ref, mod_ref, counts_ref,
    out_ref, ug_ref, dg_ref,
    T, U, D, N, NTR, HP, SL, ACT, ACTG, PO, PS, PR, ZS, ZR, MODO, GATE, GATEG, TOKT, OTA, OTB, GT, GA, GP,
    QV, XBS, XBR, A2S, A2R, A1S, A1R, B2S, B2R, B1S, B1R, AXS, AXR, FS, FO, FR, HS, HR,
    send, recv, local,
):
    dp, z, s = lax.axis_index("dp"), lax.axis_index("mp"), lax.axis_index("side")
    c = lax.rem(dp, 2)
    y = lax.rem(lax.div(dp, 2), 4)
    xl = lax.div(dp, 8)
    xo = 1 - xl
    yp, ym, y2 = lax.rem(y + 1, 4), lax.rem(y + 3, 4), lax.rem(y + 2, 4)
    oc = 1 - c

    def zz(k):
        return lax.rem(z + (k + NZ), NZ)

    def where(dp_=None, mp_=None, side_=None):
        at = {"dp": dp if dp_ is None else dp_, "mp": z if mp_ is None else mp_, "side": s if side_ is None else side_}
        return tuple(at[a] for a in axes)

    def jj(a, b):
        return a * 4 + b

    X = where(dp_=xo * 8 + y * 2 + c)
    YP = where(dp_=xl * 8 + yp * 2 + c)
    YM = where(dp_=xl * 8 + ym * 2 + c)
    ZP = where(mp_=zz(1))
    ZM = where(mp_=zz(-1))
    C = where(dp_=dp + 1 - 2 * c)
    S = where(side_=1 - s)

    barrier = pltpu.get_barrier_semaphore()
    peers = (X, YP, YM, ZP, ZM, C, S)
    for peer in peers:
        pl.semaphore_signal(barrier, inc=1, device_id=peer, device_id_type=pl.DeviceIdType.MESH)
    pl.semaphore_wait(barrier, len(peers))

    used = [0]
    started = {None: [], 1: []}

    class Copy:
        def __init__(self, refs, dev, side, at=None):
            self.refs, self.dev = refs, dev
            if at is None:
                at = used[0]
                used[0] += 1
            self.i = at
            mine = started[side]
            pool = N_SEND[side]
            self.j = len(mine) % pool + {None: 0, 1: N_SEND[None]}[side]
            if len(mine) >= pool:
                mine[-pool].wait_send()
            self.made().start()
            mine.append(self)

        def made(self):
            src, dst = self.refs()
            return pltpu.make_async_remote_copy(
                src_ref=src, dst_ref=dst, send_sem=send.at[self.j], recv_sem=recv.at[self.i],
                device_id=self.dev, device_id_type=pl.DeviceIdType.MESH,
            )

        def wait_recv(self):
            self.made().wait_recv()

        def wait_send(self):
            self.made().wait_send()

    def copy(src, dst, dev, side=None, at=None):
        return Copy(lambda: (src(), dst()), dev, side, at)

    def copy_same(ref, dev, side=None, at=None):
        return Copy(lambda: (ref(),) * 2, dev, side, at)

    def wait_bytes(i, ref):
        pltpu.make_async_copy(ref, ref, recv.at[i]).wait()

    student = s == 1

    class Gather:
        def __init__(self, buf, ra, four):
            self.buf, self.ra, self.four = buf, ra, four

        def g0(self):
            self.bx = used[0]
            used[0] += 1
            self.xa = copy_same(lambda: self.apart(xl, y), X)
            self.yp = copy_same(lambda: self.buf(own), YP)
            self.ym = copy_same(lambda: self.buf(own), YM)
            self.xb = copy_same(lambda: self.bpart(xl, y), X, at=self.bx)

        def g1(self):
            self.xa.wait_recv()
            self.xap = copy_same(lambda: self.apart(xo, y), YP)
            self.xam = copy_same(lambda: self.apart(xo, y), YM)

        def apart(self, xx, yy):
            return self.buf(jj(xx, yy)).at[:, pl.ds(0, self.ra)]

        def bpart(self, xx, yy):
            b = self.buf(jj(xx, yy))
            return b.at[:, pl.ds(self.ra, b.shape[1] - self.ra)]

        def g2(self):
            self.yp.wait_recv()
            self.rp = copy_same(lambda: self.buf(jj(xl, ym)).at[0], YP)
            self.bxm = copy_same(lambda: self.bpart(xl, ym), X, at=self.bx)
            self.ym.wait_recv()
            self.rm = copy_same(lambda: self.buf(jj(xl, yp)).at[1], YM)
            self.bxp = copy_same(lambda: self.bpart(xl, yp), X, at=self.bx)

        def g3(self):
            self.xap.wait_recv()
            self.rxp = copy_same(lambda: self.buf(jj(xo, ym)).at[0, pl.ds(0, self.ra)], YP)
            self.xam.wait_recv()
            self.rxm = copy_same(lambda: self.buf(jj(xo, yp)).at[1, pl.ds(0, self.ra)], YM)

        def g4(self):
            self.rp.wait_recv()
            self.rm.wait_recv()
            self.bx2 = copy_same(lambda: self.bpart(xl, y2), X, at=self.bx)

        def g5(self):
            self.rxp.wait_recv()
            self.rxm.wait_recv()
            wait_bytes(self.bx, self.four())

    own = jj(xl, y)
    u_out = copy(lambda: up_ref.at[:, pl.ds(pl.multiple_of(oc * BLK, 128), BLK)], lambda: U.at[own, c], C)
    d_out = copy(lambda: downt_ref.at[:, :, pl.ds(pl.multiple_of(oc * BLK, 128), BLK)], lambda: D.at[:, own, c], C)
    tok_in = pltpu.make_async_copy(tok_ref, T.at[z], local.at[0])
    tok_in.start()
    u_in = pltpu.make_async_copy(up_ref.at[:, pl.ds(pl.multiple_of(c * BLK, 128), BLK)], U.at[own, c], local.at[1])
    u_in.start()
    d_in = pltpu.make_async_copy(
        downt_ref.at[:, :, pl.ds(pl.multiple_of(c * BLK, 128), BLK)], D.at[:, own, c], local.at[2]
    )
    d_in.start()

    tk = {}

    def tok_send(hop):
        for p in range(2):
            rows = pl.ds(128 * p, 128)
            if hop:
                if ("+", hop - 1, p) in tk:
                    tk["+", hop - 1, p].wait_recv()
            at = functools.partial(lambda k, rows: tok_ref.at[rows] if k is None else T.at[zz(k), rows], rows=rows)
            src = functools.partial(at, None if hop == 0 else -hop)
            if hop < 3 or p == 0:
                tk["+", hop, p] = copy(src, functools.partial(at, -hop), ZP)
            if hop:
                if ("-", hop - 1, p) in tk:
                    tk["-", hop - 1, p].wait_recv()
            src = functools.partial(at, None if hop == 0 else hop)
            if hop < 3 or p == 1:
                tk["-", hop, p] = copy(src, functools.partial(at, hop), ZM)

    gu = Gather(lambda j: U.at[j], RU, lambda: U.at[0:4, :, RU:192])
    gd = [
        Gather(
            functools.partial(lambda r, j: D.at[r, j], r), RA[r],
            functools.partial(lambda r: D.at[r, 0:4, :, RA[r]:ROWS], r),
        )
        for r in range(R)
    ]

    tok_send(0)
    mod_out = copy(lambda: mod_ref, lambda: MODO, S)
    u_in.wait()
    u_out.wait_recv()
    gu.g0()
    tok_in.wait()
    gate = mod_ref[2:3, pl.ds(pl.multiple_of(z * BLK, 128), BLK)]
    gate = jnp.transpose(jnp.broadcast_to(gate, (128, BLK)))
    GATE[:, 0:128] = gate
    GATE[:, 128:256] = gate

    def gate_of_student():
        mod_out.wait_recv()
        at = pl.ds(pl.multiple_of(z * BLK, 128), BLK)
        g = jnp.where(jnp.full((1, BLK), s) == 1, mod_ref[2:3, at], MODO[2:3, at])
        g = jnp.transpose(jnp.broadcast_to(g, (128, BLK)))
        GATEG[:, 0:128] = g
        GATEG[:, 128:256] = g

    tt = jnp.transpose(T[z].astype(F32))
    TOKT[...] = tt
    tok_send(1)
    gu.g1()
    tok_send(2)
    gu.g2()
    d_in.wait()
    d_out.wait_recv()
    gu.g3()
    gd[0].g0()
    tok_send(3)
    gu.g4()
    gd[1].g0()
    tk["+", 3, 0].wait_recv()
    tk["-", 3, 1].wait_recv()

    def norm_rows(i, carry):
        rows = pl.ds(pl.multiple_of(i * 16, 16), 16)
        x = [T[b, rows].astype(F32) for b in range(NZ)]
        total = x[0]
        for b in range(1, NZ):
            total = total + x[b]
        mean = jnp.sum(total, axis=-1, keepdims=True) * (1.0 / (NZ * BLK))
        x = [v - mean for v in x]
        sq = x[0] * x[0]
        for b in range(1, NZ):
            sq = sq + x[b] * x[b]
        var = jnp.sum(sq, axis=-1, keepdims=True) * (1.0 / (NZ * BLK))
        rs = lax.rsqrt(var + 1e-06)
        for b in range(NZ):
            cols = slice(b * BLK, (b + 1) * BLK)
            n = x[b] * rs * (1.0 + mod_ref[1:2, cols]) + mod_ref[0:1, cols]
            N[c, b, rows] = n.astype(BF)
        return carry

    n_out = []

    def norm_half(p):
        lax.fori_loop(8 * p, 8 * p + 8, norm_rows, 0)
        n_out.append(copy_same(lambda: N.at[c, :, pl.ds(128 * p, 128)], C))

    def hidden(img):
        h = nn(N[img, 0], U[0].reshape(BLK, BLK))
        for b in range(1, NZ):
            h = h + nn(N[img, b], U[b].reshape(BLK, BLK))
        HP[...] = h

        def act_rows(i, carry):
            rows = pl.ds(pl.multiple_of(i * 32, 32), 32)
            a, g = gelu_pair(HP[rows])
            ACT[img, rows] = a.astype(BF)
            SL[img, rows] = g
            return carry

        lax.fori_loop(0, SEQ // 32, act_rows, 0)

    act_out = []

    def send_act(img):
        @pl.when(student)
        def _():
            act_out.append(copy(lambda: ACT.at[img()], lambda: ACTG.at[img()], S, 1))

    norm_half(0)
    gd[0].g1()
    gd[0].g2()
    norm_half(1)
    gu.g5()
    gd[2].g0()
    gd[1].g1()
    gd[1].g2()
    gd[0].g3()
    hidden(c)
    send_act(lambda: c)
    gd[0].g4()
    gd[3].g0()
    gd[2].g1()
    gd[2].g2()
    gd[1].g3()
    for d in n_out:
        d.wait_recv()

    m_out, zs = {}, {}
    z_sems = used[0]
    used[0] += 4 * R

    def ring(r, q, k):
        return z_sems + 4 * r + 2 * q + k % 2


    def mixed(r):
        w = D[r].reshape(NZ * 2 * ROWS, BLK)
        PS[r] = nt(w, ACT[oc]).astype(BF)
        m_out[r] = copy(lambda: PS.at[r], lambda: PR.at[r], C)
        PO[r] = nt(w, ACT[c])

    def val(r, b):
        rows = pl.ds(pl.multiple_of(b * 2 * ROWS, 32), 2 * ROWS)
        return PO[r, rows] + PR[r, rows].astype(F32)

    def zstage(r, k):
        h0, h1 = pl.ds(0, ROWS), pl.ds(ROWS, ROWS)
        if k == 0:
            m_out[r].wait_recv()
            v = val(r, zz(4)).astype(BF)
            ZS[r, 0, 0] = v
            zs[r, 0, 0] = copy(lambda: ZS.at[r, 0, 0, h0], lambda: ZR.at[r, 0, 0, h0], ZP, None, ring(r, 0, 0))
            zs[r, 1, 0] = copy(lambda: ZS.at[r, 0, 0, h1], lambda: ZR.at[r, 1, 0, h1], ZM, None, ring(r, 1, 0))
            return
        for q in range(2):
            zs[r, q, k - 1].wait_recv()
        for q in range(2):
            v = val(r, zz((4 - k) if q == 0 else (k - 4)))
            if k == 1:
                h = slice(0, ROWS) if q == 0 else slice(ROWS, 2 * ROWS)
                g = slice(ROWS, 2 * ROWS) if q == 0 else slice(0, ROWS)
                ZS[r, q, k, h] = (v[h] + ZR[r, q, 0, h].astype(F32)).astype(BF)
                ZS[r, q, k, g] = v[g].astype(BF)
            else:
                ZS[r, q, k] = (v + ZR[r, q, k - 1].astype(F32)).astype(BF)
            at = functools.partial(lambda ref, q: ref.at[r, q, k], q=q)
            to = ZP if q == 0 else ZM
            zs[r, q, k] = copy(functools.partial(at, ZS), functools.partial(at, ZR), to, None, ring(r, q, k))

    sw = {}

    def rows_of(r, h):
        return slice(192 * h + ROWS * r, 192 * h + ROWS * (r + 1))

    def output(r):
        zs[r, 0, 3].wait_recv()
        zs[r, 1, 3].wait_recv()
        m = val(r, z) + ZR[r, 0, 3].astype(F32) + ZR[r, 1, 3].astype(F32)
        for h in range(2):
            w = rows_of(r, h)
            o = (TOKT[w] + GATE[w] * m[ROWS * h:ROWS * (h + 1)]).astype(BF)
            OTA[r, h] = o
            TOKT[w] = o.astype(F32)

        sw[r] = copy(lambda: OTA.at[r], lambda: OTB.at[r], S)

    ag, fw = {}, {}
    for r in range(R):
        fw[r] = used[0]
        used[0] += 1

    def gslice(r, img, b, h):
        n = ROWS if h is not None else 2 * ROWS
        return GT.at[r, img, pl.ds(pl.multiple_of(b * 2 * ROWS + (h or 0) * ROWS, 16), n)]

    def astage(r, k):
        def push(kk, dev, h=None, at=None):
            return copy_same(lambda: gslice(r, c, zz(kk), h), dev, None, fw[r] if at is None else at)

        if k == 0:
            sw[r].wait_recv()
            total = counts_ref[0]
            for i in range(1, 16):
                total = total + counts_ref[i]
            norm = jnp.sqrt(jnp.full((1, SEQ), total, jnp.int32).astype(F32))
            at = lax.broadcasted_iota(jnp.int32, (1, SEQ), 1)
            vrow = jnp.where(at < counts_ref[dp], (2 * s - 1).astype(F32), 0.0) / norm
            for h in range(2):
                w = rows_of(r, h)
                diff = OTA[r, h].astype(F32) - OTB[r, h].astype(F32)
                rows = pl.ds(pl.multiple_of(z * 2 * ROWS + h * ROWS, 16), ROWS)
                GT[r, c, rows] = (GATEG[w] * diff * vrow).astype(BF)
            ag[r, 0, 0] = push(0, ZP, at=ring(r, 0, 4))
            ag[r, 1, 0] = push(0, ZM, at=ring(r, 1, 4))
            push(0, C)
            return
        ag[r, 0, k - 1].wait_recv()
        ag[r, 1, k - 1].wait_recv()
        if k < 4:
            ag[r, 0, k] = push(-k, ZP, 0 if k > 2 else None, ring(r, 0, 4 + k))
        push(-k, C, None if k < 4 else 0)
        if k < 4:
            ag[r, 1, k] = push(k, ZM, 1 if k > 2 else None, ring(r, 1, 4 + k))
        push(k, C, None if k < 4 else 1)

    class Reduce:
        def __init__(self, i):
            self.i, self.a, self.b = i, slice(0, RA[i]), slice(RA[i], ROWS)
            self.ra, self.rb = pl.ds(0, RA[i]), pl.ds(0, ROWS - RA[i])
            self.r = lax.rem(i + 2 * (1 - s), R)

        def both(self, src, dst):
            def one(h):
                return copy(lambda: src().at[h], lambda: dst().at[h], (YP, YM)[h])

            return [one(0), one(1)]

        def q(self, j, rows):
            return QV[self.r, j, :, rows]

        def r0(self):
            i, ra, rb = self.i, self.ra, self.rb
            for h in range(2):
                for x in range(2):
                    A2S[i, h, x, ra] = QV[self.r, jj(x, y2), h, self.a].astype(BF)
            self.a2 = self.both(lambda: A2S.at[i, :, :, ra], lambda: A2R.at[i, :, :, ra])
            for k in range(4):
                XBS[i, k, :, rb] = self.q(jj(xo, k), self.b).astype(BF)
            self.xb = copy(lambda: XBS.at[i, :, :, rb], lambda: XBR.at[i, :, :, rb], X)

        def r1(self):
            i, ra = self.i, self.ra
            for h in range(2):
                self.a2[h].wait_recv()
                for x in range(2):
                    v = self.q(jj(x, (yp, ym)[h]), self.a)
                    A1S[i, h, x, h, ra] = (v[h] + A2R[i, h, x, ra].astype(F32)).astype(BF)
                    A1S[i, h, x, 1 - h, ra] = v[1 - h].astype(BF)
            self.a1 = self.both(lambda: A1S.at[i, :, :, :, ra], lambda: A1R.at[i, :, :, :, ra])

        def r2(self):
            i, rb = self.i, self.rb
            self.xb.wait_recv()
            v = self.q(jj(xl, y2), self.b) + XBR[i, y2, :, rb].astype(F32)
            B2S[i, :, rb] = v.astype(BF)
            self.b2 = self.both(lambda: B2S.at[i, :, rb], lambda: B2R.at[i, :, rb])

        def r3(self):
            i, rb = self.i, self.rb
            for h in range(2):
                self.b2[h].wait_recv()
                yy = (yp, ym)[h]
                v = self.q(jj(xl, yy), self.b) + XBR[i, yy, :, rb].astype(F32)
                B1S[i, h, h, rb] = (v[h] + B2R[i, h, rb].astype(F32)).astype(BF)
                B1S[i, h, 1 - h, rb] = v[1 - h].astype(BF)
            self.b1 = self.both(lambda: B1S.at[i, :, :, rb], lambda: B1R.at[i, :, :, rb])

        def r4(self):
            i, ra = self.i, self.ra
            for h in range(2):
                self.a1[h].wait_recv()
            v = self.q(jj(xo, y), self.a) + A1R[i, 0, xo, :, ra].astype(F32) + A1R[i, 1, xo, :, ra].astype(F32)
            AXS[i, :, ra] = v.astype(BF)
            self.ax = copy(lambda: AXS.at[i, :, ra], lambda: AXR.at[i, :, ra], X)

        def r5(self):
            i, ra, rb = self.i, self.ra, self.rb
            va = self.q(own, self.a) + A1R[i, 0, xl, :, ra].astype(F32) + A1R[i, 1, xl, :, ra].astype(F32)
            vb = self.q(own, self.b) + XBR[i, y, :, rb].astype(F32)
            for d in self.b1:
                d.wait_recv()
            vb = vb + B1R[i, 0, :, rb].astype(F32) + B1R[i, 1, :, rb].astype(F32)
            self.ax.wait_recv()
            FO[i, :, self.a] = va + AXR[i, :, ra].astype(F32)
            FO[i, :, self.b] = vb
            FS[i] = FO[i, oc].astype(BF)
            self.f = copy(lambda: FS.at[i], lambda: FR.at[i], C)

        def r6(self):
            i = self.i
            self.f.wait_recv()
            if i < R // 2:
                HS[i, c] = FO[i, c].astype(BF)
                HS[i, oc] = FR[i]
                self.h = copy(lambda: HS.at[i], lambda: HR.at[i], S)
                return
            FO[i, oc] = FR[i].astype(F32)
            rows = slice(ROWS * (i - R // 2), ROWS * (i - R // 2 + 1))

            def keep(o):
                for h in range(2):
                    o[rows, BLK * h:BLK * (h + 1)] = FO[i, h]

            pl.when(student)(lambda: keep(ug_ref))
            pl.when(s == 0)(lambda: keep(dg_ref))

        def r7(self):
            i = self.i
            self.h.wait_recv()
            rows = slice(ROWS * i, ROWS * (i + 1))

            def keep(o):
                for h in range(2):
                    o[rows, BLK * h:BLK * (h + 1)] = HR[i, h].astype(F32)

            pl.when(student)(lambda: keep(dg_ref))
            pl.when(s == 0)(lambda: keep(ug_ref))

    red = [Reduce(i) for i in range(R)]

    def down_grads(r):
        g = [GT[r, 0], GT[r, 1]]
        q = nn(g[0], ACTG[0]) + nn(g[1], ACTG[1])
        QV[r] = q.reshape(NZ, 2, ROWS, BLK)

    def grad_act(r):
        w = D[r].reshape(NZ * 2 * ROWS, BLK)
        for img in range(2):
            v = tn(GT[r, img], w)
            if r == 0:
                GA[img] = v
            else:
                GA[img] += v

    def arrived(r):
        wait_bytes(fw[r], GT.at[r, 0])

    def transposed(part):
        def one(i, carry):
            img, j = lax.div(i, 8), lax.rem(i, 8)
            t = jnp.transpose(N[img, j].astype(F32)).astype(BF)
            for r in range(R):
                for h in range(2):
                    NTR[r, img, pl.ds(pl.multiple_of(j * 2 * ROWS + h * ROWS, 16), ROWS)] = t[rows_of(r, h)]
            return carry

        lax.fori_loop(4 * part, 4 * part + 4, one, 0)

    def up_grads(r):
        if r == 0:
            for img in range(2):
                GP[img] = (GA[img] * SL[img]).astype(BF)
        q = nn(NTR[r, 0], GP[0]) + nn(NTR[r, 1], GP[1])
        QV[r] = q.reshape(NZ, 2, ROWS, BLK)

    def stage(n, k):
        if k < 4:
            zstage(n, k)
        elif k == 4:
            output(n)
        elif k < 10:
            astage(n, k - 5)
        else:
            arrived(n)
            pl.when(student)(lambda: grad_act(n))

            @pl.when(s == 0)
            def _():
                if n == 0:
                    for d in act_out:
                        d.wait_recv()
                down_grads(n)

    def diagonal(d):
        for n in reversed(range(R)):
            k = d - n
            if 0 <= k < 11:
                stage(n, k)

    hidden(oc)
    send_act(lambda: oc)
    gd[0].g5()
    mixed(0)
    gd[3].g1()
    gd[3].g2()
    gd[1].g4()
    gd[2].g3()
    zstage(0, 0)
    gd[1].g5()
    mixed(1)
    gd[2].g4()
    gd[3].g3()
    zstage(0, 1)
    zstage(1, 0)
    gd[2].g5()
    mixed(2)
    gd[3].g4()
    gate_of_student()
    gd[3].g5()
    mixed(3)
    diagonal(2)
    for d in range(3, R + 4):
        diagonal(d)
    out_ref[...] = jnp.transpose(TOKT[...]).astype(BF)
    for d in range(R + 4, 11 + R - 1):
        diagonal(d)
        if d < R + 8:
            pl.when(student)(lambda: transposed(d - R - 4))

    def begin(n):
        pl.when(student)(lambda: up_grads(n))
        red[n].r0()

    def rstage(n, k):
        if k == 0:
            begin(n)
        elif k == 1:
            red[n].r1()
            red[n].r2()
        elif k == 2:
            red[n].r3()
            red[n].r4()
        elif k == 3:
            red[n].r5()
        else:
            red[n].r6()

    begin(0)
    begin(1)
    for d in range(2, R + 5):
        for n in reversed(range(R)):
            k = d - n if d - n < 1 else d - n - 1
            if d - n == 0 and n > 1 or 1 <= k < 5 and d - n > 1:
                rstage(n, k)
    for n in range(R // 2):
        red[n].r7()

    for d in started[None][-N_SEND[None]:]:
        d.wait_send()

    @pl.when(student)
    def _():
        for d in started[1][-N_SEND[1]:]:
            d.wait_send()


def shards(axes, tokens, up_weight, down_weight, mod_table, timesteps, valid_counts):
    mod = lax.dynamic_index_in_dim(mod_table[0], timesteps[0], 0, keepdims=False)
    downt = down_weight[0].T.reshape(R, ROWS, 2 * BLK)

    v = pltpu.VMEM
    nred = R
    scratch = [
        v((NZ, SEQ, BLK), BF),
        v((NZ, 2, 192, BLK), BF),
        v((R, NZ, 2, ROWS, BLK), BF),
        v((2, NZ, SEQ, BLK), BF),
        v((R, 2, NZ * 2 * ROWS, SEQ), BF),
        v((SEQ, BLK), F32),
        v((2, SEQ, BLK), F32),
        v((2, SEQ, BLK), BF),
        v((2, SEQ, BLK), BF),
        v((R, NZ * 2 * ROWS, SEQ), F32),
        v((R, NZ * 2 * ROWS, SEQ), BF),
        v((R, NZ * 2 * ROWS, SEQ), BF),
        v((R, 2, 4, 2 * ROWS, SEQ), BF),
        v((R, 2, 4, 2 * ROWS, SEQ), BF),
        v((3, NZ * BLK), F32),
        v((BLK, SEQ), F32),
        v((BLK, SEQ), F32),
        v((BLK, SEQ), F32),
        v((R, 2, ROWS, SEQ), BF),
        v((R, 2, ROWS, SEQ), BF),
        v((R, 2, NZ * 2 * ROWS, SEQ), BF),
        v((2, SEQ, BLK), F32),
        v((2, SEQ, BLK), BF),
        v((nred, NZ, 2, ROWS, BLK), F32),
        v((nred, 4, 2, 32, BLK), BF),
        v((nred, 4, 2, 32, BLK), BF),
        v((nred, 2, 2, 32, BLK), BF),
        v((nred, 2, 2, 32, BLK), BF),
        v((nred, 2, 2, 2, 32, BLK), BF),
        v((nred, 2, 2, 2, 32, BLK), BF),
        v((nred, 2, 32, BLK), BF),
        v((nred, 2, 32, BLK), BF),
        v((nred, 2, 2, 32, BLK), BF),
        v((nred, 2, 2, 32, BLK), BF),
        v((nred, 2, 32, BLK), BF),
        v((nred, 2, 32, BLK), BF),
        v((nred, ROWS, BLK), BF),
        v((nred, 2, ROWS, BLK), F32),
        v((nred, ROWS, BLK), BF),
        v((nred, 2, ROWS, BLK), BF),
        v((nred, 2, ROWS, BLK), BF),
        pltpu.SemaphoreType.DMA((sum(N_SEND.values()),)),
        pltpu.SemaphoreType.DMA((N_RECV,)),
        pltpu.SemaphoreType.DMA((3,)),
    ]
    hbm = pl.BlockSpec(memory_space=pl.ANY)
    vm = pl.BlockSpec(memory_space=pltpu.VMEM)
    out, up, down = pl.pallas_call(
        functools.partial(kernel, axes),
        out_shape=(
            jax.ShapeDtypeStruct((SEQ, BLK), BF),
            jax.ShapeDtypeStruct((96, 2 * BLK), F32),
            jax.ShapeDtypeStruct((96, 2 * BLK), F32),
        ),
        in_specs=[hbm, hbm, hbm, vm, pl.BlockSpec(memory_space=pltpu.SMEM)],
        out_specs=(vm, vm, vm),
        scratch_shapes=scratch,
        compiler_params=pltpu.CompilerParams(
            collective_id=0, has_side_effects=True, vmem_limit_bytes=67043328
        ),
    )(tokens, up_weight[0], downt, mod, valid_counts)
    def settle(out_in, up_in, down_in, out_to, up_to, down_to):
        out_to[...] = out_in[...]
        up_to[...] = up_in[...]
        down_to[...] = down_in[...]

    out, up, down = pl.pallas_call(
        settle,
        out_shape=(
            jax.ShapeDtypeStruct((SEQ, BLK), BF),
            jax.ShapeDtypeStruct((96, 2 * BLK), F32),
            jax.ShapeDtypeStruct((96, 2 * BLK), F32),
        ),
        in_specs=[vm] * 3,
        out_specs=(vm,) * 3,
    )(out, up, down)
    return out[None], up, down.T


def solution(mesh):
    placed = (
        P("dp", "mp"),
        P("side", "dp", "mp"),
        P("side", "mp", "dp"),
        P("side", None, None, None),
        P("dp"),
        P(),
    )
    return jax.shard_map(
        functools.partial(shards, mesh.axis_names),
        mesh=mesh,
        in_specs=placed,
        out_specs=(P("side", "dp", "mp"), P(("dp", "side"), "mp"), P("mp", ("dp", "side"))),
        check_vma=False,
    )
```

```python
import functools

import jax
import jax.numpy as jnp
from jax import lax
from jax.experimental import pallas as pl
from jax.experimental.pallas import tpu as pltpu
from jax.sharding import PartitionSpec as P

BF = jnp.bfloat16
F32 = jnp.float32
R = 4
ROWS = 192 // R
RA = (32, 32, 32, 16)
RU = 112
NZ = 8
SEQ = 256
BLK = 384
N_RECV = 145
N_SEND = {None: 40, 1: 2}


def gelu_pair(v):
    k = 0.7978845608028654
    v2 = v * v
    t = jnp.tanh(k * v * (1.0 + 0.044715 * v2))
    half = 0.5 * (1.0 + t)
    act = v * half
    slope = half + 0.5 * v * (1.0 - t * t) * (k * (1.0 + 3.0 * 0.044715 * v2))
    return act, slope


def nn(a, b):
    return lax.dot_general(a, b, (((1,), (0,)), ((), ())), preferred_element_type=F32)


def nt(a, b):
    return lax.dot_general(a, b, (((1,), (1,)), ((), ())), preferred_element_type=F32)


def tn(a, b):
    return lax.dot_general(a, b, (((0,), (0,)), ((), ())), preferred_element_type=F32)


def kernel(
    axes,
    tok_ref, up_ref, downt_ref, mod_ref, counts_ref,
    out_ref, ug_ref, dg_ref,
    T, U, D, N, NTR, HP, SL, ACT, ACTG, PO, PS, PR, ZS, ZR, MODO, GATE, GATEG, TOKT, OTA, OTB, GT, GA, GP,
    QV, XBS, XBR, A2S, A2R, A1S, A1R, B2S, B2R, B1S, B1R, AXS, AXR, FS, FO, FR, HS, HR,
    send, recv, local,
):
    dp, z, s = lax.axis_index("dp"), lax.axis_index("mp"), lax.axis_index("side")
    c = lax.rem(dp, 2)
    y = lax.rem(lax.div(dp, 2), 4)
    xl = lax.div(dp, 8)
    xo = 1 - xl
    yp, ym, y2 = lax.rem(y + 1, 4), lax.rem(y + 3, 4), lax.rem(y + 2, 4)
    oc = 1 - c

    def zz(k):
        return lax.rem(z + (k + NZ), NZ)

    def where(dp_=None, mp_=None, side_=None):
        at = {"dp": dp if dp_ is None else dp_, "mp": z if mp_ is None else mp_, "side": s if side_ is None else side_}
        return tuple(at[a] for a in axes)

    def jj(a, b):
        return a * 4 + b

    X = where(dp_=xo * 8 + y * 2 + c)
    YP = where(dp_=xl * 8 + yp * 2 + c)
    YM = where(dp_=xl * 8 + ym * 2 + c)
    ZP = where(mp_=zz(1))
    ZM = where(mp_=zz(-1))
    C = where(dp_=dp + 1 - 2 * c)
    S = where(side_=1 - s)

    barrier = pltpu.get_barrier_semaphore()
    peers = (X, YP, YM, ZP, ZM, C, S)
    for peer in peers:
        pl.semaphore_signal(barrier, inc=1, device_id=peer, device_id_type=pl.DeviceIdType.MESH)
    pl.semaphore_wait(barrier, len(peers))

    used = [0]
    started = {None: [], 1: []}

    class Copy:
        def __init__(self, refs, dev, side, at=None):
            self.refs, self.dev = refs, dev
            if at is None:
                at = used[0]
                used[0] += 1
            self.i = at
            mine = started[side]
            pool = N_SEND[side]
            self.j = len(mine) % pool + {None: 0, 1: N_SEND[None]}[side]
            if len(mine) >= pool:
                mine[-pool].wait_send()
            self.made().start()
            mine.append(self)

        def made(self):
            src, dst = self.refs()
            return pltpu.make_async_remote_copy(
                src_ref=src, dst_ref=dst, send_sem=send.at[self.j], recv_sem=recv.at[self.i],
                device_id=self.dev, device_id_type=pl.DeviceIdType.MESH,
            )

        def wait_recv(self):
            self.made().wait_recv()

        def wait_send(self):
            self.made().wait_send()

    def copy(src, dst, dev, side=None, at=None):
        return Copy(lambda: (src(), dst()), dev, side, at)

    def copy_same(ref, dev, side=None, at=None):
        return Copy(lambda: (ref(),) * 2, dev, side, at)

    def wait_bytes(i, ref):
        pltpu.make_async_copy(ref, ref, recv.at[i]).wait()

    student = s == 1

    class Gather:
        def __init__(self, buf, ra, four):
            self.buf, self.ra, self.four = buf, ra, four

        def g0(self):
            self.bx = used[0]
            used[0] += 1
            self.xa = copy_same(lambda: self.apart(xl, y), X)
            self.yp = copy_same(lambda: self.buf(own), YP)
            self.ym = copy_same(lambda: self.buf(own), YM)
            self.xb = copy_same(lambda: self.bpart(xl, y), X, at=self.bx)

        def g1(self):
            self.xa.wait_recv()
            self.xap = copy_same(lambda: self.apart(xo, y), YP)
            self.xam = copy_same(lambda: self.apart(xo, y), YM)

        def apart(self, xx, yy):
            return self.buf(jj(xx, yy)).at[:, pl.ds(0, self.ra)]

        def bpart(self, xx, yy):
            b = self.buf(jj(xx, yy))
            return b.at[:, pl.ds(self.ra, b.shape[1] - self.ra)]

        def g2(self):
            self.yp.wait_recv()
            self.rp = copy_same(lambda: self.buf(jj(xl, ym)).at[0], YP)
            self.bxm = copy_same(lambda: self.bpart(xl, ym), X, at=self.bx)
            self.ym.wait_recv()
            self.rm = copy_same(lambda: self.buf(jj(xl, yp)).at[1], YM)
            self.bxp = copy_same(lambda: self.bpart(xl, yp), X, at=self.bx)

        def g3(self):
            self.xap.wait_recv()
            self.rxp = copy_same(lambda: self.buf(jj(xo, ym)).at[0, pl.ds(0, self.ra)], YP)
            self.xam.wait_recv()
            self.rxm = copy_same(lambda: self.buf(jj(xo, yp)).at[1, pl.ds(0, self.ra)], YM)

        def g4(self):
            self.rp.wait_recv()
            self.rm.wait_recv()
            self.bx2 = copy_same(lambda: self.bpart(xl, y2), X, at=self.bx)

        def g5(self):
            self.rxp.wait_recv()
            self.rxm.wait_recv()
            wait_bytes(self.bx, self.four())

    own = jj(xl, y)
    u_out = copy(lambda: up_ref.at[:, pl.ds(pl.multiple_of(oc * BLK, 128), BLK)], lambda: U.at[own, c], C)
    d_out = copy(lambda: downt_ref.at[:, :, pl.ds(pl.multiple_of(oc * BLK, 128), BLK)], lambda: D.at[:, own, c], C)
    tok_in = pltpu.make_async_copy(tok_ref, T.at[z], local.at[0])
    tok_in.start()
    u_in = pltpu.make_async_copy(up_ref.at[:, pl.ds(pl.multiple_of(c * BLK, 128), BLK)], U.at[own, c], local.at[1])
    u_in.start()
    d_in = pltpu.make_async_copy(
        downt_ref.at[:, :, pl.ds(pl.multiple_of(c * BLK, 128), BLK)], D.at[:, own, c], local.at[2]
    )
    d_in.start()

    tk = {}

    def tok_send(hop):
        for p in range(2):
            rows = pl.ds(128 * p, 128)
            if hop:
                if ("+", hop - 1, p) in tk:
                    tk["+", hop - 1, p].wait_recv()
            at = functools.partial(lambda k, rows: tok_ref.at[rows] if k is None else T.at[zz(k), rows], rows=rows)
            src = functools.partial(at, None if hop == 0 else -hop)
            if hop < 3 or p == 0:
                tk["+", hop, p] = copy(src, functools.partial(at, -hop), ZP)
            if hop:
                if ("-", hop - 1, p) in tk:
                    tk["-", hop - 1, p].wait_recv()
            src = functools.partial(at, None if hop == 0 else hop)
            if hop < 3 or p == 1:
                tk["-", hop, p] = copy(src, functools.partial(at, hop), ZM)

    gu = Gather(lambda j: U.at[j], RU, lambda: U.at[0:4, :, RU:192])
    gd = [
        Gather(
            functools.partial(lambda r, j: D.at[r, j], r), RA[r],
            functools.partial(lambda r: D.at[r, 0:4, :, RA[r]:ROWS], r),
        )
        for r in range(R)
    ]

    tok_send(0)
    mod_out = copy(lambda: mod_ref, lambda: MODO, S)
    u_in.wait()
    u_out.wait_recv()
    gu.g0()
    tok_in.wait()
    gate = mod_ref[2:3, pl.ds(pl.multiple_of(z * BLK, 128), BLK)]
    gate = jnp.transpose(jnp.broadcast_to(gate, (128, BLK)))
    GATE[:, 0:128] = gate
    GATE[:, 128:256] = gate

    def gate_of_student():
        mod_out.wait_recv()
        at = pl.ds(pl.multiple_of(z * BLK, 128), BLK)
        g = jnp.where(jnp.full((1, BLK), s) == 1, mod_ref[2:3, at], MODO[2:3, at])
        g = jnp.transpose(jnp.broadcast_to(g, (128, BLK)))
        GATEG[:, 0:128] = g
        GATEG[:, 128:256] = g

    tt = jnp.transpose(T[z].astype(F32))
    TOKT[...] = tt
    tok_send(1)
    gu.g1()
    tok_send(2)
    gu.g2()
    d_in.wait()
    d_out.wait_recv()
    gu.g3()
    gd[0].g0()
    gd[1].g0()
    tok_send(3)
    gu.g4()
    gd[2].g0()
    gd[3].g0()
    tk["+", 3, 0].wait_recv()
    tk["-", 3, 1].wait_recv()

    def norm_rows(i, carry):
        rows = pl.ds(pl.multiple_of(i * 16, 16), 16)
        x = [T[b, rows].astype(F32) for b in range(NZ)]
        total = x[0]
        for b in range(1, NZ):
            total = total + x[b]
        mean = jnp.sum(total, axis=-1, keepdims=True) * (1.0 / (NZ * BLK))
        x = [v - mean for v in x]
        sq = x[0] * x[0]
        for b in range(1, NZ):
            sq = sq + x[b] * x[b]
        var = jnp.sum(sq, axis=-1, keepdims=True) * (1.0 / (NZ * BLK))
        rs = lax.rsqrt(var + 1e-06)
        for b in range(NZ):
            cols = slice(b * BLK, (b + 1) * BLK)
            n = x[b] * rs * (1.0 + mod_ref[1:2, cols]) + mod_ref[0:1, cols]
            N[c, b, rows] = n.astype(BF)
        return carry

    n_out = []

    def norm_half(p):
        lax.fori_loop(8 * p, 8 * p + 8, norm_rows, 0)
        n_out.append(copy_same(lambda: N.at[c, :, pl.ds(128 * p, 128)], C))

    def hidden(img):
        h = nn(N[img, 0], U[0].reshape(BLK, BLK))
        for b in range(1, NZ):
            h = h + nn(N[img, b], U[b].reshape(BLK, BLK))
        HP[...] = h

        def act_rows(i, carry):
            rows = pl.ds(pl.multiple_of(i * 32, 32), 32)
            a, g = gelu_pair(HP[rows])
            ACT[img, rows] = a.astype(BF)
            SL[img, rows] = g
            return carry

        lax.fori_loop(0, SEQ // 32, act_rows, 0)

    act_out = []

    def send_act(img):
        @pl.when(student)
        def _():
            act_out.append(copy(lambda: ACT.at[img()], lambda: ACTG.at[img()], S, 1))

    norm_half(0)
    gd[0].g1()
    gd[0].g2()
    gd[1].g1()
    gd[1].g2()
    norm_half(1)
    gu.g5()
    gd[2].g1()
    gd[2].g2()
    gd[0].g3()
    hidden(c)
    gd[3].g1()
    gd[3].g2()
    gd[0].g4()
    gd[1].g3()
    gd[1].g4()
    for d in n_out:
        d.wait_recv()

    m_out, zs = {}, {}
    z_sems = used[0]
    used[0] += 4 * R

    def ring(r, q, k):
        return z_sems + 4 * r + 2 * q + k % 2


    def mixed(r):
        w = D[r].reshape(NZ * 2 * ROWS, BLK)
        PS[r] = nt(w, ACT[oc]).astype(BF)
        m_out[r] = copy(lambda: PS.at[r], lambda: PR.at[r], C)
        PO[r] = nt(w, ACT[c])

    def val(r, b):
        rows = pl.ds(pl.multiple_of(b * 2 * ROWS, 32), 2 * ROWS)
        return PO[r, rows] + PR[r, rows].astype(F32)

    def zstage(r, k):
        h0, h1 = pl.ds(0, ROWS), pl.ds(ROWS, ROWS)
        if k == 0:
            m_out[r].wait_recv()
            v = val(r, zz(4)).astype(BF)
            ZS[r, 0, 0] = v
            zs[r, 0, 0] = copy(lambda: ZS.at[r, 0, 0, h0], lambda: ZR.at[r, 0, 0, h0], ZP, None, ring(r, 0, 0))
            zs[r, 1, 0] = copy(lambda: ZS.at[r, 0, 0, h1], lambda: ZR.at[r, 1, 0, h1], ZM, None, ring(r, 1, 0))
            return
        for q in range(2):
            zs[r, q, k - 1].wait_recv()
        for q in range(2):
            v = val(r, zz((4 - k) if q == 0 else (k - 4)))
            if k == 1:
                h = slice(0, ROWS) if q == 0 else slice(ROWS, 2 * ROWS)
                g = slice(ROWS, 2 * ROWS) if q == 0 else slice(0, ROWS)
                ZS[r, q, k, h] = (v[h] + ZR[r, q, 0, h].astype(F32)).astype(BF)
                ZS[r, q, k, g] = v[g].astype(BF)
            else:
                ZS[r, q, k] = (v + ZR[r, q, k - 1].astype(F32)).astype(BF)
            at = functools.partial(lambda ref, q: ref.at[r, q, k], q=q)
            to = ZP if q == 0 else ZM
            zs[r, q, k] = copy(functools.partial(at, ZS), functools.partial(at, ZR), to, None, ring(r, q, k))

    sw = {}

    def rows_of(r, h):
        return slice(192 * h + ROWS * r, 192 * h + ROWS * (r + 1))

    def output(r):
        zs[r, 0, 3].wait_recv()
        zs[r, 1, 3].wait_recv()
        m = val(r, z) + ZR[r, 0, 3].astype(F32) + ZR[r, 1, 3].astype(F32)
        for h in range(2):
            w = rows_of(r, h)
            o = (TOKT[w] + GATE[w] * m[ROWS * h:ROWS * (h + 1)]).astype(BF)
            OTA[r, h] = o
            TOKT[w] = o.astype(F32)

        sw[r] = copy(lambda: OTA.at[r], lambda: OTB.at[r], S)

    ag, fw = {}, {}
    for r in range(R):
        fw[r] = used[0]
        used[0] += 1

    def gslice(r, img, b, h):
        n = ROWS if h is not None else 2 * ROWS
        return GT.at[r, img, pl.ds(pl.multiple_of(b * 2 * ROWS + (h or 0) * ROWS, 16), n)]

    def astage(r, k):
        def push(kk, dev, h=None, at=None):
            return copy_same(lambda: gslice(r, c, zz(kk), h), dev, None, fw[r] if at is None else at)

        if k == 0:
            sw[r].wait_recv()
            total = counts_ref[0]
            for i in range(1, 16):
                total = total + counts_ref[i]
            norm = jnp.sqrt(jnp.full((1, SEQ), total, jnp.int32).astype(F32))
            at = lax.broadcasted_iota(jnp.int32, (1, SEQ), 1)
            vrow = jnp.where(at < counts_ref[dp], (2 * s - 1).astype(F32), 0.0) / norm
            for h in range(2):
                w = rows_of(r, h)
                diff = OTA[r, h].astype(F32) - OTB[r, h].astype(F32)
                rows = pl.ds(pl.multiple_of(z * 2 * ROWS + h * ROWS, 16), ROWS)
                GT[r, c, rows] = (GATEG[w] * diff * vrow).astype(BF)
            ag[r, 0, 0] = push(0, ZP, at=ring(r, 0, 4))
            ag[r, 1, 0] = push(0, ZM, at=ring(r, 1, 4))
            push(0, C)
            return
        ag[r, 0, k - 1].wait_recv()
        ag[r, 1, k - 1].wait_recv()
        if k < 4:
            ag[r, 0, k] = push(-k, ZP, 0 if k > 2 else None, ring(r, 0, 4 + k))
        push(-k, C, None if k < 4 else 0)
        if k < 4:
            ag[r, 1, k] = push(k, ZM, 1 if k > 2 else None, ring(r, 1, 4 + k))
        push(k, C, None if k < 4 else 1)

    class Reduce:
        def __init__(self, i):
            self.i, self.a, self.b = i, slice(0, RA[i]), slice(RA[i], ROWS)
            self.ra, self.rb = pl.ds(0, RA[i]), pl.ds(0, ROWS - RA[i])
            self.r = lax.rem(i + 2 * (1 - s), R)

        def both(self, src, dst):
            def one(h):
                return copy(lambda: src().at[h], lambda: dst().at[h], (YP, YM)[h])

            return [one(0), one(1)]

        def q(self, j, rows):
            return QV[self.r, j, :, rows]

        def r0(self):
            i, ra, rb = self.i, self.ra, self.rb
            for h in range(2):
                for x in range(2):
                    A2S[i, h, x, ra] = QV[self.r, jj(x, y2), h, self.a].astype(BF)
            self.a2 = self.both(lambda: A2S.at[i, :, :, ra], lambda: A2R.at[i, :, :, ra])
            for k in range(4):
                XBS[i, k, :, rb] = self.q(jj(xo, k), self.b).astype(BF)
            self.xb = copy(lambda: XBS.at[i, :, :, rb], lambda: XBR.at[i, :, :, rb], X)

        def r1(self):
            i, ra = self.i, self.ra
            for h in range(2):
                self.a2[h].wait_recv()
                for x in range(2):
                    v = self.q(jj(x, (yp, ym)[h]), self.a)
                    A1S[i, h, x, h, ra] = (v[h] + A2R[i, h, x, ra].astype(F32)).astype(BF)
                    A1S[i, h, x, 1 - h, ra] = v[1 - h].astype(BF)
            self.a1 = self.both(lambda: A1S.at[i, :, :, :, ra], lambda: A1R.at[i, :, :, :, ra])

        def r2(self):
            i, rb = self.i, self.rb
            self.xb.wait_recv()
            v = self.q(jj(xl, y2), self.b) + XBR[i, y2, :, rb].astype(F32)
            B2S[i, :, rb] = v.astype(BF)
            self.b2 = self.both(lambda: B2S.at[i, :, rb], lambda: B2R.at[i, :, rb])

        def r3(self):
            i, rb = self.i, self.rb
            for h in range(2):
                self.b2[h].wait_recv()
                yy = (yp, ym)[h]
                v = self.q(jj(xl, yy), self.b) + XBR[i, yy, :, rb].astype(F32)
                B1S[i, h, h, rb] = (v[h] + B2R[i, h, rb].astype(F32)).astype(BF)
                B1S[i, h, 1 - h, rb] = v[1 - h].astype(BF)
            self.b1 = self.both(lambda: B1S.at[i, :, :, rb], lambda: B1R.at[i, :, :, rb])

        def r4(self):
            i, ra = self.i, self.ra
            for h in range(2):
                self.a1[h].wait_recv()
            v = self.q(jj(xo, y), self.a) + A1R[i, 0, xo, :, ra].astype(F32) + A1R[i, 1, xo, :, ra].astype(F32)
            AXS[i, :, ra] = v.astype(BF)
            self.ax = copy(lambda: AXS.at[i, :, ra], lambda: AXR.at[i, :, ra], X)

        def r5(self):
            i, ra, rb = self.i, self.ra, self.rb
            va = self.q(own, self.a) + A1R[i, 0, xl, :, ra].astype(F32) + A1R[i, 1, xl, :, ra].astype(F32)
            vb = self.q(own, self.b) + XBR[i, y, :, rb].astype(F32)
            for d in self.b1:
                d.wait_recv()
            vb = vb + B1R[i, 0, :, rb].astype(F32) + B1R[i, 1, :, rb].astype(F32)
            self.ax.wait_recv()
            FO[i, :, self.a] = va + AXR[i, :, ra].astype(F32)
            FO[i, :, self.b] = vb
            FS[i] = FO[i, oc].astype(BF)
            self.f = copy(lambda: FS.at[i], lambda: FR.at[i], C)

        def r6(self):
            i = self.i
            self.f.wait_recv()
            if i < R // 2:
                HS[i, c] = FO[i, c].astype(BF)
                HS[i, oc] = FR[i]
                self.h = copy(lambda: HS.at[i], lambda: HR.at[i], S)
                return
            FO[i, oc] = FR[i].astype(F32)
            rows = slice(ROWS * (i - R // 2), ROWS * (i - R // 2 + 1))

            def keep(o):
                for h in range(2):
                    o[rows, BLK * h:BLK * (h + 1)] = FO[i, h]

            pl.when(student)(lambda: keep(ug_ref))
            pl.when(s == 0)(lambda: keep(dg_ref))

        def r7(self):
            i = self.i
            self.h.wait_recv()
            rows = slice(ROWS * i, ROWS * (i + 1))

            def keep(o):
                for h in range(2):
                    o[rows, BLK * h:BLK * (h + 1)] = HR[i, h].astype(F32)

            pl.when(student)(lambda: keep(dg_ref))
            pl.when(s == 0)(lambda: keep(ug_ref))

    red = [Reduce(i) for i in range(R)]

    def down_grads(r):
        g = [GT[r, 0], GT[r, 1]]
        q = nn(g[0], ACTG[0]) + nn(g[1], ACTG[1])
        QV[r] = q.reshape(NZ, 2, ROWS, BLK)

    def grad_act(r):
        w = D[r].reshape(NZ * 2 * ROWS, BLK)
        for img in range(2):
            v = tn(GT[r, img], w)
            if r == 0:
                GA[img] = v
            else:
                GA[img] += v

    def arrived(r):
        wait_bytes(fw[r], GT.at[r, 0])

    def transposed(part):
        def one(i, carry):
            img, j = lax.div(i, 8), lax.rem(i, 8)
            t = jnp.transpose(N[img, j].astype(F32)).astype(BF)
            for r in range(R):
                for h in range(2):
                    NTR[r, img, pl.ds(pl.multiple_of(j * 2 * ROWS + h * ROWS, 16), ROWS)] = t[rows_of(r, h)]
            return carry

        lax.fori_loop(4 * part, 4 * part + 4, one, 0)

    def up_grads(r):
        if r == 0:
            for img in range(2):
                GP[img] = (GA[img] * SL[img]).astype(BF)
        q = nn(NTR[r, 0], GP[0]) + nn(NTR[r, 1], GP[1])
        QV[r] = q.reshape(NZ, 2, ROWS, BLK)

    def stage(n, k):
        if k < 4:
            zstage(n, k)
        elif k == 4:
            output(n)
        elif k < 10:
            astage(n, k - 5)
        else:
            arrived(n)
            pl.when(student)(lambda: grad_act(n))

            @pl.when(s == 0)
            def _():
                if n == 0:
                    for d in act_out:
                        d.wait_recv()
                down_grads(n)

    def diagonal(d):
        for n in reversed(range(R)):
            k = d - n
            if 0 <= k < 11:
                stage(n, k)

    hidden(oc)
    gd[2].g3()
    gd[2].g4()
    gd[0].g5()
    mixed(0)
    gd[3].g3()
    gd[3].g4()
    gd[1].g5()
    mixed(1)
    zstage(0, 0)
    gd[2].g5()
    mixed(2)
    zstage(1, 0)
    zstage(0, 1)
    gate_of_student()
    gd[3].g5()
    mixed(3)
    send_act(lambda: c)
    send_act(lambda: oc)
    diagonal(2)
    for d in range(3, R + 4):
        diagonal(d)
    out_ref[...] = jnp.transpose(TOKT[...]).astype(BF)
    for d in range(R + 4, 11 + R - 1):
        diagonal(d)
        if d < R + 8:
            pl.when(student)(lambda: transposed(d - R - 4))

    def begin(n):
        pl.when(student)(lambda: up_grads(n))
        red[n].r0()

    def rstage(n, k):
        if k == 0:
            begin(n)
        elif k == 1:
            red[n].r1()
            red[n].r2()
        elif k == 2:
            red[n].r3()
            red[n].r4()
        elif k == 3:
            red[n].r5()
        else:
            red[n].r6()

    begin(0)
    begin(1)
    for d in range(2, R + 5):
        for n in reversed(range(R)):
            k = d - n if d - n < 1 else d - n - 1
            if d - n == 0 and n > 1 or 1 <= k < 5 and d - n > 1:
                rstage(n, k)
    for n in range(R // 2):
        red[n].r7()

    for d in started[None][-N_SEND[None]:]:
        d.wait_send()

    @pl.when(student)
    def _():
        for d in started[1][-N_SEND[1]:]:
            d.wait_send()


def shards(axes, tokens, up_weight, down_weight, mod_table, timesteps, valid_counts):
    mod = lax.dynamic_index_in_dim(mod_table[0], timesteps[0], 0, keepdims=False)
    downt = down_weight[0].T.reshape(R, ROWS, 2 * BLK)

    v = pltpu.VMEM
    nred = R
    scratch = [
        v((NZ, SEQ, BLK), BF),
        v((NZ, 2, 192, BLK), BF),
        v((R, NZ, 2, ROWS, BLK), BF),
        v((2, NZ, SEQ, BLK), BF),
        v((R, 2, NZ * 2 * ROWS, SEQ), BF),
        v((SEQ, BLK), F32),
        v((2, SEQ, BLK), F32),
        v((2, SEQ, BLK), BF),
        v((2, SEQ, BLK), BF),
        v((R, NZ * 2 * ROWS, SEQ), F32),
        v((R, NZ * 2 * ROWS, SEQ), BF),
        v((R, NZ * 2 * ROWS, SEQ), BF),
        v((R, 2, 4, 2 * ROWS, SEQ), BF),
        v((R, 2, 4, 2 * ROWS, SEQ), BF),
        v((3, NZ * BLK), F32),
        v((BLK, SEQ), F32),
        v((BLK, SEQ), F32),
        v((BLK, SEQ), F32),
        v((R, 2, ROWS, SEQ), BF),
        v((R, 2, ROWS, SEQ), BF),
        v((R, 2, NZ * 2 * ROWS, SEQ), BF),
        v((2, SEQ, BLK), F32),
        v((2, SEQ, BLK), BF),
        v((nred, NZ, 2, ROWS, BLK), F32),
        v((nred, 4, 2, 32, BLK), BF),
        v((nred, 4, 2, 32, BLK), BF),
        v((nred, 2, 2, 32, BLK), BF),
        v((nred, 2, 2, 32, BLK), BF),
        v((nred, 2, 2, 2, 32, BLK), BF),
        v((nred, 2, 2, 2, 32, BLK), BF),
        v((nred, 2, 32, BLK), BF),
        v((nred, 2, 32, BLK), BF),
        v((nred, 2, 2, 32, BLK), BF),
        v((nred, 2, 2, 32, BLK), BF),
        v((nred, 2, 32, BLK), BF),
        v((nred, 2, 32, BLK), BF),
        v((nred, ROWS, BLK), BF),
        v((nred, 2, ROWS, BLK), F32),
        v((nred, ROWS, BLK), BF),
        v((nred, 2, ROWS, BLK), BF),
        v((nred, 2, ROWS, BLK), BF),
        pltpu.SemaphoreType.DMA((sum(N_SEND.values()),)),
        pltpu.SemaphoreType.DMA((N_RECV,)),
        pltpu.SemaphoreType.DMA((3,)),
    ]
    hbm = pl.BlockSpec(memory_space=pl.ANY)
    vm = pl.BlockSpec(memory_space=pltpu.VMEM)
    out, up, down = pl.pallas_call(
        functools.partial(kernel, axes),
        out_shape=(
            jax.ShapeDtypeStruct((SEQ, BLK), BF),
            jax.ShapeDtypeStruct((96, 2 * BLK), F32),
            jax.ShapeDtypeStruct((96, 2 * BLK), F32),
        ),
        in_specs=[hbm, hbm, hbm, vm, pl.BlockSpec(memory_space=pltpu.SMEM)],
        out_specs=(vm, vm, vm),
        scratch_shapes=scratch,
        compiler_params=pltpu.CompilerParams(
            collective_id=0, has_side_effects=True, vmem_limit_bytes=67043328
        ),
    )(tokens, up_weight[0], downt, mod, valid_counts)
    def settle(out_in, up_in, down_in, out_to, up_to, down_to):
        out_to[...] = out_in[...]
        up_to[...] = up_in[...]
        down_to[...] = down_in[...]

    out, up, down = pl.pallas_call(
        settle,
        out_shape=(
            jax.ShapeDtypeStruct((SEQ, BLK), BF),
            jax.ShapeDtypeStruct((96, 2 * BLK), F32),
            jax.ShapeDtypeStruct((96, 2 * BLK), F32),
        ),
        in_specs=[vm] * 3,
        out_specs=(vm,) * 3,
    )(out, up, down)
    return out[None], up, down.T


def solution(mesh):
    placed = (
        P("dp", "mp"),
        P("side", "dp", "mp"),
        P("side", "mp", "dp"),
        P("side", None, None, None),
        P("dp"),
        P(),
    )
    return jax.shard_map(
        functools.partial(shards, mesh.axis_names),
        mesh=mesh,
        in_specs=placed,
        out_specs=(P("side", "dp", "mp"), P(("dp", "side"), "mp"), P("mp", ("dp", "side"))),
        check_vma=False,
    )
```

```python
import functools

import jax
import jax.numpy as jnp
from jax import lax
from jax.experimental import pallas as pl
from jax.experimental.pallas import tpu as pltpu
from jax.sharding import PartitionSpec as P

BF = jnp.bfloat16
F32 = jnp.float32
R = 4
ROWS = 192 // R
RA = (32, 32, 32, 16)
RU = 112
ORDER = (
    ("g2", 3), ("g1", 3), ("hc", 0), ("ho", 0), ("g1", 0), ("g4", 3), ("g2", 0), ("g3", 3), ("g1", 1), ("g2", 1),
    ("g2", 2), ("g1", 2), ("g3", 0), ("g4", 0), ("g5", 3), ("m", 3), ("g3", 1), ("g4", 1), ("g4", 2), ("s0", 3),
    ("g3", 2), ("g5", 0), ("m", 0), ("g5", 1), ("m", 1), ("s1", 3), ("g5", 2), ("m", 2), ("s0", 0), ("s0", 1),
    ("s0", 2), ("s2", 3), ("s1", 0), ("s1", 1), ("s1", 2), ("s3", 3), ("s2", 0), ("s2", 1), ("s2", 2), ("s4", 3),
    ("s3", 0), ("s3", 1), ("s3", 2), ("s4", 0), ("s5", 3), ("s4", 1), ("s4", 2), ("s6", 3), ("s5", 0), ("s5", 1),
    ("s5", 2), ("s7", 3), ("s6", 0), ("s6", 1), ("s6", 2), ("s8", 3), ("s7", 0), ("s7", 1), ("s7", 2), ("s9", 3),
    ("s8", 0), ("s10", 3), ("s8", 1), ("s8", 2), ("s9", 0), ("s9", 1), ("s10", 0), ("s9", 2), ("s10", 1), ("s10", 2),
    ("b", 1), ("b", 0), ("b", 3), ("b", 2), ("r1", 1), ("r2", 1), ("r1", 0), ("r1", 3), ("r1", 2), ("r2", 0),
    ("r4", 1), ("r3", 1), ("r4", 0), ("r2", 3), ("r4", 3), ("r2", 2), ("r4", 2), ("r3", 0), ("r5", 1), ("r3", 3),
    ("r3", 2), ("r6", 1), ("r5", 0), ("r6", 0), ("r5", 3), ("r5", 2), ("r6", 3), ("r7", 1), ("r6", 2), ("r7", 0),
)
NZ = 8
SEQ = 256
BLK = 384
N_RECV = 161
N_SEND = {None: 40, 1: 2}


def gelu_pair(v):
    k = 0.7978845608028654
    v2 = v * v
    t = jnp.tanh(k * v * (1.0 + 0.044715 * v2))
    half = 0.5 * (1.0 + t)
    act = v * half
    slope = half + 0.5 * v * (1.0 - t * t) * (k * (1.0 + 3.0 * 0.044715 * v2))
    return act, slope


def nn(a, b):
    return lax.dot_general(a, b, (((1,), (0,)), ((), ())), preferred_element_type=F32)


def nt(a, b):
    return lax.dot_general(a, b, (((1,), (1,)), ((), ())), preferred_element_type=F32)


def tn(a, b):
    return lax.dot_general(a, b, (((0,), (0,)), ((), ())), preferred_element_type=F32)


def kernel(
    axes,
    tok_ref, up_ref, downt_ref, table_ref, step_ref, counts_ref,
    out_ref, ug_ref, dg_ref,
    T, ST, MEAN, RSTD, U, D, N, NTR, HP, SL, ACT, ACTG, PO, PS, PR, ZS, ZR, TAB, mod_ref, MODO, GATE, GATEG, TOKT, OTA, OTB, GT, GA, GP,
    QV, XBS, XBR, A2S, A2R, A1S, A1R, B2S, B2R, B1S, B1R, AXS, AXR, FS, FO, FR, HS, HR,
    send, recv, local,
):
    dp, z, s = lax.axis_index("dp"), lax.axis_index("mp"), lax.axis_index("side")
    c = lax.rem(dp, 2)
    y = lax.rem(lax.div(dp, 2), 4)
    xl = lax.div(dp, 8)
    xo = 1 - xl
    yp, ym, y2 = lax.rem(y + 1, 4), lax.rem(y + 3, 4), lax.rem(y + 2, 4)
    oc = 1 - c

    def zz(k):
        return lax.rem(z + (k + NZ), NZ)

    def where(dp_=None, mp_=None, side_=None):
        at = {"dp": dp if dp_ is None else dp_, "mp": z if mp_ is None else mp_, "side": s if side_ is None else side_}
        return tuple(at[a] for a in axes)

    def jj(a, b):
        return a * 4 + b

    X = where(dp_=xo * 8 + y * 2 + c)
    YP = where(dp_=xl * 8 + yp * 2 + c)
    YM = where(dp_=xl * 8 + ym * 2 + c)
    ZP = where(mp_=zz(1))
    ZM = where(mp_=zz(-1))
    C = where(dp_=dp + 1 - 2 * c)
    S = where(side_=1 - s)

    table_in = pltpu.make_async_copy(table_ref, TAB, local.at[3])
    table_in.start()
    barrier = pltpu.get_barrier_semaphore()
    peers = (X, YP, YM, ZP, ZM, C, S)
    for peer in peers:
        pl.semaphore_signal(barrier, inc=1, device_id=peer, device_id_type=pl.DeviceIdType.MESH)
    pl.semaphore_wait(barrier, len(peers))

    used = [0]
    started = {None: [], 1: []}

    class Copy:
        def __init__(self, refs, dev, side, at=None):
            self.refs, self.dev = refs, dev
            if at is None:
                at = used[0]
                used[0] += 1
            self.i = at
            mine = started[side]
            pool = N_SEND[side]
            self.j = len(mine) % pool + {None: 0, 1: N_SEND[None]}[side]
            if len(mine) >= pool:
                mine[-pool].wait_send()
            self.made().start()
            mine.append(self)

        def made(self):
            src, dst = self.refs()
            return pltpu.make_async_remote_copy(
                src_ref=src, dst_ref=dst, send_sem=send.at[self.j], recv_sem=recv.at[self.i],
                device_id=self.dev, device_id_type=pl.DeviceIdType.MESH,
            )

        def wait_recv(self):
            self.made().wait_recv()

        def wait_send(self):
            self.made().wait_send()

    def copy(src, dst, dev, side=None, at=None):
        return Copy(lambda: (src(), dst()), dev, side, at)

    def copy_same(ref, dev, side=None, at=None):
        return Copy(lambda: (ref(),) * 2, dev, side, at)

    def wait_bytes(i, ref):
        pltpu.make_async_copy(ref, ref, recv.at[i]).wait()

    student = s == 1

    class Gather:
        def __init__(self, buf, ra, four):
            self.buf, self.ra, self.four = buf, ra, four

        def g0(self):
            self.bx = used[0]
            used[0] += 1
            self.xa = copy_same(lambda: self.apart(xl, y), X)
            self.yp = copy_same(lambda: self.buf(own), YP)
            self.ym = copy_same(lambda: self.buf(own), YM)
            self.xb = copy_same(lambda: self.bpart(xl, y), X, at=self.bx)

        def g1(self):
            self.xa.wait_recv()
            self.xap = copy_same(lambda: self.apart(xo, y), YP)
            self.xam = copy_same(lambda: self.apart(xo, y), YM)

        def apart(self, xx, yy):
            return self.buf(jj(xx, yy)).at[:, pl.ds(0, self.ra)]

        def bpart(self, xx, yy):
            b = self.buf(jj(xx, yy))
            return b.at[:, pl.ds(self.ra, b.shape[1] - self.ra)]

        def g2(self):
            self.yp.wait_recv()
            self.rp = copy_same(lambda: self.bpart(xl, ym).at[0], YP)
            self.bxm = copy_same(lambda: self.bpart(xl, ym), X, at=self.bx)
            self.rpa = copy_same(lambda: self.apart(xl, ym).at[0], YP)
            self.ym.wait_recv()
            self.rm = copy_same(lambda: self.bpart(xl, yp).at[1], YM)
            self.bxp = copy_same(lambda: self.bpart(xl, yp), X, at=self.bx)
            self.rma = copy_same(lambda: self.apart(xl, yp).at[1], YM)

        def g3(self):
            self.xap.wait_recv()
            self.rxp = copy_same(lambda: self.buf(jj(xo, ym)).at[0, pl.ds(0, self.ra)], YP)
            self.xam.wait_recv()
            self.rxm = copy_same(lambda: self.buf(jj(xo, yp)).at[1, pl.ds(0, self.ra)], YM)

        def g4(self):
            self.rp.wait_recv()
            self.rm.wait_recv()
            self.bx2 = copy_same(lambda: self.bpart(xl, y2), X, at=self.bx)

        def g5(self):
            for d in (self.rpa, self.rma, self.rxp, self.rxm):
                d.wait_recv()
            wait_bytes(self.bx, self.four())

    own = jj(xl, y)
    u_out = copy(lambda: up_ref.at[:, pl.ds(pl.multiple_of(oc * BLK, 128), BLK)], lambda: U.at[own, c], C)
    d_out = copy(lambda: downt_ref.at[:, :, pl.ds(pl.multiple_of(oc * BLK, 128), BLK)], lambda: D.at[:, own, c], C)
    tok_in = pltpu.make_async_copy(tok_ref, T.at[z], local.at[0])
    tok_in.start()
    u_in = pltpu.make_async_copy(up_ref.at[:, pl.ds(pl.multiple_of(c * BLK, 128), BLK)], U.at[own, c], local.at[1])
    u_in.start()
    d_in = pltpu.make_async_copy(
        downt_ref.at[:, :, pl.ds(pl.multiple_of(c * BLK, 128), BLK)], D.at[:, own, c], local.at[2]
    )
    d_in.start()

    tk = {}

    def tok(hop, p):
        rows = pl.ds(128 * p, 128)
        for q, sign, dev in ((0, -1, ZP), (1, 1, ZM)):
            if (q, hop - 1, p) in tk:
                tk[q, hop - 1, p].wait_recv()
            if hop < 3 or hop == 3 and p == q:
                at = functools.partial(lambda k, rows: tok_ref.at[rows] if k is None else T.at[zz(k), rows], rows=rows)
                src = functools.partial(at, None if hop == 0 else sign * hop)
                tk[q, hop, p] = copy(src, functools.partial(at, sign * hop), dev)

    st = {}

    def stats(hop):
        for q, sign, dev in ((0, -1, ZP), (1, 1, ZM)):
            if (q, hop - 1) in st:
                st[q, hop - 1].wait_recv()
            if hop < 3 or hop == 3 and q == 0:
                st[q, hop] = copy_same(functools.partial(lambda k: ST.at[zz(k)], sign * hop), dev)

    def own_stats():
        x = T[z].astype(F32)
        m = jnp.sum(x, axis=-1, keepdims=True) * (1.0 / BLK)
        x = x - m
        sq = jnp.sum(x * x, axis=-1, keepdims=True)
        lane = lax.broadcasted_iota(jnp.int32, (SEQ, 128), 1)
        ST[z] = jnp.transpose(jnp.where(lane == 0, m, sq))[0:8]

    def all_stats():
        ms = [ST[b, 0:1] for b in range(NZ)]
        mean = ms[0]
        sq = ST[0, 1:2]
        for b in range(1, NZ):
            mean = mean + ms[b]
            sq = sq + ST[b, 1:2]
        mean = mean * (1.0 / NZ)
        apart = (ms[0] - mean) * (ms[0] - mean)
        for b in range(1, NZ):
            apart = apart + (ms[b] - mean) * (ms[b] - mean)
        rs = lax.rsqrt((sq + BLK * apart) * (1.0 / (NZ * BLK)) + 1e-06)
        MEAN[...] = jnp.transpose(jnp.broadcast_to(mean, (128, SEQ)))
        RSTD[...] = jnp.transpose(jnp.broadcast_to(rs, (128, SEQ)))

    n_sem = used[0]
    used[0] += 1

    def norm(k, p):
        b = zz(k)
        at = pl.ds(pl.multiple_of(b * BLK, 128), BLK)
        scale, shift = 1.0 + mod_ref[1:2, at], mod_ref[0:1, at]

        def tile(i, carry):
            rows = pl.ds(pl.multiple_of(128 * p + i * 32, 32), 32)
            m, rs = MEAN[rows], RSTD[rows]
            m, rs = jnp.concatenate([m] * 3, axis=1), jnp.concatenate([rs] * 3, axis=1)
            N[c, b, rows] = ((T[b, rows].astype(F32) - m) * rs * scale + shift).astype(BF)
            return carry

        lax.fori_loop(0, 4, tile, 0)
        copy_same(lambda: N.at[c, zz(k), pl.ds(128 * p, 128)], C, at=n_sem)

    gu = Gather(lambda j: U.at[j], RU, lambda: U.at[0:4, :, RU:192])
    gd = [
        Gather(
            functools.partial(lambda r, j: D.at[r, j], r), RA[r],
            functools.partial(lambda r: D.at[r, 0:4, :, RA[r]:ROWS], r),
        )
        for r in range(R)
    ]

    tok(0, 0)
    u_in.wait()
    u_out.wait_recv()
    gu.g0()
    tok_in.wait()
    own_stats()
    stats(0)
    tok(0, 1)
    table_in.wait()
    n = 3 * NZ * BLK // 128
    plan = TAB[step_ref[0]]
    for i in range(n):
        k, at = divmod(128 * i, NZ * BLK)
        mod_ref[k:k + 1, at:at + 128] = plan[i:i + 1]
    mod_out = copy(lambda: mod_ref, lambda: MODO, S)
    gate = mod_ref[2:3, pl.ds(pl.multiple_of(z * BLK, 128), BLK)]
    gate = jnp.transpose(jnp.broadcast_to(gate, (128, BLK)))
    GATE[:, 0:128] = gate
    GATE[:, 128:256] = gate

    def gate_of_student():
        mod_out.wait_recv()
        at = pl.ds(pl.multiple_of(z * BLK, 128), BLK)
        g = jnp.where(jnp.full((1, BLK), s) == 1, mod_ref[2:3, at], MODO[2:3, at])
        g = jnp.transpose(jnp.broadcast_to(g, (128, BLK)))
        GATEG[:, 0:128] = g
        GATEG[:, 128:256] = g

    tt = jnp.transpose(T[z].astype(F32))
    TOKT[...] = tt
    stats(1)
    tok(1, 0)
    gu.g1()
    tok(1, 1)
    stats(2)
    gu.g2()
    tok(2, 0)
    stats(3)
    tok(2, 1)
    d_in.wait()
    d_out.wait_recv()
    gu.g3()
    gd[3].g0()
    st[0, 3].wait_recv()
    all_stats()
    for k in (0, -1, 1):
        for p in range(2):
            norm(k, p)
    gu.g4()
    gd[1].g0()
    tok(3, 0)
    norm(-2, 0)
    norm(2, 0)
    tok(3, 1)
    norm(-2, 1)
    norm(2, 1)
    gd[0].g0()
    for k in (-3, 3):
        for p in range(2):
            norm(k, p)
    tok(4, 0)
    norm(4, 0)
    tok(4, 1)
    norm(4, 1)
    gd[2].g0()

    def hidden(img):
        h = nn(N[img, 0], U[0].reshape(BLK, BLK))
        for b in range(1, NZ):
            h = h + nn(N[img, b], U[b].reshape(BLK, BLK))
        HP[...] = h

        def act_rows(i, carry):
            rows = pl.ds(pl.multiple_of(i * 32, 32), 32)
            a, g = gelu_pair(HP[rows])
            ACT[img, rows] = a.astype(BF)
            SL[img, rows] = g
            return carry

        lax.fori_loop(0, SEQ // 32, act_rows, 0)

    act_out = []

    def send_act(img):
        @pl.when(student)
        def _():
            act_out.append(copy(lambda: ACT.at[img()], lambda: ACTG.at[img()], S, 1))

    m_out, zs = {}, {}
    z_sems = used[0]
    used[0] += 4 * R

    def ring(r, q, k):
        return z_sems + 4 * r + 2 * q + k % 2


    def mixed(r):
        w = D[r].reshape(NZ * 2 * ROWS, BLK)
        PS[r] = nt(w, ACT[oc]).astype(BF)
        m_out[r] = copy(lambda: PS.at[r], lambda: PR.at[r], C)
        PO[r] = nt(w, ACT[c])

    def val(r, b):
        rows = pl.ds(pl.multiple_of(b * 2 * ROWS, 32), 2 * ROWS)
        return PO[r, rows] + PR[r, rows].astype(F32)

    def zstage(r, k):
        h0, h1 = pl.ds(0, ROWS), pl.ds(ROWS, ROWS)
        if k == 0:
            m_out[r].wait_recv()
            v = val(r, zz(4)).astype(BF)
            ZS[r, 0, 0] = v
            zs[r, 0, 0] = copy(lambda: ZS.at[r, 0, 0, h0], lambda: ZR.at[r, 0, 0, h0], ZP, None, ring(r, 0, 0))
            zs[r, 1, 0] = copy(lambda: ZS.at[r, 0, 0, h1], lambda: ZR.at[r, 1, 0, h1], ZM, None, ring(r, 1, 0))
            return
        for q in range(2):
            zs[r, q, k - 1].wait_recv()
        for q in range(2):
            v = val(r, zz((4 - k) if q == 0 else (k - 4)))
            if k == 1:
                h = slice(0, ROWS) if q == 0 else slice(ROWS, 2 * ROWS)
                g = slice(ROWS, 2 * ROWS) if q == 0 else slice(0, ROWS)
                ZS[r, q, k, h] = (v[h] + ZR[r, q, 0, h].astype(F32)).astype(BF)
                ZS[r, q, k, g] = v[g].astype(BF)
            else:
                ZS[r, q, k] = (v + ZR[r, q, k - 1].astype(F32)).astype(BF)
            at = functools.partial(lambda ref, q: ref.at[r, q, k], q=q)
            to = ZP if q == 0 else ZM
            zs[r, q, k] = copy(functools.partial(at, ZS), functools.partial(at, ZR), to, None, ring(r, q, k))

    sw = {}

    def rows_of(r, h):
        return slice(192 * h + ROWS * r, 192 * h + ROWS * (r + 1))

    def output(r):
        zs[r, 0, 3].wait_recv()
        zs[r, 1, 3].wait_recv()
        m = val(r, z) + ZR[r, 0, 3].astype(F32) + ZR[r, 1, 3].astype(F32)
        for h in range(2):
            w = rows_of(r, h)
            o = (TOKT[w] + GATE[w] * m[ROWS * h:ROWS * (h + 1)]).astype(BF)
            OTA[r, h] = o
            TOKT[w] = o.astype(F32)

        sw[r] = copy(lambda: OTA.at[r], lambda: OTB.at[r], S)

    ag, fw = {}, {}
    for r in range(R):
        fw[r] = used[0]
        used[0] += 1

    def gslice(r, img, b, h):
        n = ROWS if h is not None else 2 * ROWS
        return GT.at[r, img, pl.ds(pl.multiple_of(b * 2 * ROWS + (h or 0) * ROWS, 16), n)]

    def astage(r, k):
        def push(kk, dev, h=None, at=None):
            return copy_same(lambda: gslice(r, c, zz(kk), h), dev, None, fw[r] if at is None else at)

        if k == 0:
            sw[r].wait_recv()
            total = counts_ref[0]
            for i in range(1, 16):
                total = total + counts_ref[i]
            norm = jnp.sqrt(jnp.full((1, SEQ), total, jnp.int32).astype(F32))
            at = lax.broadcasted_iota(jnp.int32, (1, SEQ), 1)
            vrow = jnp.where(at < counts_ref[dp], (2 * s - 1).astype(F32), 0.0) / norm
            for h in range(2):
                w = rows_of(r, h)
                diff = OTA[r, h].astype(F32) - OTB[r, h].astype(F32)
                rows = pl.ds(pl.multiple_of(z * 2 * ROWS + h * ROWS, 16), ROWS)
                GT[r, c, rows] = (GATEG[w] * diff * vrow).astype(BF)
            ag[r, 0, 0] = push(0, ZP, at=ring(r, 0, 4))
            ag[r, 1, 0] = push(0, ZM, at=ring(r, 1, 4))
            push(0, C)
            return
        ag[r, 0, k - 1].wait_recv()
        ag[r, 1, k - 1].wait_recv()
        if k < 4:
            ag[r, 0, k] = push(-k, ZP, 0 if k > 2 else None, ring(r, 0, 4 + k))
        push(-k, C, None if k < 4 else 0)
        if k < 4:
            ag[r, 1, k] = push(k, ZM, 1 if k > 2 else None, ring(r, 1, 4 + k))
        push(k, C, None if k < 4 else 1)

    class Reduce:
        def __init__(self, i):
            self.i, self.a, self.b = i, slice(0, RA[i]), slice(RA[i], ROWS)
            self.ra, self.rb = pl.ds(0, RA[i]), pl.ds(0, ROWS - RA[i])
            self.r = lax.rem(i + 2 * (1 - s), R)

        def both(self, src, dst):
            def one(h):
                return copy(lambda: src().at[h], lambda: dst().at[h], (YP, YM)[h])

            return [one(0), one(1)]

        def q(self, j, rows):
            return QV[self.r, j, :, rows]

        def r0(self):
            i, ra, rb = self.i, self.ra, self.rb
            for h in range(2):
                for x in range(2):
                    A2S[i, h, x, ra] = QV[self.r, jj(x, y2), h, self.a].astype(BF)
            self.a2 = self.both(lambda: A2S.at[i, :, :, ra], lambda: A2R.at[i, :, :, ra])
            for k in range(4):
                XBS[i, k, :, rb] = self.q(jj(xo, k), self.b).astype(BF)
            self.xb = copy(lambda: XBS.at[i, :, :, rb], lambda: XBR.at[i, :, :, rb], X)

        def r1(self):
            i, ra = self.i, self.ra
            for h in range(2):
                self.a2[h].wait_recv()
                for x in range(2):
                    v = self.q(jj(x, (yp, ym)[h]), self.a)
                    A1S[i, h, x, h, ra] = (v[h] + A2R[i, h, x, ra].astype(F32)).astype(BF)
                    A1S[i, h, x, 1 - h, ra] = v[1 - h].astype(BF)
            self.a1 = self.both(lambda: A1S.at[i, :, :, :, ra], lambda: A1R.at[i, :, :, :, ra])

        def r2(self):
            i, rb = self.i, self.rb
            self.xb.wait_recv()
            v = self.q(jj(xl, y2), self.b) + XBR[i, y2, :, rb].astype(F32)
            B2S[i, :, rb] = v.astype(BF)
            self.b2 = self.both(lambda: B2S.at[i, :, rb], lambda: B2R.at[i, :, rb])

        def r3(self):
            i, rb = self.i, self.rb
            for h in range(2):
                self.b2[h].wait_recv()
                yy = (yp, ym)[h]
                v = self.q(jj(xl, yy), self.b) + XBR[i, yy, :, rb].astype(F32)
                B1S[i, h, h, rb] = (v[h] + B2R[i, h, rb].astype(F32)).astype(BF)
                B1S[i, h, 1 - h, rb] = v[1 - h].astype(BF)
            self.b1 = self.both(lambda: B1S.at[i, :, :, rb], lambda: B1R.at[i, :, :, rb])

        def r4(self):
            i, ra = self.i, self.ra
            for h in range(2):
                self.a1[h].wait_recv()
            v = self.q(jj(xo, y), self.a) + A1R[i, 0, xo, :, ra].astype(F32) + A1R[i, 1, xo, :, ra].astype(F32)
            AXS[i, :, ra] = v.astype(BF)
            self.ax = copy(lambda: AXS.at[i, :, ra], lambda: AXR.at[i, :, ra], X)

        def r5(self):
            i, ra, rb = self.i, self.ra, self.rb
            va = self.q(own, self.a) + A1R[i, 0, xl, :, ra].astype(F32) + A1R[i, 1, xl, :, ra].astype(F32)
            vb = self.q(own, self.b) + XBR[i, y, :, rb].astype(F32)
            for d in self.b1:
                d.wait_recv()
            vb = vb + B1R[i, 0, :, rb].astype(F32) + B1R[i, 1, :, rb].astype(F32)
            self.ax.wait_recv()
            FO[i, :, self.a] = va + AXR[i, :, ra].astype(F32)
            FO[i, :, self.b] = vb
            FS[i] = FO[i, oc].astype(BF)
            self.f = copy(lambda: FS.at[i], lambda: FR.at[i], C)

        def r6(self):
            i = self.i
            self.f.wait_recv()
            if i < R // 2:
                HS[i, c] = FO[i, c].astype(BF)
                HS[i, oc] = FR[i]
                self.h = copy(lambda: HS.at[i], lambda: HR.at[i], S)
                return
            FO[i, oc] = FR[i].astype(F32)
            rows = slice(ROWS * (i - R // 2), ROWS * (i - R // 2 + 1))

            def keep(o):
                for h in range(2):
                    o[rows, BLK * h:BLK * (h + 1)] = FO[i, h]

            pl.when(student)(lambda: keep(ug_ref))
            pl.when(s == 0)(lambda: keep(dg_ref))

        def r7(self):
            i = self.i
            self.h.wait_recv()
            rows = slice(ROWS * i, ROWS * (i + 1))

            def keep(o):
                for h in range(2):
                    o[rows, BLK * h:BLK * (h + 1)] = HR[i, h].astype(F32)

            pl.when(student)(lambda: keep(dg_ref))
            pl.when(s == 0)(lambda: keep(ug_ref))

    red = [Reduce(i) for i in range(R)]

    def down_grads(r):
        g = [GT[r, 0], GT[r, 1]]
        q = nn(g[0], ACTG[0]) + nn(g[1], ACTG[1])
        QV[r] = q.reshape(NZ, 2, ROWS, BLK)

    def grad_act(r, first):
        w = D[r].reshape(NZ * 2 * ROWS, BLK)
        for img in range(2):
            v = tn(GT[r, img], w)
            if first:
                GA[img] = v
            else:
                GA[img] += v

    def arrived(r):
        wait_bytes(fw[r], GT.at[r, 0])

    def transposed(part):
        def one(i, carry):
            img, j = lax.div(i, 8), lax.rem(i, 8)
            t = jnp.transpose(N[img, j].astype(F32)).astype(BF)
            for r in range(R):
                for h in range(2):
                    NTR[r, img, pl.ds(pl.multiple_of(j * 2 * ROWS + h * ROWS, 16), ROWS)] = t[rows_of(r, h)]
            return carry

        lax.fori_loop(4 * part, 4 * part + 4, one, 0)

    def up_grads(r):
        q = nn(NTR[r, 0], GP[0]) + nn(NTR[r, 1], GP[1])
        QV[r] = q.reshape(NZ, 2, ROWS, BLK)

    summed = []

    def stage(n, k):
        if k < 4:
            zstage(n, k)
        elif k == 4:
            output(n)
        elif k < 10:
            astage(n, k - 5)
        else:
            arrived(n)
            first = not summed
            summed.append(n)
            pl.when(student)(lambda: grad_act(n, first))

            @pl.when(s == 0)
            def _():
                if first:
                    for d in act_out:
                        d.wait_recv()
                down_grads(n)

    def begin(n):
        if not begun:
            out_ref[...] = jnp.transpose(TOKT[...]).astype(BF)

            @pl.when(student)
            def _():
                for img in range(2):
                    GP[img] = (GA[img] * SL[img]).astype(BF)

        begun.append(n)
        pl.when(student)(lambda: up_grads(n))
        red[n].r0()

    begun, mixed_of, swapped, far = [], [], [], []
    gu.g5()
    for what, n in ORDER:
        if what == "hc":
            hidden(c)
        elif what == "ho":
            wait_bytes(n_sem, N.at[oc])
            hidden(oc)
        elif what[0] == "g":
            getattr(gd[n], what)()
        elif what == "m":
            mixed(n)
            mixed_of.append(n)
            if len(mixed_of) == R:
                send_act(lambda: c)
                send_act(lambda: oc)
        elif what[0] == "s":
            k = int(what[1:])
            if k == 5:
                if not swapped:
                    gate_of_student()
                swapped.append(n)
            stage(n, k)
            if k == 8:
                pl.when(student)(functools.partial(transposed, len(far)))
                far.append(n)
        elif what == "b":
            begin(n)
        else:
            getattr(red[n], what)()

    for d in started[None][-N_SEND[None]:]:
        d.wait_send()

    @pl.when(student)
    def _():
        for d in started[1][-N_SEND[1]:]:
            d.wait_send()


def shards(axes, tokens, up_weight, down_weight, mod_table, timesteps, valid_counts):
    table = mod_table.reshape(mod_table.shape[1], -1, 128)
    downt = down_weight[0].T.reshape(R, ROWS, 2 * BLK)

    v = pltpu.VMEM
    nred = R
    scratch = [
        v((NZ, SEQ, BLK), BF),
        v((NZ, 8, SEQ), F32),
        v((SEQ, 128), F32),
        v((SEQ, 128), F32),
        v((NZ, 2, 192, BLK), BF),
        v((R, NZ, 2, ROWS, BLK), BF),
        v((2, NZ, SEQ, BLK), BF),
        v((R, 2, NZ * 2 * ROWS, SEQ), BF),
        v((SEQ, BLK), F32),
        v((2, SEQ, BLK), F32),
        v((2, SEQ, BLK), BF),
        v((2, SEQ, BLK), BF),
        v((R, NZ * 2 * ROWS, SEQ), F32),
        v((R, NZ * 2 * ROWS, SEQ), BF),
        v((R, NZ * 2 * ROWS, SEQ), BF),
        v((R, 2, 4, 2 * ROWS, SEQ), BF),
        v((R, 2, 4, 2 * ROWS, SEQ), BF),
        v(table.shape, F32),
        v((3, NZ * BLK), F32),
        v((3, NZ * BLK), F32),
        v((BLK, SEQ), F32),
        v((BLK, SEQ), F32),
        v((BLK, SEQ), F32),
        v((R, 2, ROWS, SEQ), BF),
        v((R, 2, ROWS, SEQ), BF),
        v((R, 2, NZ * 2 * ROWS, SEQ), BF),
        v((2, SEQ, BLK), F32),
        v((2, SEQ, BLK), BF),
        v((nred, NZ, 2, ROWS, BLK), F32),
        v((nred, 4, 2, 32, BLK), BF),
        v((nred, 4, 2, 32, BLK), BF),
        v((nred, 2, 2, 32, BLK), BF),
        v((nred, 2, 2, 32, BLK), BF),
        v((nred, 2, 2, 2, 32, BLK), BF),
        v((nred, 2, 2, 2, 32, BLK), BF),
        v((nred, 2, 32, BLK), BF),
        v((nred, 2, 32, BLK), BF),
        v((nred, 2, 2, 32, BLK), BF),
        v((nred, 2, 2, 32, BLK), BF),
        v((nred, 2, 32, BLK), BF),
        v((nred, 2, 32, BLK), BF),
        v((nred, ROWS, BLK), BF),
        v((nred, 2, ROWS, BLK), F32),
        v((nred, ROWS, BLK), BF),
        v((nred, 2, ROWS, BLK), BF),
        v((nred, 2, ROWS, BLK), BF),
        pltpu.SemaphoreType.DMA((sum(N_SEND.values()),)),
        pltpu.SemaphoreType.DMA((N_RECV,)),
        pltpu.SemaphoreType.DMA((4,)),
    ]
    hbm = pl.BlockSpec(memory_space=pl.ANY)
    vm = pl.BlockSpec(memory_space=pltpu.VMEM)
    out, up, down = pl.pallas_call(
        functools.partial(kernel, axes),
        out_shape=(
            jax.ShapeDtypeStruct((SEQ, BLK), BF),
            jax.ShapeDtypeStruct((96, 2 * BLK), F32),
            jax.ShapeDtypeStruct((96, 2 * BLK), F32),
        ),
        in_specs=[hbm, hbm, hbm, hbm] + [pl.BlockSpec(memory_space=pltpu.SMEM)] * 2,
        out_specs=(vm, vm, vm),
        scratch_shapes=scratch,
        compiler_params=pltpu.CompilerParams(
            collective_id=0, has_side_effects=True, vmem_limit_bytes=67043328
        ),
    )(tokens, up_weight[0], downt, table, timesteps, valid_counts)
    def settle(out_in, up_in, down_in, out_to, up_to, down_to):
        out_to[...] = out_in[...]
        up_to[...] = up_in[...]
        down_to[...] = down_in[...]

    out, up, down = pl.pallas_call(
        settle,
        out_shape=(
            jax.ShapeDtypeStruct((SEQ, BLK), BF),
            jax.ShapeDtypeStruct((96, 2 * BLK), F32),
            jax.ShapeDtypeStruct((96, 2 * BLK), F32),
        ),
        in_specs=[vm] * 3,
        out_specs=(vm,) * 3,
    )(out, up, down)
    return out[None], up, down.T


def solution(mesh):
    placed = (
        P("dp", "mp"),
        P("side", "dp", "mp"),
        P("side", "mp", "dp"),
        P("side", None, None, None),
        P("dp"),
        P(),
    )
    return jax.shard_map(
        functools.partial(shards, mesh.axis_names),
        mesh=mesh,
        in_specs=placed,
        out_specs=(P("side", "dp", "mp"), P(("dp", "side"), "mp"), P("mp", ("dp", "side"))),
        check_vma=False,
    )
```

```python
import functools

import jax
import jax.numpy as jnp
from jax import lax
from jax.experimental import pallas as pl
from jax.experimental.pallas import tpu as pltpu
from jax.sharding import PartitionSpec as P

BF = jnp.bfloat16
F32 = jnp.float32
R = 4
ROWS = 192 // R
RA = (32, 32, 32, 16)
RU = 112
ORDER = (
    ("g2", 3), ("g1", 3), ("hc", 0), ("ho", 0), ("g1", 0), ("g4", 3), ("g2", 0), ("g3", 3), ("g1", 1), ("g2", 1),
    ("g2", 2), ("g1", 2), ("g3", 0), ("g4", 0), ("g5", 3), ("m", 3), ("g3", 1), ("g4", 1), ("g4", 2), ("s0", 3),
    ("g3", 2), ("g5", 0), ("m", 0), ("g5", 1), ("m", 1), ("s1", 3), ("g5", 2), ("m", 2), ("s0", 0), ("s0", 1),
    ("s0", 2), ("s2", 3), ("s1", 0), ("s1", 1), ("s1", 2), ("s3", 3), ("s2", 0), ("s2", 1), ("s2", 2), ("s4", 3),
    ("s3", 0), ("s3", 1), ("s3", 2), ("s4", 0), ("s5", 3), ("s4", 1), ("s4", 2), ("s6", 3), ("s5", 0), ("s5", 1),
    ("s5", 2), ("s7", 3), ("s6", 0), ("s6", 1), ("s6", 2), ("s8", 3), ("s7", 0), ("s7", 1), ("s7", 2), ("s9", 3),
    ("s8", 0), ("s10", 3), ("s8", 1), ("s8", 2), ("s9", 0), ("s9", 1), ("s10", 0), ("s9", 2), ("s10", 1), ("s10", 2),
    ("b", 1), ("b", 0), ("b", 3), ("b", 2), ("r1", 1), ("r2", 1), ("r1", 0), ("r1", 3), ("r1", 2), ("r2", 0),
    ("r4", 1), ("r3", 1), ("r4", 0), ("r2", 3), ("r4", 3), ("r2", 2), ("r4", 2), ("r3", 0), ("r5", 1), ("r3", 3),
    ("r3", 2), ("r6", 1), ("r5", 0), ("r6", 0), ("r5", 3), ("r5", 2), ("r6", 3), ("r7", 1), ("r6", 2), ("r7", 0),
)
NZ = 8
SEQ = 256
BLK = 384
N_RECV = 121
N_SEND = {None: 40, 1: 2}


K = 0.7978845608028654


def gelu(v):
    return v * (0.5 * (1.0 + jnp.tanh(K * v * (1.0 + 0.044715 * (v * v)))))


def gelu_slope(v):
    v2 = v * v
    t = jnp.tanh(K * v * (1.0 + 0.044715 * v2))
    return 0.5 * (1.0 + t) + 0.5 * v * (1.0 - t * t) * (K * (1.0 + 3.0 * 0.044715 * v2))


def nn(a, b):
    return lax.dot_general(a, b, (((1,), (0,)), ((), ())), preferred_element_type=F32)


def nt(a, b):
    return lax.dot_general(a, b, (((1,), (1,)), ((), ())), preferred_element_type=F32)


def tn(a, b):
    return lax.dot_general(a, b, (((0,), (0,)), ((), ())), preferred_element_type=F32)


def kernel(
    axes,
    tok_ref, up_ref, downt_ref, table_ref, step_in, counts_in,
    out_ref, ug_ref, dg_ref,
    T, ST, MEAN, RSTD, U, D, N, NTR, HP, SL, ACT, ACTG, PO, PS, PR, ZS, ZR, TAB, step_ref, counts_ref, mod_ref, MODO, GATE, GATEG, TOKT, OTA, OTB, GT, GA, GP,
    QV, XBS, XBR, A2S, A2R, A1S, A1R, B2S, B2R, B1S, B1R, AXS, AXR, FS, FO, FR, HS, HR,
    send, recv, local,
):
    dp, z, s = lax.axis_index("dp"), lax.axis_index("mp"), lax.axis_index("side")
    c = lax.rem(dp, 2)
    y = lax.rem(lax.div(dp, 2), 4)
    xl = lax.div(dp, 8)
    xo = 1 - xl
    yp, ym, y2 = lax.rem(y + 1, 4), lax.rem(y + 3, 4), lax.rem(y + 2, 4)
    oc = 1 - c

    def zz(k):
        return lax.rem(z + (k + NZ), NZ)

    def where(dp_=None, mp_=None, side_=None):
        at = {"dp": dp if dp_ is None else dp_, "mp": z if mp_ is None else mp_, "side": s if side_ is None else side_}
        return tuple(at[a] for a in axes)

    def jj(a, b):
        return a * 4 + b

    X = where(dp_=xo * 8 + y * 2 + c)
    YP = where(dp_=xl * 8 + yp * 2 + c)
    YM = where(dp_=xl * 8 + ym * 2 + c)
    ZP = where(mp_=zz(1))
    ZM = where(mp_=zz(-1))
    C = where(dp_=dp + 1 - 2 * c)
    S = where(side_=1 - s)

    table_in = pltpu.make_async_copy(table_ref, TAB, local.at[3])
    table_in.start()
    step_copy = pltpu.make_async_copy(step_in, step_ref, local.at[4])
    step_copy.start()
    counts_copy = pltpu.make_async_copy(counts_in, counts_ref, local.at[5])
    counts_copy.start()
    barrier = pltpu.get_barrier_semaphore()
    peers = (X, YP, YM, ZP, ZM, C, S)
    for peer in peers:
        pl.semaphore_signal(barrier, inc=1, device_id=peer, device_id_type=pl.DeviceIdType.MESH)
    pl.semaphore_wait(barrier, len(peers))

    used = [0]
    started = {None: [], 1: []}

    class Copy:
        def __init__(self, refs, dev, side, at=None):
            self.refs, self.dev = refs, dev
            if at is None:
                at = used[0]
                used[0] += 1
            self.i = at
            mine = started[side]
            pool = N_SEND[side]
            self.j = len(mine) % pool + {None: 0, 1: N_SEND[None]}[side]
            if len(mine) >= pool:
                mine[-pool].wait_send()
            self.made().start()
            mine.append(self)

        def made(self):
            src, dst = self.refs()
            return pltpu.make_async_remote_copy(
                src_ref=src, dst_ref=dst, send_sem=send.at[self.j], recv_sem=recv.at[self.i],
                device_id=self.dev, device_id_type=pl.DeviceIdType.MESH,
            )

        def wait_recv(self):
            self.made().wait_recv()

        def wait_send(self):
            self.made().wait_send()

    def copy(src, dst, dev, side=None, at=None):
        return Copy(lambda: (src(), dst()), dev, side, at)

    def copy_same(ref, dev, side=None, at=None):
        return Copy(lambda: (ref(),) * 2, dev, side, at)

    def wait_bytes(i, ref):
        pltpu.make_async_copy(ref, ref, recv.at[i]).wait()

    student = s == 1

    class Whole:
        def __init__(self, i, ref):
            self.wait_recv = lambda: wait_bytes(i, ref())

    class Gather:
        def __init__(self, buf, ra, two, four):
            self.buf, self.ra, self.two, self.four = buf, ra, two, four

        def g0(self):
            self.bx = used[0]
            used[0] += 1
            self.xa = copy_same(lambda: self.apart(xl, y), X)
            self.yp = copy_same(lambda: self.buf(own), YP)
            self.ym = copy_same(lambda: self.buf(own), YM)
            self.xb = copy_same(lambda: self.bpart(xl, y), X, at=self.bx)

        def direct(self, mine):
            if mine:
                self.xi, self.yi, self.wi, self.bx = range(used[0], used[0] + 4)
                used[0] += 4
            h, ra = (c if mine else oc), self.ra
            cols = pl.ds(pl.multiple_of(c * BLK, 128), BLK)

            def send(dev, rows, at):
                copy(
                    lambda: up_ref.at[rows, cols] if mine else self.buf(own).at[h, rows],
                    lambda: self.buf(own).at[h, rows], dev, None, at,
                )

            send(X, pl.ds(0, ra), self.xi)
            send(YP, pl.ds(0, 192), self.yi)
            send(YM, pl.ds(0, 192), self.wi)
            send(X, pl.ds(ra, 192 - ra), self.bx)
            self.xa = Whole(self.xi, lambda: self.apart(xo, y))
            self.yp = Whole(self.yi, lambda: self.buf(jj(xl, ym)))
            self.ym = Whole(self.wi, lambda: self.buf(jj(xl, yp)))

        def g1(self):
            self.xa.wait_recv()
            self.xap = copy_same(lambda: self.apart(xo, y), YP)
            self.xam = copy_same(lambda: self.apart(xo, y), YM)

        def apart(self, xx, yy):
            return self.buf(jj(xx, yy)).at[:, pl.ds(0, self.ra)]

        def bpart(self, xx, yy):
            b = self.buf(jj(xx, yy))
            return b.at[:, pl.ds(self.ra, b.shape[1] - self.ra)]

        def g2(self):
            self.yp.wait_recv()
            late = self.late = used[0]
            used[0] += 1
            self.rp = copy_same(lambda: self.bpart(xl, ym).at[0], YP)
            self.bxm = copy_same(lambda: self.bpart(xl, ym), X, at=self.bx)
            copy_same(lambda: self.apart(xl, ym).at[0], YP, None, late)
            self.ym.wait_recv()
            self.rm = copy_same(lambda: self.bpart(xl, yp).at[1], YM)
            self.bxp = copy_same(lambda: self.bpart(xl, yp), X, at=self.bx)
            copy_same(lambda: self.apart(xl, yp).at[1], YM, None, late)

        def g3(self):
            self.xap.wait_recv()
            copy_same(lambda: self.buf(jj(xo, ym)).at[0, pl.ds(0, self.ra)], YP, None, self.late)
            self.xam.wait_recv()
            copy_same(lambda: self.buf(jj(xo, yp)).at[1, pl.ds(0, self.ra)], YM, None, self.late)

        def g4(self):
            self.rp.wait_recv()
            self.rm.wait_recv()
            self.bx2 = copy_same(lambda: self.bpart(xl, y2), X, at=self.bx)

        def g5(self):
            wait_bytes(self.late, self.two())
            wait_bytes(self.bx, self.four())

    own = jj(xl, y)
    u_out = copy(lambda: up_ref.at[:, pl.ds(pl.multiple_of(oc * BLK, 128), BLK)], lambda: U.at[own, c], C)
    gu = Gather(lambda j: U.at[j], RU, lambda: U.at[0:2, :, 0:RU], lambda: U.at[0:4, :, RU:192])
    gu.direct(True)
    tok_in = pltpu.make_async_copy(tok_ref, T.at[z], local.at[0])
    tok_in.start()
    u_in = pltpu.make_async_copy(up_ref.at[:, pl.ds(pl.multiple_of(c * BLK, 128), BLK)], U.at[own, c], local.at[1])
    u_in.start()
    d_in = pltpu.make_async_copy(
        downt_ref.at[:, :, pl.ds(pl.multiple_of(c * BLK, 128), BLK)], D.at[:, own, c], local.at[2]
    )
    d_in.start()

    tk = {}
    t_sems = used[0]
    used[0] += 12

    def tok(hop, p):
        rows = pl.ds(128 * p, 128)
        for q in range(2):
            if (q, hop - 1, p) in tk:
                tk[q, hop - 1, p].wait_recv()
        for q, sign, dev in ((0, -1, ZP), (1, 1, ZM)):
            if hop < 3 or hop == 3 and p == q:
                at = functools.partial(lambda k, rows: tok_ref.at[rows] if k is None else T.at[zz(k), rows], rows=rows)
                src = functools.partial(at, None if hop == 0 else sign * hop)
                tk[q, hop, p] = copy(src, functools.partial(at, sign * hop), dev, None, t_sems + 4 * p + 2 * q + hop % 2)

    st = {}

    def stats(hop):
        for q in range(2):
            if (q, hop - 1) in st:
                st[q, hop - 1].wait_recv()
        for q, sign, dev in ((0, -1, ZP), (1, 1, ZM)):
            if hop < 3 or hop == 3 and q == 0:
                st[q, hop] = copy_same(
                    functools.partial(lambda k: ST.at[zz(k)], sign * hop), dev, None, t_sems + 8 + 2 * q + hop % 2
                )

    def own_stats():
        x = T[z].astype(F32)
        m = jnp.sum(x, axis=-1, keepdims=True) * (1.0 / BLK)
        x = x - m
        sq = jnp.sum(x * x, axis=-1, keepdims=True)
        lane = lax.broadcasted_iota(jnp.int32, (SEQ, 128), 1)
        ST[z] = jnp.transpose(jnp.where(lane == 0, m, sq))[0:8]

    def all_stats():
        ms = [ST[b, 0:1] for b in range(NZ)]
        mean = ms[0]
        sq = ST[0, 1:2]
        for b in range(1, NZ):
            mean = mean + ms[b]
            sq = sq + ST[b, 1:2]
        mean = mean * (1.0 / NZ)
        apart = (ms[0] - mean) * (ms[0] - mean)
        for b in range(1, NZ):
            apart = apart + (ms[b] - mean) * (ms[b] - mean)
        rs = lax.rsqrt((sq + BLK * apart) * (1.0 / (NZ * BLK)) + 1e-06)
        MEAN[...] = jnp.transpose(jnp.broadcast_to(mean, (128, SEQ)))
        RSTD[...] = jnp.transpose(jnp.broadcast_to(rs, (128, SEQ)))

    n_sem = used[0]
    used[0] += 1

    def norm(k, p):
        b = zz(k)
        at = pl.ds(pl.multiple_of(b * BLK, 128), BLK)
        scale, shift = 1.0 + mod_ref[1:2, at], mod_ref[0:1, at]

        def tile(i, carry):
            rows = pl.ds(pl.multiple_of(128 * p + i * 32, 32), 32)
            m, rs = MEAN[rows], RSTD[rows]
            m, rs = jnp.concatenate([m] * 3, axis=1), jnp.concatenate([rs] * 3, axis=1)
            N[c, b, rows] = ((T[b, rows].astype(F32) - m) * rs * scale + shift).astype(BF)
            return carry

        lax.fori_loop(0, 4, tile, 0)
        copy_same(lambda: N.at[c, zz(k), pl.ds(128 * p, 128)], C, at=n_sem)

    gd = [
        Gather(
            functools.partial(lambda r, j: D.at[r, j], r), RA[r],
            functools.partial(lambda r: D.at[r, 0:2, :, 0:RA[r]], r),
            functools.partial(lambda r: D.at[r, 0:4, :, RA[r]:ROWS], r),
        )
        for r in range(R)
    ]

    tok(0, 0)
    u_out.wait_recv()
    gu.direct(False)
    tok_in.wait()
    own_stats()
    stats(0)
    tok(0, 1)
    d_out = copy(lambda: downt_ref.at[:, :, pl.ds(pl.multiple_of(oc * BLK, 128), BLK)], lambda: D.at[:, own, c], C)
    table_in.wait()
    step_copy.wait()
    counts_copy.wait()
    n = 3 * NZ * BLK // 128
    plan = TAB[step_ref[0]]
    for i in range(n):
        k, at = divmod(128 * i, NZ * BLK)
        mod_ref[k:k + 1, at:at + 128] = plan[i:i + 1]
    mod_out = copy(lambda: mod_ref, lambda: MODO, S)
    gate = mod_ref[2:3, pl.ds(pl.multiple_of(z * BLK, 128), BLK)]
    gate = jnp.transpose(jnp.broadcast_to(gate, (128, BLK)))
    GATE[:, 0:128] = gate
    GATE[:, 128:256] = gate

    def gate_of_student():
        mod_out.wait_recv()
        at = pl.ds(pl.multiple_of(z * BLK, 128), BLK)
        g = jnp.where(jnp.full((1, BLK), s) == 1, mod_ref[2:3, at], MODO[2:3, at])
        g = jnp.transpose(jnp.broadcast_to(g, (128, BLK)))
        GATEG[:, 0:128] = g
        GATEG[:, 128:256] = g

    tt = jnp.transpose(T[z].astype(F32))
    TOKT[...] = tt
    stats(1)
    tok(1, 0)
    gu.g1()
    tok(1, 1)
    stats(2)
    gu.g2()
    tok(2, 0)
    stats(3)
    tok(2, 1)
    d_in.wait()
    d_out.wait_recv()
    gu.g3()
    gd[3].g0()
    st[0, 3].wait_recv()
    all_stats()
    for k in (0, -1, 1):
        for p in range(2):
            norm(k, p)
    gu.g4()
    gd[1].g0()
    tok(3, 0)
    norm(-2, 0)
    norm(2, 0)
    tok(3, 1)
    norm(-2, 1)
    norm(2, 1)
    gd[0].g0()
    for k in (-3, 3):
        for p in range(2):
            norm(k, p)
    tok(4, 0)
    norm(4, 0)
    tok(4, 1)
    norm(4, 1)
    gd[2].g0()

    def hidden(img):
        h = nn(N[img, 0], U[0].reshape(BLK, BLK))
        for b in range(1, NZ):
            h = h + nn(N[img, b], U[b].reshape(BLK, BLK))
        HP[img] = h

        def act_rows(i, carry):
            rows = pl.ds(pl.multiple_of(i * 32, 32), 32)
            ACT[img, rows] = gelu(HP[img, rows]).astype(BF)
            return carry

        lax.fori_loop(0, SEQ // 32, act_rows, 0)

    def slopes(img):
        def rows_of_slope(i, carry):
            rows = pl.ds(pl.multiple_of(i * 32, 32), 32)
            SL[img, rows] = gelu_slope(HP[img, rows])
            return carry

        lax.fori_loop(0, SEQ // 32, rows_of_slope, 0)

    act_out = []

    def send_act(img):
        @pl.when(student)
        def _():
            act_out.append(copy(lambda: ACT.at[img()], lambda: ACTG.at[img()], S, 1))

    m_out, zs = {}, {}
    z_sems = used[0]
    used[0] += 4 * R

    def ring(r, q, k):
        return z_sems + 4 * r + 2 * q + k % 2


    def mixed(r):
        w = D[r].reshape(NZ * 2 * ROWS, BLK)
        PS[r] = nt(w, ACT[oc]).astype(BF)
        m_out[r] = copy(lambda: PS.at[r], lambda: PR.at[r], C)
        PO[r] = nt(w, ACT[c])

    def val(r, b):
        rows = pl.ds(pl.multiple_of(b * 2 * ROWS, 32), 2 * ROWS)
        return PO[r, rows] + PR[r, rows].astype(F32)

    def zstage(r, k):
        h0, h1 = pl.ds(0, ROWS), pl.ds(ROWS, ROWS)
        if k == 0:
            m_out[r].wait_recv()
            v = val(r, zz(4)).astype(BF)
            ZS[r, 0, 0] = v
            zs[r, 0, 0] = copy(lambda: ZS.at[r, 0, 0, h0], lambda: ZR.at[r, 0, 0, h0], ZP, None, ring(r, 0, 0))
            zs[r, 1, 0] = copy(lambda: ZS.at[r, 0, 0, h1], lambda: ZR.at[r, 1, 0, h1], ZM, None, ring(r, 1, 0))
            return
        for q in range(2):
            zs[r, q, k - 1].wait_recv()
        for q in range(2):
            v = val(r, zz((4 - k) if q == 0 else (k - 4)))
            if k == 1:
                h = slice(0, ROWS) if q == 0 else slice(ROWS, 2 * ROWS)
                g = slice(ROWS, 2 * ROWS) if q == 0 else slice(0, ROWS)
                ZS[r, q, k, h] = (v[h] + ZR[r, q, 0, h].astype(F32)).astype(BF)
                ZS[r, q, k, g] = v[g].astype(BF)
            else:
                ZS[r, q, k] = (v + ZR[r, q, k - 1].astype(F32)).astype(BF)
            at = functools.partial(lambda ref, q: ref.at[r, q, k], q=q)
            to = ZP if q == 0 else ZM
            zs[r, q, k] = copy(functools.partial(at, ZS), functools.partial(at, ZR), to, None, ring(r, q, k))

    sw = {}

    def rows_of(r, h):
        return slice(192 * h + ROWS * r, 192 * h + ROWS * (r + 1))

    def output(r):
        zs[r, 0, 3].wait_recv()
        zs[r, 1, 3].wait_recv()
        m = val(r, z) + ZR[r, 0, 3].astype(F32) + ZR[r, 1, 3].astype(F32)
        for h in range(2):
            w = rows_of(r, h)
            o = (TOKT[w] + GATE[w] * m[ROWS * h:ROWS * (h + 1)]).astype(BF)
            OTA[r, h] = o
            TOKT[w] = o.astype(F32)

        sw[r] = copy(lambda: OTA.at[r], lambda: OTB.at[r], S)

    ag, fw = {}, {}
    for r in range(R):
        fw[r] = used[0]
        used[0] += 1

    def gslice(r, img, b, h):
        n = ROWS if h is not None else 2 * ROWS
        return GT.at[r, img, pl.ds(pl.multiple_of(b * 2 * ROWS + (h or 0) * ROWS, 16), n)]

    def astage(r, k):
        def push(kk, dev, h=None, at=None):
            return copy_same(lambda: gslice(r, c, zz(kk), h), dev, None, fw[r] if at is None else at)

        if k == 0:
            sw[r].wait_recv()
            total = counts_ref[0]
            for i in range(1, 16):
                total = total + counts_ref[i]
            norm = jnp.sqrt(jnp.full((1, SEQ), total, jnp.int32).astype(F32))
            at = lax.broadcasted_iota(jnp.int32, (1, SEQ), 1)
            vrow = jnp.where(at < counts_ref[dp], (2 * s - 1).astype(F32), 0.0) / norm
            for h in range(2):
                w = rows_of(r, h)
                diff = OTA[r, h].astype(F32) - OTB[r, h].astype(F32)
                rows = pl.ds(pl.multiple_of(z * 2 * ROWS + h * ROWS, 16), ROWS)
                GT[r, c, rows] = (GATEG[w] * diff * vrow).astype(BF)
            ag[r, 0, 0] = push(0, ZP, at=ring(r, 0, 4))
            ag[r, 1, 0] = push(0, ZM, at=ring(r, 1, 4))
            push(0, C)
            return
        ag[r, 0, k - 1].wait_recv()
        ag[r, 1, k - 1].wait_recv()
        if k < 4:
            ag[r, 0, k] = push(-k, ZP, 0 if k > 2 else None, ring(r, 0, 4 + k))
        push(-k, C, None if k < 4 else 0)
        if k < 4:
            ag[r, 1, k] = push(k, ZM, 1 if k > 2 else None, ring(r, 1, 4 + k))
        push(k, C, None if k < 4 else 1)

    class Reduce:
        def __init__(self, i):
            self.i, self.a, self.b = i, slice(0, RA[i]), slice(RA[i], ROWS)
            self.ra, self.rb = pl.ds(0, RA[i]), pl.ds(0, ROWS - RA[i])
            self.r = lax.rem(i + 2 * (1 - s), R)

        def both(self, src, dst):
            at = used[0]
            used[0] += 1
            for h in range(2):
                copy(lambda: src().at[h], lambda: dst().at[h], (YP, YM)[h], None, at)
            return Whole(at, dst)

        def q(self, j, rows):
            return QV[self.r, j, :, rows]

        def r0(self):
            i, ra, rb = self.i, self.ra, self.rb
            for h in range(2):
                for x in range(2):
                    A2S[i, h, x, ra] = QV[self.r, jj(x, y2), h, self.a].astype(BF)
            self.a2 = self.both(lambda: A2S.at[i, :, :, ra], lambda: A2R.at[i, :, :, ra])
            for k in range(4):
                XBS[i, k, :, rb] = self.q(jj(xo, k), self.b).astype(BF)
            self.xb = copy(lambda: XBS.at[i, :, :, rb], lambda: XBR.at[i, :, :, rb], X)

        def r1(self):
            i, ra = self.i, self.ra
            self.a2.wait_recv()
            for h in range(2):
                for x in range(2):
                    v = self.q(jj(x, (yp, ym)[h]), self.a)
                    A1S[i, h, x, h, ra] = (v[h] + A2R[i, h, x, ra].astype(F32)).astype(BF)
                    A1S[i, h, x, 1 - h, ra] = v[1 - h].astype(BF)
            self.a1 = self.both(lambda: A1S.at[i, :, :, :, ra], lambda: A1R.at[i, :, :, :, ra])

        def r2(self):
            i, rb = self.i, self.rb
            self.xb.wait_recv()
            v = self.q(jj(xl, y2), self.b) + XBR[i, y2, :, rb].astype(F32)
            B2S[i, :, rb] = v.astype(BF)
            self.b2 = self.both(lambda: B2S.at[i, :, rb], lambda: B2R.at[i, :, rb])

        def r3(self):
            i, rb = self.i, self.rb
            self.b2.wait_recv()
            for h in range(2):
                yy = (yp, ym)[h]
                v = self.q(jj(xl, yy), self.b) + XBR[i, yy, :, rb].astype(F32)
                B1S[i, h, h, rb] = (v[h] + B2R[i, h, rb].astype(F32)).astype(BF)
                B1S[i, h, 1 - h, rb] = v[1 - h].astype(BF)
            self.b1 = self.both(lambda: B1S.at[i, :, :, rb], lambda: B1R.at[i, :, :, rb])

        def r4(self):
            i, ra = self.i, self.ra
            self.a1.wait_recv()
            v = self.q(jj(xo, y), self.a) + A1R[i, 0, xo, :, ra].astype(F32) + A1R[i, 1, xo, :, ra].astype(F32)
            AXS[i, :, ra] = v.astype(BF)
            self.ax = copy(lambda: AXS.at[i, :, ra], lambda: AXR.at[i, :, ra], X)

        def r5(self):
            i, ra, rb = self.i, self.ra, self.rb
            va = self.q(own, self.a) + A1R[i, 0, xl, :, ra].astype(F32) + A1R[i, 1, xl, :, ra].astype(F32)
            vb = self.q(own, self.b) + XBR[i, y, :, rb].astype(F32)
            self.b1.wait_recv()
            vb = vb + B1R[i, 0, :, rb].astype(F32) + B1R[i, 1, :, rb].astype(F32)
            self.ax.wait_recv()
            FO[i, :, self.a] = va + AXR[i, :, ra].astype(F32)
            FO[i, :, self.b] = vb
            FS[i] = FO[i, oc].astype(BF)
            self.f = copy(lambda: FS.at[i], lambda: FR.at[i], C)

        def r6(self):
            i = self.i
            self.f.wait_recv()
            if i < R // 2:
                HS[i, c] = FO[i, c].astype(BF)
                HS[i, oc] = FR[i]
                self.h = copy(lambda: HS.at[i], lambda: HR.at[i], S)
                return
            FO[i, oc] = FR[i].astype(F32)
            rows = slice(ROWS * (i - R // 2), ROWS * (i - R // 2 + 1))

            def keep(o):
                for h in range(2):
                    o[rows, BLK * h:BLK * (h + 1)] = FO[i, h]

            pl.when(student)(lambda: keep(ug_ref))
            pl.when(s == 0)(lambda: keep(dg_ref))

        def r7(self):
            i = self.i
            self.h.wait_recv()
            rows = slice(ROWS * i, ROWS * (i + 1))

            def keep(o):
                for h in range(2):
                    o[rows, BLK * h:BLK * (h + 1)] = HR[i, h].astype(F32)

            pl.when(student)(lambda: keep(dg_ref))
            pl.when(s == 0)(lambda: keep(ug_ref))

    red = [Reduce(i) for i in range(R)]

    def down_grads(r):
        g = [GT[r, 0], GT[r, 1]]
        q = nn(g[0], ACTG[0]) + nn(g[1], ACTG[1])
        QV[r] = q.reshape(NZ, 2, ROWS, BLK)

    def grad_act(r, first):
        w = D[r].reshape(NZ * 2 * ROWS, BLK)
        for img in range(2):
            v = tn(GT[r, img], w)
            if first:
                GA[img] = v
            else:
                GA[img] += v

    def arrived(r):
        wait_bytes(fw[r], GT.at[r, 0])

    def transposed(part):
        def one(i, carry):
            img, j = lax.div(i, 8), lax.rem(i, 8)
            t = jnp.transpose(N[img, j].astype(F32)).astype(BF)
            for r in range(R):
                for h in range(2):
                    NTR[r, img, pl.ds(pl.multiple_of(j * 2 * ROWS + h * ROWS, 16), ROWS)] = t[rows_of(r, h)]
            return carry

        lax.fori_loop(4 * part, 4 * part + 4, one, 0)

    def up_grads(r):
        q = nn(NTR[r, 0], GP[0]) + nn(NTR[r, 1], GP[1])
        QV[r] = q.reshape(NZ, 2, ROWS, BLK)

    summed = []

    def stage(n, k):
        if k < 4:
            zstage(n, k)
        elif k == 4:
            output(n)
        elif k < 10:
            astage(n, k - 5)
        else:
            arrived(n)
            first = not summed
            summed.append(n)
            pl.when(student)(lambda: grad_act(n, first))

            @pl.when(s == 0)
            def _():
                if first:
                    for d in act_out:
                        d.wait_recv()
                down_grads(n)

    def begin(n):
        if not begun:
            @pl.when(student)
            def _():
                for img in range(2):
                    GP[img] = (GA[img] * SL[img]).astype(BF)

        begun.append(n)
        pl.when(student)(lambda: up_grads(n))
        red[n].r0()

    u_in.wait()
    begun, mixed_of, swapped, far, put, sloped = [], [], [], [], [], []
    gu.g5()
    for what, n in ORDER:
        if what == "hc":
            hidden(c)
        elif what == "ho":
            wait_bytes(n_sem, N.at[oc])
            hidden(oc)
        elif what[0] == "g":
            getattr(gd[n], what)()
        elif what == "m":
            mixed(n)
            mixed_of.append(n)
            if len(mixed_of) == R:
                send_act(lambda: c)
                send_act(lambda: oc)
        elif what[0] == "s":
            k = int(what[1:])
            if k == 5:
                if not swapped:
                    gate_of_student()
                swapped.append(n)
            stage(n, k)
            if k == 4:
                put.append(n)
                if len(put) == R:
                    out_ref[...] = jnp.transpose(TOKT[...]).astype(BF)
            if k == 6 and len(sloped) < 2:
                pl.when(student)(functools.partial(slopes, len(sloped)))
                sloped.append(n)
            if k == 8:
                pl.when(student)(functools.partial(transposed, len(far)))
                far.append(n)
        elif what == "b":
            begin(n)
        else:
            getattr(red[n], what)()

    for d in started[None][-N_SEND[None]:]:
        d.wait_send()

    @pl.when(student)
    def _():
        for d in started[1][-N_SEND[1]:]:
            d.wait_send()


def shards(axes, tokens, up_weight, down_weight, mod_table, timesteps, valid_counts):
    table = mod_table.reshape(mod_table.shape[1], -1, 128)
    downt = down_weight[0].T.reshape(R, ROWS, 2 * BLK)

    v = pltpu.VMEM
    nred = R
    scratch = [
        v((NZ, SEQ, BLK), BF),
        v((NZ, 8, SEQ), F32),
        v((SEQ, 128), F32),
        v((SEQ, 128), F32),
        v((NZ, 2, 192, BLK), BF),
        v((R, NZ, 2, ROWS, BLK), BF),
        v((2, NZ, SEQ, BLK), BF),
        v((R, 2, NZ * 2 * ROWS, SEQ), BF),
        v((2, SEQ, BLK), F32),
        v((2, SEQ, BLK), F32),
        v((2, SEQ, BLK), BF),
        v((2, SEQ, BLK), BF),
        v((R, NZ * 2 * ROWS, SEQ), F32),
        v((R, NZ * 2 * ROWS, SEQ), BF),
        v((R, NZ * 2 * ROWS, SEQ), BF),
        v((R, 2, 4, 2 * ROWS, SEQ), BF),
        v((R, 2, 4, 2 * ROWS, SEQ), BF),
        v(table.shape, F32),
        pltpu.SMEM(timesteps.shape, jnp.int32),
        pltpu.SMEM(valid_counts.shape, jnp.int32),
        v((3, NZ * BLK), F32),
        v((3, NZ * BLK), F32),
        v((BLK, SEQ), F32),
        v((BLK, SEQ), F32),
        v((BLK, SEQ), F32),
        v((R, 2, ROWS, SEQ), BF),
        v((R, 2, ROWS, SEQ), BF),
        v((R, 2, NZ * 2 * ROWS, SEQ), BF),
        v((2, SEQ, BLK), F32),
        v((2, SEQ, BLK), BF),
        v((nred, NZ, 2, ROWS, BLK), F32),
        v((nred, 4, 2, 32, BLK), BF),
        v((nred, 4, 2, 32, BLK), BF),
        v((nred, 2, 2, 32, BLK), BF),
        v((nred, 2, 2, 32, BLK), BF),
        v((nred, 2, 2, 2, 32, BLK), BF),
        v((nred, 2, 2, 2, 32, BLK), BF),
        v((nred, 2, 32, BLK), BF),
        v((nred, 2, 32, BLK), BF),
        v((nred, 2, 2, 32, BLK), BF),
        v((nred, 2, 2, 32, BLK), BF),
        v((nred, 2, 32, BLK), BF),
        v((nred, 2, 32, BLK), BF),
        v((nred, ROWS, BLK), BF),
        v((nred, 2, ROWS, BLK), F32),
        v((nred, ROWS, BLK), BF),
        v((nred, 2, ROWS, BLK), BF),
        v((nred, 2, ROWS, BLK), BF),
        pltpu.SemaphoreType.DMA((sum(N_SEND.values()),)),
        pltpu.SemaphoreType.DMA((N_RECV,)),
        pltpu.SemaphoreType.DMA((6,)),
    ]
    hbm = pl.BlockSpec(memory_space=pl.ANY)
    vm = pl.BlockSpec(memory_space=pltpu.VMEM)
    out, up, down = pl.pallas_call(
        functools.partial(kernel, axes),
        out_shape=(
            jax.ShapeDtypeStruct((SEQ, BLK), BF),
            jax.ShapeDtypeStruct((96, 2 * BLK), F32),
            jax.ShapeDtypeStruct((96, 2 * BLK), F32),
        ),
        in_specs=[hbm] * 6,
        out_specs=(vm, vm, vm),
        scratch_shapes=scratch,
        compiler_params=pltpu.CompilerParams(
            collective_id=0, has_side_effects=True, vmem_limit_bytes=67043328
        ),
    )(tokens, up_weight[0], downt, table, timesteps, valid_counts)
    def settle(out_in, up_in, down_in, out_to, up_to, down_to):
        out_to[...] = out_in[...]
        up_to[...] = up_in[...]
        down_to[...] = down_in[...]

    out, up, down = pl.pallas_call(
        settle,
        out_shape=(
            jax.ShapeDtypeStruct((SEQ, BLK), BF),
            jax.ShapeDtypeStruct((96, 2 * BLK), F32),
            jax.ShapeDtypeStruct((96, 2 * BLK), F32),
        ),
        in_specs=[vm] * 3,
        out_specs=(vm,) * 3,
    )(out, up, down)
    return out[None], up, down.T


def solution(mesh):
    placed = (
        P("dp", "mp"),
        P("side", "dp", "mp"),
        P("side", "mp", "dp"),
        P("side", None, None, None),
        P("dp"),
        P(),
    )
    return jax.shard_map(
        functools.partial(shards, mesh.axis_names),
        mesh=mesh,
        in_specs=placed,
        out_specs=(P("side", "dp", "mp"), P(("dp", "side"), "mp"), P("mp", ("dp", "side"))),
        check_vma=False,
    )
```

```python
import functools

import jax
import jax.numpy as jnp
from jax import lax
from jax.experimental import pallas as pl
from jax.experimental.pallas import tpu as pltpu
from jax.sharding import PartitionSpec as P

BF = jnp.bfloat16
F32 = jnp.float32
R = 4
ROWS = 192 // R
RA = (32, 32, 32, 16)
RU = 112
ORDER = (
    ("g0", 0), ("g2", 3), ("g1", 3), ("g0", 2), ("hc", 0), ("g1", 1), ("ho", 0), ("g4", 3), ("g2", 1), ("g3", 3),
    ("g1", 0), ("g3", 1), ("g4", 1), ("g2", 0), ("g1", 2), ("g2", 2), ("g5", 3), ("m", 3), ("g4", 0), ("g3", 0),
    ("g5", 1), ("m", 1), ("g4", 2), ("g3", 2), ("s0", 3), ("g5", 0), ("s0", 1), ("m", 0), ("g5", 2), ("s1", 3),
    ("m", 2), ("s0", 0), ("s1", 1), ("s0", 2), ("sl", 1), ("s2", 3), ("s1", 0), ("s2", 1), ("s1", 2), ("tr", 1),
    ("s3", 3), ("tr", 3), ("s2", 0), ("s3", 1), ("tr", 0), ("tr", 2), ("s2", 2), ("s4", 3), ("s3", 0), ("s4", 1),
    ("s3", 2), ("s4", 0), ("s5", 3), ("s4", 2), ("s5", 1), ("s6", 3), ("s5", 0), ("s6", 1), ("s5", 2), ("s7", 3),
    ("s6", 0), ("s6", 2), ("s7", 1), ("s7", 0), ("s7", 2), ("s8", 3), ("s8", 1), ("s8", 0), ("s8", 2), ("s9", 3),
    ("sl", 0), ("s9", 1), ("s9", 0), ("s10", 3), ("s9", 2), ("s10", 1), ("s10", 0), ("s10", 2), ("b", 1), ("b", 0),
    ("b", 2), ("b", 3), ("r1", 1), ("r2", 1), ("r1", 0), ("r2", 0), ("r4", 1), ("r1", 2), ("r3", 1), ("r2", 2),
    ("r3", 0), ("r4", 0), ("r1", 3), ("r4", 2), ("r2", 3), ("r5", 1), ("r5", 0), ("r4", 3), ("r6", 1), ("r3", 2),
    ("r3", 3), ("r6", 0), ("r5", 2), ("r5", 3), ("r6", 2), ("r7", 1), ("r6", 3), ("r7", 0),
)
NZ = 8
SEQ = 256
BLK = 384
N_RECV = 121
N_SEND = {None: 40, 1: 2}


K = 0.7978845608028654


def gelu(v):
    return v * (0.5 * (1.0 + jnp.tanh(K * v * (1.0 + 0.044715 * (v * v)))))


def gelu_slope(v):
    v2 = v * v
    t = jnp.tanh(K * v * (1.0 + 0.044715 * v2))
    return 0.5 * (1.0 + t) + 0.5 * v * (1.0 - t * t) * (K * (1.0 + 3.0 * 0.044715 * v2))


def nn(a, b):
    return lax.dot_general(a, b, (((1,), (0,)), ((), ())), preferred_element_type=F32)


def nt(a, b):
    return lax.dot_general(a, b, (((1,), (1,)), ((), ())), preferred_element_type=F32)


def tn(a, b):
    return lax.dot_general(a, b, (((0,), (0,)), ((), ())), preferred_element_type=F32)


def kernel(
    axes,
    tok_ref, up_ref, downt_ref, table_ref, step_in, counts_in,
    out_to, ug_ref, dg_ref,
    out_ref, T, ST, MEAN, RSTD, U, D, N, NTR, HP, SL, ACT, ACTG, PO, PS, PR, ZS, ZR, TAB, step_ref, counts_ref, mod_ref, MODO, GATE, GATEG, TOKT, OTA, OTB, GT, GA, GP,
    QV, XBS, XBR, A2S, A2R, A1S, A1R, B2S, B2R, B1S, B1R, AXS, AXR, FS, FO, FR, HS, HR,
    send, recv, local,
):
    dp, z, s = lax.axis_index("dp"), lax.axis_index("mp"), lax.axis_index("side")
    c = lax.rem(dp, 2)
    y = lax.rem(lax.div(dp, 2), 4)
    xl = lax.div(dp, 8)
    xo = 1 - xl
    yp, ym, y2 = lax.rem(y + 1, 4), lax.rem(y + 3, 4), lax.rem(y + 2, 4)
    oc = 1 - c

    def zz(k):
        return lax.rem(z + (k + NZ), NZ)

    def where(dp_=None, mp_=None, side_=None):
        at = {"dp": dp if dp_ is None else dp_, "mp": z if mp_ is None else mp_, "side": s if side_ is None else side_}
        return tuple(at[a] for a in axes)

    def jj(a, b):
        return a * 4 + b

    X = where(dp_=xo * 8 + y * 2 + c)
    YP = where(dp_=xl * 8 + yp * 2 + c)
    YM = where(dp_=xl * 8 + ym * 2 + c)
    ZP = where(mp_=zz(1))
    ZM = where(mp_=zz(-1))
    C = where(dp_=dp + 1 - 2 * c)
    S = where(side_=1 - s)

    table_in = pltpu.make_async_copy(table_ref, TAB, local.at[3])
    table_in.start()
    step_copy = pltpu.make_async_copy(step_in, step_ref, local.at[4])
    step_copy.start()
    counts_copy = pltpu.make_async_copy(counts_in, counts_ref, local.at[5])
    counts_copy.start()
    barrier = pltpu.get_barrier_semaphore()
    peers = (X, YP, YM, ZP, ZM, C, S)
    for peer in peers:
        pl.semaphore_signal(barrier, inc=1, device_id=peer, device_id_type=pl.DeviceIdType.MESH)
    pl.semaphore_wait(barrier, len(peers))

    used = [0]
    started = {None: [], 1: []}

    class Copy:
        def __init__(self, refs, dev, side, at=None):
            self.refs, self.dev = refs, dev
            if at is None:
                at = used[0]
                used[0] += 1
            self.i = at
            mine = started[side]
            pool = N_SEND[side]
            self.j = len(mine) % pool + {None: 0, 1: N_SEND[None]}[side]
            if len(mine) >= pool:
                mine[-pool].wait_send()
            self.made().start()
            mine.append(self)

        def made(self):
            src, dst = self.refs()
            return pltpu.make_async_remote_copy(
                src_ref=src, dst_ref=dst, send_sem=send.at[self.j], recv_sem=recv.at[self.i],
                device_id=self.dev, device_id_type=pl.DeviceIdType.MESH,
            )

        def wait_recv(self):
            self.made().wait_recv()

        def wait_send(self):
            self.made().wait_send()

    def copy(src, dst, dev, side=None, at=None):
        return Copy(lambda: (src(), dst()), dev, side, at)

    def copy_same(ref, dev, side=None, at=None):
        return Copy(lambda: (ref(),) * 2, dev, side, at)

    def wait_bytes(i, ref):
        pltpu.make_async_copy(ref, ref, recv.at[i]).wait()

    student = s == 1

    class Whole:
        def __init__(self, i, ref):
            self.wait_recv = lambda: wait_bytes(i, ref())

    class Gather:
        def __init__(self, buf, ra, two, four):
            self.buf, self.ra, self.two, self.four = buf, ra, two, four

        def g0(self):
            self.bx = used[0]
            used[0] += 1
            self.xa = copy_same(lambda: self.apart(xl, y), X)
            self.yp = copy_same(lambda: self.buf(own), YP)
            self.ym = copy_same(lambda: self.buf(own), YM)
            self.xb = copy_same(lambda: self.bpart(xl, y), X, at=self.bx)

        def direct(self, mine):
            if mine:
                self.xi, self.yi, self.wi, self.bx = range(used[0], used[0] + 4)
                used[0] += 4
            h, ra = (c if mine else oc), self.ra
            cols = pl.ds(pl.multiple_of(c * BLK, 128), BLK)

            def send(dev, rows, at):
                copy(
                    lambda: up_ref.at[rows, cols] if mine else self.buf(own).at[h, rows],
                    lambda: self.buf(own).at[h, rows], dev, None, at,
                )

            send(X, pl.ds(0, ra), self.xi)
            send(YP, pl.ds(0, 192), self.yi)
            send(YM, pl.ds(0, 192), self.wi)
            send(X, pl.ds(ra, 192 - ra), self.bx)
            self.xa = Whole(self.xi, lambda: self.apart(xo, y))
            self.yp = Whole(self.yi, lambda: self.buf(jj(xl, ym)))
            self.ym = Whole(self.wi, lambda: self.buf(jj(xl, yp)))

        def g1(self):
            self.xa.wait_recv()
            self.xap = copy_same(lambda: self.apart(xo, y), YP)
            self.xam = copy_same(lambda: self.apart(xo, y), YM)

        def apart(self, xx, yy):
            return self.buf(jj(xx, yy)).at[:, pl.ds(0, self.ra)]

        def bpart(self, xx, yy):
            b = self.buf(jj(xx, yy))
            return b.at[:, pl.ds(self.ra, b.shape[1] - self.ra)]

        def g2(self):
            self.yp.wait_recv()
            late = self.late = used[0]
            used[0] += 1
            self.rp = copy_same(lambda: self.bpart(xl, ym).at[0], YP)
            self.bxm = copy_same(lambda: self.bpart(xl, ym), X, at=self.bx)
            copy_same(lambda: self.apart(xl, ym).at[0], YP, None, late)
            self.ym.wait_recv()
            self.rm = copy_same(lambda: self.bpart(xl, yp).at[1], YM)
            self.bxp = copy_same(lambda: self.bpart(xl, yp), X, at=self.bx)
            copy_same(lambda: self.apart(xl, yp).at[1], YM, None, late)

        def g3(self):
            self.xap.wait_recv()
            copy_same(lambda: self.buf(jj(xo, ym)).at[0, pl.ds(0, self.ra)], YP, None, self.late)
            self.xam.wait_recv()
            copy_same(lambda: self.buf(jj(xo, yp)).at[1, pl.ds(0, self.ra)], YM, None, self.late)

        def g4(self):
            self.rp.wait_recv()
            self.rm.wait_recv()
            self.bx2 = copy_same(lambda: self.bpart(xl, y2), X, at=self.bx)

        def g5(self):
            wait_bytes(self.late, self.two())
            wait_bytes(self.bx, self.four())

    own = jj(xl, y)
    u_out = copy(lambda: up_ref.at[:, pl.ds(pl.multiple_of(oc * BLK, 128), BLK)], lambda: U.at[own, c], C)
    gu = Gather(lambda j: U.at[j], RU, lambda: U.at[0:2, :, 0:RU], lambda: U.at[0:4, :, RU:192])
    gu.direct(True)
    tok_in = pltpu.make_async_copy(tok_ref, T.at[z], local.at[0])
    tok_in.start()
    u_in = pltpu.make_async_copy(up_ref.at[:, pl.ds(pl.multiple_of(c * BLK, 128), BLK)], U.at[own, c], local.at[1])
    u_in.start()
    d_in = pltpu.make_async_copy(
        downt_ref.at[:, :, pl.ds(pl.multiple_of(c * BLK, 128), BLK)], D.at[:, own, c], local.at[2]
    )
    d_in.start()

    tk = {}
    t_sems = used[0]
    used[0] += 12

    def tok(hop, p):
        rows = pl.ds(128 * p, 128)
        for q in range(2):
            if (q, hop - 1, p) in tk:
                tk[q, hop - 1, p].wait_recv()
        for q, sign, dev in ((0, -1, ZP), (1, 1, ZM)):
            if hop < 3 or hop == 3 and p == q:
                at = functools.partial(lambda k, rows: tok_ref.at[rows] if k is None else T.at[zz(k), rows], rows=rows)
                src = functools.partial(at, None if hop == 0 else sign * hop)
                tk[q, hop, p] = copy(src, functools.partial(at, sign * hop), dev, None, t_sems + 4 * p + 2 * q + hop % 2)

    st = {}

    def stats(hop):
        for q in range(2):
            if (q, hop - 1) in st:
                st[q, hop - 1].wait_recv()
        for q, sign, dev in ((0, -1, ZP), (1, 1, ZM)):
            if hop < 3 or hop == 3 and q == 0:
                st[q, hop] = copy_same(
                    functools.partial(lambda k: ST.at[zz(k)], sign * hop), dev, None, t_sems + 8 + 2 * q + hop % 2
                )

    def own_stats():
        x = T[z].astype(F32)
        m = jnp.sum(x, axis=-1, keepdims=True) * (1.0 / BLK)
        x = x - m
        sq = jnp.sum(x * x, axis=-1, keepdims=True)
        lane = lax.broadcasted_iota(jnp.int32, (SEQ, 128), 1)
        ST[z] = jnp.transpose(jnp.where(lane == 0, m, sq))[0:8]

    def all_stats():
        ms = [ST[b, 0:1] for b in range(NZ)]
        mean = ms[0]
        sq = ST[0, 1:2]
        for b in range(1, NZ):
            mean = mean + ms[b]
            sq = sq + ST[b, 1:2]
        mean = mean * (1.0 / NZ)
        apart = (ms[0] - mean) * (ms[0] - mean)
        for b in range(1, NZ):
            apart = apart + (ms[b] - mean) * (ms[b] - mean)
        rs = lax.rsqrt((sq + BLK * apart) * (1.0 / (NZ * BLK)) + 1e-06)
        MEAN[...] = jnp.transpose(jnp.broadcast_to(mean, (128, SEQ)))
        RSTD[...] = jnp.transpose(jnp.broadcast_to(rs, (128, SEQ)))

    n_sem = used[0]
    used[0] += 1

    def norm(k, p):
        b = zz(k)
        at = pl.ds(pl.multiple_of(b * BLK, 128), BLK)
        scale, shift = 1.0 + mod_ref[1:2, at], mod_ref[0:1, at]

        def tile(i, carry):
            rows = pl.ds(pl.multiple_of(128 * p + i * 32, 32), 32)
            m, rs = MEAN[rows], RSTD[rows]
            m, rs = jnp.concatenate([m] * 3, axis=1), jnp.concatenate([rs] * 3, axis=1)
            N[c, b, rows] = ((T[b, rows].astype(F32) - m) * rs * scale + shift).astype(BF)
            return carry

        lax.fori_loop(0, 4, tile, 0)
        copy_same(lambda: N.at[c, zz(k), pl.ds(128 * p, 128)], C, at=n_sem)

    gd = [
        Gather(
            functools.partial(lambda r, j: D.at[r, j], r), RA[r],
            functools.partial(lambda r: D.at[r, 0:2, :, 0:RA[r]], r),
            functools.partial(lambda r: D.at[r, 0:4, :, RA[r]:ROWS], r),
        )
        for r in range(R)
    ]

    tok(0, 0)
    u_out.wait_recv()
    gu.direct(False)
    tok_in.wait()
    own_stats()
    stats(0)
    tok(0, 1)
    d_out = copy(lambda: downt_ref.at[:, :, pl.ds(pl.multiple_of(oc * BLK, 128), BLK)], lambda: D.at[:, own, c], C)
    table_in.wait()
    step_copy.wait()
    counts_copy.wait()
    n = 3 * NZ * BLK // 128
    plan = TAB[step_ref[0]]
    for i in range(n):
        k, at = divmod(128 * i, NZ * BLK)
        mod_ref[k:k + 1, at:at + 128] = plan[i:i + 1]
    mod_out = copy(lambda: mod_ref, lambda: MODO, S)
    gate = mod_ref[2:3, pl.ds(pl.multiple_of(z * BLK, 128), BLK)]
    gate = jnp.transpose(jnp.broadcast_to(gate, (128, BLK)))
    GATE[:, 0:128] = gate
    GATE[:, 128:256] = gate

    def gate_of_student():
        mod_out.wait_recv()
        at = pl.ds(pl.multiple_of(z * BLK, 128), BLK)
        g = jnp.where(jnp.full((1, BLK), s) == 1, mod_ref[2:3, at], MODO[2:3, at])
        g = jnp.transpose(jnp.broadcast_to(g, (128, BLK)))
        GATEG[:, 0:128] = g
        GATEG[:, 128:256] = g

    tt = jnp.transpose(T[z].astype(F32))
    TOKT[...] = tt
    stats(1)
    tok(1, 0)
    gu.g1()
    tok(1, 1)
    stats(2)
    gu.g2()
    tok(2, 0)
    stats(3)
    tok(2, 1)
    d_in.wait()
    d_out.wait_recv()
    gu.g3()
    gd[3].g0()
    st[0, 3].wait_recv()
    all_stats()
    for k in (0, -1, 1):
        for p in range(2):
            norm(k, p)
    gu.g4()
    gd[1].g0()
    tok(3, 0)
    norm(-2, 0)
    norm(2, 0)
    tok(3, 1)
    norm(-2, 1)
    norm(2, 1)
    for k in (-3, 3):
        for p in range(2):
            norm(k, p)
    tok(4, 0)
    norm(4, 0)
    tok(4, 1)
    norm(4, 1)

    def hidden(img):
        h = nn(N[img, 0], U[0].reshape(BLK, BLK))
        for b in range(1, NZ):
            h = h + nn(N[img, b], U[b].reshape(BLK, BLK))
        HP[img] = h

        def act_rows(i, carry):
            rows = pl.ds(pl.multiple_of(i * 32, 32), 32)
            ACT[img, rows] = gelu(HP[img, rows]).astype(BF)
            return carry

        lax.fori_loop(0, SEQ // 32, act_rows, 0)

    def slopes(img):
        def rows_of_slope(i, carry):
            rows = pl.ds(pl.multiple_of(i * 32, 32), 32)
            SL[img, rows] = gelu_slope(HP[img, rows])
            return carry

        lax.fori_loop(0, SEQ // 32, rows_of_slope, 0)

    act_out = []

    def send_act(img):
        @pl.when(student)
        def _():
            act_out.append(copy(lambda: ACT.at[img()], lambda: ACTG.at[img()], S, 1))

    m_out, zs = {}, {}
    z_sems = used[0]
    used[0] += 4 * R

    def ring(r, q, k):
        return z_sems + 4 * r + 2 * q + k % 2


    def mixed(r):
        w = D[r].reshape(NZ * 2 * ROWS, BLK)
        PS[r] = nt(w, ACT[oc]).astype(BF)
        m_out[r] = copy(lambda: PS.at[r], lambda: PR.at[r], C)
        PO[r] = nt(w, ACT[c])

    def val(r, b):
        rows = pl.ds(pl.multiple_of(b * 2 * ROWS, 32), 2 * ROWS)
        return PO[r, rows] + PR[r, rows].astype(F32)

    def zstage(r, k):
        h0, h1 = pl.ds(0, ROWS), pl.ds(ROWS, ROWS)
        if k == 0:
            m_out[r].wait_recv()
            v = val(r, zz(4)).astype(BF)
            ZS[r, 0, 0] = v
            zs[r, 0, 0] = copy(lambda: ZS.at[r, 0, 0, h0], lambda: ZR.at[r, 0, 0, h0], ZP, None, ring(r, 0, 0))
            zs[r, 1, 0] = copy(lambda: ZS.at[r, 0, 0, h1], lambda: ZR.at[r, 1, 0, h1], ZM, None, ring(r, 1, 0))
            return
        for q in range(2):
            zs[r, q, k - 1].wait_recv()
        for q in range(2):
            v = val(r, zz((4 - k) if q == 0 else (k - 4)))
            if k == 1:
                h = slice(0, ROWS) if q == 0 else slice(ROWS, 2 * ROWS)
                g = slice(ROWS, 2 * ROWS) if q == 0 else slice(0, ROWS)
                ZS[r, q, k, h] = (v[h] + ZR[r, q, 0, h].astype(F32)).astype(BF)
                ZS[r, q, k, g] = v[g].astype(BF)
            else:
                ZS[r, q, k] = (v + ZR[r, q, k - 1].astype(F32)).astype(BF)
            at = functools.partial(lambda ref, q: ref.at[r, q, k], q=q)
            to = ZP if q == 0 else ZM
            zs[r, q, k] = copy(functools.partial(at, ZS), functools.partial(at, ZR), to, None, ring(r, q, k))

    sw = {}

    def rows_of(r, h):
        return slice(192 * h + ROWS * r, 192 * h + ROWS * (r + 1))

    def output(r):
        zs[r, 0, 3].wait_recv()
        zs[r, 1, 3].wait_recv()
        m = val(r, z) + ZR[r, 0, 3].astype(F32) + ZR[r, 1, 3].astype(F32)
        for h in range(2):
            w = rows_of(r, h)
            o = (TOKT[w] + GATE[w] * m[ROWS * h:ROWS * (h + 1)]).astype(BF)
            OTA[r, h] = o
            TOKT[w] = o.astype(F32)

        sw[r] = copy(lambda: OTA.at[r], lambda: OTB.at[r], S)

    ag, fw = {}, {}
    for r in range(R):
        fw[r] = used[0]
        used[0] += 1

    def gslice(r, img, b, h):
        n = ROWS if h is not None else 2 * ROWS
        return GT.at[r, img, pl.ds(pl.multiple_of(b * 2 * ROWS + (h or 0) * ROWS, 16), n)]

    def astage(r, k):
        def push(kk, dev, h=None, at=None):
            return copy_same(lambda: gslice(r, c, zz(kk), h), dev, None, fw[r] if at is None else at)

        if k == 0:
            sw[r].wait_recv()
            total = counts_ref[0]
            for i in range(1, 16):
                total = total + counts_ref[i]
            norm = jnp.sqrt(jnp.full((1, SEQ), total, jnp.int32).astype(F32))
            at = lax.broadcasted_iota(jnp.int32, (1, SEQ), 1)
            vrow = jnp.where(at < counts_ref[dp], (2 * s - 1).astype(F32), 0.0) / norm
            for h in range(2):
                w = rows_of(r, h)
                diff = OTA[r, h].astype(F32) - OTB[r, h].astype(F32)
                rows = pl.ds(pl.multiple_of(z * 2 * ROWS + h * ROWS, 16), ROWS)
                GT[r, c, rows] = (GATEG[w] * diff * vrow).astype(BF)
            ag[r, 0, 0] = push(0, ZP, at=ring(r, 0, 4))
            ag[r, 1, 0] = push(0, ZM, at=ring(r, 1, 4))
            push(0, C)
            return
        ag[r, 0, k - 1].wait_recv()
        ag[r, 1, k - 1].wait_recv()
        if k < 4:
            ag[r, 0, k] = push(-k, ZP, 0 if k > 2 else None, ring(r, 0, 4 + k))
        push(-k, C, None if k < 4 else 0)
        if k < 4:
            ag[r, 1, k] = push(k, ZM, 1 if k > 2 else None, ring(r, 1, 4 + k))
        push(k, C, None if k < 4 else 1)

    class Reduce:
        def __init__(self, i):
            self.i, self.a, self.b = i, slice(0, RA[i]), slice(RA[i], ROWS)
            self.ra, self.rb = pl.ds(0, RA[i]), pl.ds(0, ROWS - RA[i])
            self.r = lax.rem(i + 2 * (1 - s), R)

        def both(self, src, dst):
            at = used[0]
            used[0] += 1
            for h in range(2):
                copy(lambda: src().at[h], lambda: dst().at[h], (YP, YM)[h], None, at)
            return Whole(at, dst)

        def q(self, j, rows):
            return QV[self.r, j, :, rows]

        def r0(self):
            i, ra, rb = self.i, self.ra, self.rb
            for h in range(2):
                for x in range(2):
                    A2S[i, h, x, ra] = QV[self.r, jj(x, y2), h, self.a].astype(BF)
            self.a2 = self.both(lambda: A2S.at[i, :, :, ra], lambda: A2R.at[i, :, :, ra])
            for k in range(4):
                XBS[i, k, :, rb] = self.q(jj(xo, k), self.b).astype(BF)
            self.xb = copy(lambda: XBS.at[i, :, :, rb], lambda: XBR.at[i, :, :, rb], X)

        def r1(self):
            i, ra = self.i, self.ra
            self.a2.wait_recv()
            for h in range(2):
                for x in range(2):
                    v = self.q(jj(x, (yp, ym)[h]), self.a)
                    A1S[i, h, x, h, ra] = (v[h] + A2R[i, h, x, ra].astype(F32)).astype(BF)
                    A1S[i, h, x, 1 - h, ra] = v[1 - h].astype(BF)
            self.a1 = self.both(lambda: A1S.at[i, :, :, :, ra], lambda: A1R.at[i, :, :, :, ra])

        def r2(self):
            i, rb = self.i, self.rb
            self.xb.wait_recv()
            v = self.q(jj(xl, y2), self.b) + XBR[i, y2, :, rb].astype(F32)
            B2S[i, :, rb] = v.astype(BF)
            self.b2 = self.both(lambda: B2S.at[i, :, rb], lambda: B2R.at[i, :, rb])

        def r3(self):
            i, rb = self.i, self.rb
            self.b2.wait_recv()
            for h in range(2):
                yy = (yp, ym)[h]
                v = self.q(jj(xl, yy), self.b) + XBR[i, yy, :, rb].astype(F32)
                B1S[i, h, h, rb] = (v[h] + B2R[i, h, rb].astype(F32)).astype(BF)
                B1S[i, h, 1 - h, rb] = v[1 - h].astype(BF)
            self.b1 = self.both(lambda: B1S.at[i, :, :, rb], lambda: B1R.at[i, :, :, rb])

        def r4(self):
            i, ra = self.i, self.ra
            self.a1.wait_recv()
            v = self.q(jj(xo, y), self.a) + A1R[i, 0, xo, :, ra].astype(F32) + A1R[i, 1, xo, :, ra].astype(F32)
            AXS[i, :, ra] = v.astype(BF)
            self.ax = copy(lambda: AXS.at[i, :, ra], lambda: AXR.at[i, :, ra], X)

        def r5(self):
            i, ra, rb = self.i, self.ra, self.rb
            va = self.q(own, self.a) + A1R[i, 0, xl, :, ra].astype(F32) + A1R[i, 1, xl, :, ra].astype(F32)
            vb = self.q(own, self.b) + XBR[i, y, :, rb].astype(F32)
            self.b1.wait_recv()
            vb = vb + B1R[i, 0, :, rb].astype(F32) + B1R[i, 1, :, rb].astype(F32)
            self.ax.wait_recv()
            FO[i, :, self.a] = va + AXR[i, :, ra].astype(F32)
            FO[i, :, self.b] = vb
            FS[i] = FO[i, oc].astype(BF)
            self.f = copy(lambda: FS.at[i], lambda: FR.at[i], C)

        def r6(self):
            i = self.i
            self.f.wait_recv()
            if i < R // 2:
                HS[i, c] = FO[i, c].astype(BF)
                HS[i, oc] = FR[i]
                self.h = copy(lambda: HS.at[i], lambda: HR.at[i], S)
                return
            FO[i, oc] = FR[i].astype(F32)
            rows = slice(ROWS * (i - R // 2), ROWS * (i - R // 2 + 1))

            def keep(o):
                for h in range(2):
                    o[rows, BLK * h:BLK * (h + 1)] = FO[i, h]

            pl.when(student)(lambda: keep(ug_ref))
            pl.when(s == 0)(lambda: keep(dg_ref))

        def r7(self):
            i = self.i
            self.h.wait_recv()
            rows = slice(ROWS * i, ROWS * (i + 1))

            def keep(o):
                for h in range(2):
                    o[rows, BLK * h:BLK * (h + 1)] = HR[i, h].astype(F32)

            pl.when(student)(lambda: keep(dg_ref))
            pl.when(s == 0)(lambda: keep(ug_ref))

    red = [Reduce(i) for i in range(R)]

    def down_grads(r):
        g = [GT[r, 0], GT[r, 1]]
        q = nn(g[0], ACTG[0]) + nn(g[1], ACTG[1])
        QV[r] = q.reshape(NZ, 2, ROWS, BLK)

    def grad_act(r, first):
        w = D[r].reshape(NZ * 2 * ROWS, BLK)
        for img in range(2):
            v = tn(GT[r, img], w)
            if first:
                GA[img] = v
            else:
                GA[img] += v

    def arrived(r):
        wait_bytes(fw[r], GT.at[r, 0])

    def transposed(part):
        def one(i, carry):
            img, j = lax.div(i, 8), lax.rem(i, 8)
            t = jnp.transpose(N[img, j].astype(F32)).astype(BF)
            for r in range(R):
                for h in range(2):
                    NTR[r, img, pl.ds(pl.multiple_of(j * 2 * ROWS + h * ROWS, 16), ROWS)] = t[rows_of(r, h)]
            return carry

        lax.fori_loop(4 * part, 4 * part + 4, one, 0)

    def up_grads(r):
        q = nn(NTR[r, 0], GP[0]) + nn(NTR[r, 1], GP[1])
        QV[r] = q.reshape(NZ, 2, ROWS, BLK)

    summed = []

    def stage(n, k):
        if k < 4:
            zstage(n, k)
        elif k == 4:
            output(n)
        elif k < 10:
            astage(n, k - 5)
        else:
            arrived(n)
            first = not summed
            summed.append(n)
            pl.when(student)(lambda: grad_act(n, first))

            @pl.when(s == 0)
            def _():
                if first:
                    for d in act_out:
                        d.wait_recv()
                down_grads(n)

    def begin(n):
        if not begun:
            @pl.when(student)
            def _():
                for img in range(2):
                    GP[img] = (GA[img] * SL[img]).astype(BF)

        begun.append(n)
        pl.when(student)(lambda: up_grads(n))
        red[n].r0()

    u_in.wait()
    out_put = pltpu.make_async_copy(out_ref, out_to, local.at[6])
    begun, mixed_of, swapped, put = [], [], [], []
    gu.g5()
    for what, n in ORDER:
        if what == "hc":
            hidden(c)
        elif what == "ho":
            wait_bytes(n_sem, N.at[oc])
            hidden(oc)
        elif what[0] == "g":
            getattr(gd[n], what)()
        elif what == "m":
            mixed(n)
            mixed_of.append(n)
            if len(mixed_of) == R:
                send_act(lambda: c)
                send_act(lambda: oc)
        elif what == "tr":
            pl.when(student)(functools.partial(transposed, n))
        elif what == "sl":
            pl.when(student)(functools.partial(slopes, n))
        elif what[0] == "s":
            k = int(what[1:])
            if k == 5:
                if not swapped:
                    gate_of_student()
                swapped.append(n)
            stage(n, k)
            if k == 4:
                put.append(n)
                if len(put) == R:
                    out_ref[...] = jnp.transpose(TOKT[...]).astype(BF)
                    out_put.start()
        elif what == "b":
            begin(n)
        else:
            getattr(red[n], what)()

    out_put.wait()
    for d in started[None][-N_SEND[None]:]:
        d.wait_send()

    @pl.when(student)
    def _():
        for d in started[1][-N_SEND[1]:]:
            d.wait_send()


def shards(axes, tokens, up_weight, down_weight, mod_table, timesteps, valid_counts):
    table = mod_table.reshape(mod_table.shape[1], -1, 128)
    downt = down_weight[0].T.reshape(R, ROWS, 2 * BLK)

    v = pltpu.VMEM
    nred = R
    scratch = [
        v((SEQ, BLK), BF),
        v((NZ, SEQ, BLK), BF),
        v((NZ, 8, SEQ), F32),
        v((SEQ, 128), F32),
        v((SEQ, 128), F32),
        v((NZ, 2, 192, BLK), BF),
        v((R, NZ, 2, ROWS, BLK), BF),
        v((2, NZ, SEQ, BLK), BF),
        v((R, 2, NZ * 2 * ROWS, SEQ), BF),
        v((2, SEQ, BLK), F32),
        v((2, SEQ, BLK), F32),
        v((2, SEQ, BLK), BF),
        v((2, SEQ, BLK), BF),
        v((R, NZ * 2 * ROWS, SEQ), F32),
        v((R, NZ * 2 * ROWS, SEQ), BF),
        v((R, NZ * 2 * ROWS, SEQ), BF),
        v((R, 2, 4, 2 * ROWS, SEQ), BF),
        v((R, 2, 4, 2 * ROWS, SEQ), BF),
        v(table.shape, F32),
        pltpu.SMEM(timesteps.shape, jnp.int32),
        pltpu.SMEM(valid_counts.shape, jnp.int32),
        v((3, NZ * BLK), F32),
        v((3, NZ * BLK), F32),
        v((BLK, SEQ), F32),
        v((BLK, SEQ), F32),
        v((BLK, SEQ), F32),
        v((R, 2, ROWS, SEQ), BF),
        v((R, 2, ROWS, SEQ), BF),
        v((R, 2, NZ * 2 * ROWS, SEQ), BF),
        v((2, SEQ, BLK), F32),
        v((2, SEQ, BLK), BF),
        v((nred, NZ, 2, ROWS, BLK), F32),
        v((nred, 4, 2, 32, BLK), BF),
        v((nred, 4, 2, 32, BLK), BF),
        v((nred, 2, 2, 32, BLK), BF),
        v((nred, 2, 2, 32, BLK), BF),
        v((nred, 2, 2, 2, 32, BLK), BF),
        v((nred, 2, 2, 2, 32, BLK), BF),
        v((nred, 2, 32, BLK), BF),
        v((nred, 2, 32, BLK), BF),
        v((nred, 2, 2, 32, BLK), BF),
        v((nred, 2, 2, 32, BLK), BF),
        v((nred, 2, 32, BLK), BF),
        v((nred, 2, 32, BLK), BF),
        v((nred, ROWS, BLK), BF),
        v((nred, 2, ROWS, BLK), F32),
        v((nred, ROWS, BLK), BF),
        v((nred, 2, ROWS, BLK), BF),
        v((nred, 2, ROWS, BLK), BF),
        pltpu.SemaphoreType.DMA((sum(N_SEND.values()),)),
        pltpu.SemaphoreType.DMA((N_RECV,)),
        pltpu.SemaphoreType.DMA((7,)),
    ]
    hbm = pl.BlockSpec(memory_space=pl.ANY)
    vm = pl.BlockSpec(memory_space=pltpu.VMEM)
    out, up, down = pl.pallas_call(
        functools.partial(kernel, axes),
        out_shape=(
            jax.ShapeDtypeStruct((SEQ, BLK), BF),
            jax.ShapeDtypeStruct((96, 2 * BLK), F32),
            jax.ShapeDtypeStruct((96, 2 * BLK), F32),
        ),
        in_specs=[hbm] * 6,
        out_specs=(hbm, vm, vm),
        scratch_shapes=scratch,
        compiler_params=pltpu.CompilerParams(
            collective_id=0, has_side_effects=True, vmem_limit_bytes=67043328
        ),
    )(tokens, up_weight[0], downt, table, timesteps, valid_counts)
    def settle(*refs):
        came, sems = refs[6:9], refs[9]
        into = [pltpu.make_async_copy(refs[i], came[i], sems.at[i]) for i in range(3)]
        outof = [pltpu.make_async_copy(came[i], refs[3 + i], sems.at[3 + i]) for i in range(3)]
        for d in into:
            d.start()
        for d, e in zip(into, outof):
            d.wait()
            e.start()
        for e in outof:
            e.wait()

    shapes = [((SEQ, BLK), BF), ((96, 2 * BLK), F32), ((96, 2 * BLK), F32)]
    out, up, down = pl.pallas_call(
        settle,
        out_shape=tuple(jax.ShapeDtypeStruct(*i) for i in shapes),
        in_specs=[hbm] * 3,
        out_specs=(hbm,) * 3,
        scratch_shapes=[v(*i) for i in shapes] + [pltpu.SemaphoreType.DMA((6,))],
        compiler_params=pltpu.CompilerParams(vmem_limit_bytes=67043328),
    )(out, up, down)
    return out[None], up, down.T


def solution(mesh):
    placed = (
        P("dp", "mp"),
        P("side", "dp", "mp"),
        P("side", "mp", "dp"),
        P("side", None, None, None),
        P("dp"),
        P(),
    )
    return jax.shard_map(
        functools.partial(shards, mesh.axis_names),
        mesh=mesh,
        in_specs=placed,
        out_specs=(P("side", "dp", "mp"), P(("dp", "side"), "mp"), P("mp", ("dp", "side"))),
        check_vma=False,
    )
```

```python
import functools

import jax
import jax.numpy as jnp
from jax import lax
from jax.experimental import pallas as pl
from jax.experimental.pallas import tpu as pltpu
from jax.sharding import PartitionSpec as P

BF = jnp.bfloat16
F32 = jnp.float32
R = 4
ROWS = 192 // R
RA = (32, 32, 32, 16)
RU = 112
ORDER = (
    ("g2", 3), ("g1", 3), ("g0", 2), ("hc", 0), ("ho", 0), ("g1", 0), ("g4", 3), ("g2", 0), ("g3", 3), ("g1", 1),
    ("g2", 1), ("g2", 2), ("g1", 2), ("g3", 0), ("g4", 0), ("g5", 3), ("m", 3), ("g3", 1), ("g4", 1), ("g4", 2),
    ("s0", 3), ("g3", 2), ("g5", 0), ("m", 0), ("g5", 1), ("m", 1), ("s1", 3), ("g5", 2), ("m", 2), ("s0", 0),
    ("s0", 1), ("s0", 2), ("s2", 3), ("s1", 0), ("s1", 1), ("s1", 2), ("s3", 3), ("s2", 0), ("s2", 1), ("s2", 2),
    ("s4", 3), ("s3", 0), ("s3", 1), ("s3", 2), ("s4", 0), ("s5", 3), ("s4", 1), ("s4", 2), ("s6", 3), ("sl", 0),
    ("s5", 0), ("s5", 1), ("s5", 2), ("s7", 3), ("s6", 0), ("sl", 1), ("s6", 1), ("s6", 2), ("s8", 3), ("tr", 0),
    ("s7", 0), ("s7", 1), ("s7", 2), ("s9", 3), ("s8", 0), ("tr", 1), ("s10", 3), ("s8", 1), ("tr", 2), ("s8", 2),
    ("tr", 3), ("s9", 0), ("s9", 1), ("s10", 0), ("s9", 2), ("s10", 1), ("s10", 2), ("b", 1), ("b", 0), ("b", 2),
    ("b", 3), ("r1", 1), ("r2", 1), ("r1", 0), ("r2", 0), ("r1", 2), ("r4", 1), ("r2", 2), ("r3", 1), ("r3", 0),
    ("r4", 0), ("r1", 3), ("r2", 3), ("r4", 2), ("r3", 2), ("r5", 1), ("r5", 0), ("r6", 1), ("r4", 3), ("r3", 3),
    ("r6", 0), ("r5", 2), ("r6", 2), ("r5", 3), ("r7", 1), ("r6", 3), ("r7", 0),
)
NZ = 8
SEQ = 256
BLK = 384
N_RECV = 121
N_SEND = {None: 40, 1: 2}


K = 0.7978845608028654


def gelu(v):
    return v * (0.5 * (1.0 + jnp.tanh(K * v * (1.0 + 0.044715 * (v * v)))))


def gelu_slope(v):
    v2 = v * v
    t = jnp.tanh(K * v * (1.0 + 0.044715 * v2))
    return 0.5 * (1.0 + t) + 0.5 * v * (1.0 - t * t) * (K * (1.0 + 3.0 * 0.044715 * v2))


def nn(a, b):
    return lax.dot_general(a, b, (((1,), (0,)), ((), ())), preferred_element_type=F32)


def nt(a, b):
    return lax.dot_general(a, b, (((1,), (1,)), ((), ())), preferred_element_type=F32)


def tn(a, b):
    return lax.dot_general(a, b, (((0,), (0,)), ((), ())), preferred_element_type=F32)


def kernel(
    axes,
    tok_ref, up_ref, downt_ref, table_ref, step_in, counts_in,
    out_to, ug_ref, dg_ref,
    out_ref, T, ST, MEAN, RSTD, U, D, N, NTR, HP, SL, ACT, ACTG, PO, PS, PR, ZS, ZR, TAB, step_ref, counts_ref, mod_ref, MODO, GATE, GATEG, TOKT, OTA, OTB, GT, GA, GP,
    QV, XBS, XBR, A2S, A2R, A1S, A1R, B2S, B2R, B1S, B1R, AXS, AXR, FS, FO, FR, HS, HR,
    send, recv, local,
):
    dp, z, s = lax.axis_index("dp"), lax.axis_index("mp"), lax.axis_index("side")
    c = lax.rem(dp, 2)
    y = lax.rem(lax.div(dp, 2), 4)
    xl = lax.div(dp, 8)
    xo = 1 - xl
    yp, ym, y2 = lax.rem(y + 1, 4), lax.rem(y + 3, 4), lax.rem(y + 2, 4)
    oc = 1 - c

    def zz(k):
        return lax.rem(z + (k + NZ), NZ)

    def where(dp_=None, mp_=None, side_=None):
        at = {"dp": dp if dp_ is None else dp_, "mp": z if mp_ is None else mp_, "side": s if side_ is None else side_}
        return tuple(at[a] for a in axes)

    def jj(a, b):
        return a * 4 + b

    X = where(dp_=xo * 8 + y * 2 + c)
    YP = where(dp_=xl * 8 + yp * 2 + c)
    YM = where(dp_=xl * 8 + ym * 2 + c)
    ZP = where(mp_=zz(1))
    ZM = where(mp_=zz(-1))
    C = where(dp_=dp + 1 - 2 * c)
    S = where(side_=1 - s)

    table_in = pltpu.make_async_copy(table_ref, TAB, local.at[3])
    table_in.start()
    step_copy = pltpu.make_async_copy(step_in, step_ref, local.at[4])
    step_copy.start()
    counts_copy = pltpu.make_async_copy(counts_in, counts_ref, local.at[5])
    counts_copy.start()
    barrier = pltpu.get_barrier_semaphore()
    peers = (X, YP, YM, ZP, ZM, C, S)
    for peer in peers:
        pl.semaphore_signal(barrier, inc=1, device_id=peer, device_id_type=pl.DeviceIdType.MESH)
    pl.semaphore_wait(barrier, len(peers))

    used = [0]
    started = {None: [], 1: []}

    class Copy:
        def __init__(self, refs, dev, side, at=None):
            self.refs, self.dev = refs, dev
            if at is None:
                at = used[0]
                used[0] += 1
            self.i = at
            mine = started[side]
            pool = N_SEND[side]
            self.j = len(mine) % pool + {None: 0, 1: N_SEND[None]}[side]
            if len(mine) >= pool:
                mine[-pool].wait_send()
            self.made().start()
            mine.append(self)

        def made(self):
            src, dst = self.refs()
            return pltpu.make_async_remote_copy(
                src_ref=src, dst_ref=dst, send_sem=send.at[self.j], recv_sem=recv.at[self.i],
                device_id=self.dev, device_id_type=pl.DeviceIdType.MESH,
            )

        def wait_recv(self):
            self.made().wait_recv()

        def wait_send(self):
            self.made().wait_send()

    def copy(src, dst, dev, side=None, at=None):
        return Copy(lambda: (src(), dst()), dev, side, at)

    def copy_same(ref, dev, side=None, at=None):
        return Copy(lambda: (ref(),) * 2, dev, side, at)

    def wait_bytes(i, ref):
        pltpu.make_async_copy(ref, ref, recv.at[i]).wait()

    student = s == 1

    class Whole:
        def __init__(self, i, ref):
            self.wait_recv = lambda: wait_bytes(i, ref())

    class Gather:
        def __init__(self, buf, ra, two, four):
            self.buf, self.ra, self.two, self.four = buf, ra, two, four

        def g0(self):
            self.bx = used[0]
            used[0] += 1
            self.xa = copy_same(lambda: self.apart(xl, y), X)
            self.yp = copy_same(lambda: self.buf(own), YP)
            self.ym = copy_same(lambda: self.buf(own), YM)
            self.xb = copy_same(lambda: self.bpart(xl, y), X, at=self.bx)

        def direct(self, mine):
            if mine:
                self.xi, self.yi, self.wi, self.bx = range(used[0], used[0] + 4)
                used[0] += 4
            h, ra = (c if mine else oc), self.ra
            cols = pl.ds(pl.multiple_of(c * BLK, 128), BLK)

            def send(dev, rows, at):
                copy(
                    lambda: up_ref.at[rows, cols] if mine else self.buf(own).at[h, rows],
                    lambda: self.buf(own).at[h, rows], dev, None, at,
                )

            send(X, pl.ds(0, ra), self.xi)
            send(YP, pl.ds(0, 192), self.yi)
            send(YM, pl.ds(0, 192), self.wi)
            send(X, pl.ds(ra, 192 - ra), self.bx)
            self.xa = Whole(self.xi, lambda: self.apart(xo, y))
            self.yp = Whole(self.yi, lambda: self.buf(jj(xl, ym)))
            self.ym = Whole(self.wi, lambda: self.buf(jj(xl, yp)))

        def g1(self):
            self.xa.wait_recv()
            self.xap = copy_same(lambda: self.apart(xo, y), YP)
            self.xam = copy_same(lambda: self.apart(xo, y), YM)

        def apart(self, xx, yy):
            return self.buf(jj(xx, yy)).at[:, pl.ds(0, self.ra)]

        def bpart(self, xx, yy):
            b = self.buf(jj(xx, yy))
            return b.at[:, pl.ds(self.ra, b.shape[1] - self.ra)]

        def g2(self):
            self.yp.wait_recv()
            late = self.late = used[0]
            used[0] += 1
            self.rp = copy_same(lambda: self.bpart(xl, ym).at[0], YP)
            self.bxm = copy_same(lambda: self.bpart(xl, ym), X, at=self.bx)
            copy_same(lambda: self.apart(xl, ym).at[0], YP, None, late)
            self.ym.wait_recv()
            self.rm = copy_same(lambda: self.bpart(xl, yp).at[1], YM)
            self.bxp = copy_same(lambda: self.bpart(xl, yp), X, at=self.bx)
            copy_same(lambda: self.apart(xl, yp).at[1], YM, None, late)

        def g3(self):
            self.xap.wait_recv()
            copy_same(lambda: self.buf(jj(xo, ym)).at[0, pl.ds(0, self.ra)], YP, None, self.late)
            self.xam.wait_recv()
            copy_same(lambda: self.buf(jj(xo, yp)).at[1, pl.ds(0, self.ra)], YM, None, self.late)

        def g4(self):
            self.rp.wait_recv()
            self.rm.wait_recv()
            self.bx2 = copy_same(lambda: self.bpart(xl, y2), X, at=self.bx)

        def g5(self):
            wait_bytes(self.late, self.two())
            wait_bytes(self.bx, self.four())

    own = jj(xl, y)
    u_out = copy(lambda: up_ref.at[:, pl.ds(pl.multiple_of(oc * BLK, 128), BLK)], lambda: U.at[own, c], C)
    gu = Gather(lambda j: U.at[j], RU, lambda: U.at[0:2, :, 0:RU], lambda: U.at[0:4, :, RU:192])
    gu.direct(True)
    tok_in = pltpu.make_async_copy(tok_ref, T.at[z], local.at[0])
    tok_in.start()
    u_in = pltpu.make_async_copy(up_ref.at[:, pl.ds(pl.multiple_of(c * BLK, 128), BLK)], U.at[own, c], local.at[1])
    u_in.start()
    d_in = pltpu.make_async_copy(
        downt_ref.at[:, :, pl.ds(pl.multiple_of(c * BLK, 128), BLK)], D.at[:, own, c], local.at[2]
    )
    d_in.start()

    tk = {}
    t_sems = used[0]
    used[0] += 12

    def tok(hop, p):
        rows = pl.ds(128 * p, 128)
        for q in range(2):
            if (q, hop - 1, p) in tk:
                tk[q, hop - 1, p].wait_recv()
        for q, sign, dev in ((0, -1, ZP), (1, 1, ZM)):
            if hop < 3 or hop == 3 and p == q:
                at = functools.partial(lambda k, rows: tok_ref.at[rows] if k is None else T.at[zz(k), rows], rows=rows)
                src = functools.partial(at, None if hop == 0 else sign * hop)
                tk[q, hop, p] = copy(src, functools.partial(at, sign * hop), dev, None, t_sems + 4 * p + 2 * q + hop % 2)

    st = {}

    def stats(hop):
        for q in range(2):
            if (q, hop - 1) in st:
                st[q, hop - 1].wait_recv()
        for q, sign, dev in ((0, -1, ZP), (1, 1, ZM)):
            if hop < 3 or hop == 3 and q == 0:
                st[q, hop] = copy_same(
                    functools.partial(lambda k: ST.at[zz(k)], sign * hop), dev, None, t_sems + 8 + 2 * q + hop % 2
                )

    def own_stats():
        x = T[z].astype(F32)
        m = jnp.sum(x, axis=-1, keepdims=True) * (1.0 / BLK)
        x = x - m
        sq = jnp.sum(x * x, axis=-1, keepdims=True)
        lane = lax.broadcasted_iota(jnp.int32, (SEQ, 128), 1)
        ST[z] = jnp.transpose(jnp.where(lane == 0, m, sq))[0:8]

    def all_stats():
        ms = [ST[b, 0:1] for b in range(NZ)]
        mean = ms[0]
        sq = ST[0, 1:2]
        for b in range(1, NZ):
            mean = mean + ms[b]
            sq = sq + ST[b, 1:2]
        mean = mean * (1.0 / NZ)
        apart = (ms[0] - mean) * (ms[0] - mean)
        for b in range(1, NZ):
            apart = apart + (ms[b] - mean) * (ms[b] - mean)
        rs = lax.rsqrt((sq + BLK * apart) * (1.0 / (NZ * BLK)) + 1e-06)
        MEAN[...] = jnp.transpose(jnp.broadcast_to(mean, (128, SEQ)))
        RSTD[...] = jnp.transpose(jnp.broadcast_to(rs, (128, SEQ)))

    n_sem = used[0]
    used[0] += 1

    def norm(k, p):
        b = zz(k)
        at = pl.ds(pl.multiple_of(b * BLK, 128), BLK)
        scale, shift = 1.0 + mod_ref[1:2, at], mod_ref[0:1, at]

        def tile(i, carry):
            rows = pl.ds(pl.multiple_of(128 * p + i * 32, 32), 32)
            m, rs = MEAN[rows], RSTD[rows]
            m, rs = jnp.concatenate([m] * 3, axis=1), jnp.concatenate([rs] * 3, axis=1)
            N[c, b, rows] = ((T[b, rows].astype(F32) - m) * rs * scale + shift).astype(BF)
            return carry

        lax.fori_loop(0, 4, tile, 0)
        copy_same(lambda: N.at[c, zz(k), pl.ds(128 * p, 128)], C, at=n_sem)

    gd = [
        Gather(
            functools.partial(lambda r, j: D.at[r, j], r), RA[r],
            functools.partial(lambda r: D.at[r, 0:2, :, 0:RA[r]], r),
            functools.partial(lambda r: D.at[r, 0:4, :, RA[r]:ROWS], r),
        )
        for r in range(R)
    ]

    tok(0, 0)
    u_out.wait_recv()
    gu.direct(False)
    tok_in.wait()
    own_stats()
    stats(0)
    tok(0, 1)
    d_out = copy(lambda: downt_ref.at[:, :, pl.ds(pl.multiple_of(oc * BLK, 128), BLK)], lambda: D.at[:, own, c], C)
    table_in.wait()
    step_copy.wait()
    counts_copy.wait()
    n = 3 * NZ * BLK // 128
    plan = TAB[step_ref[0]]
    for i in range(n):
        k, at = divmod(128 * i, NZ * BLK)
        mod_ref[k:k + 1, at:at + 128] = plan[i:i + 1]
    mod_out = copy(lambda: mod_ref, lambda: MODO, S)
    gate = mod_ref[2:3, pl.ds(pl.multiple_of(z * BLK, 128), BLK)]
    gate = jnp.transpose(jnp.broadcast_to(gate, (128, BLK)))
    GATE[:, 0:128] = gate
    GATE[:, 128:256] = gate

    def gate_of_student():
        mod_out.wait_recv()
        at = pl.ds(pl.multiple_of(z * BLK, 128), BLK)
        g = jnp.where(jnp.full((1, BLK), s) == 1, mod_ref[2:3, at], MODO[2:3, at])
        g = jnp.transpose(jnp.broadcast_to(g, (128, BLK)))
        GATEG[:, 0:128] = g
        GATEG[:, 128:256] = g

    tt = jnp.transpose(T[z].astype(F32))
    TOKT[...] = tt
    stats(1)
    tok(1, 0)
    gu.g1()
    tok(1, 1)
    stats(2)
    gu.g2()
    tok(2, 0)
    stats(3)
    tok(2, 1)
    d_in.wait()
    d_out.wait_recv()
    gu.g3()
    gd[3].g0()
    st[0, 3].wait_recv()
    all_stats()
    for k in (0, -1, 1):
        for p in range(2):
            norm(k, p)
    gu.g4()
    gd[1].g0()
    tok(3, 0)
    norm(-2, 0)
    norm(2, 0)
    tok(3, 1)
    norm(-2, 1)
    norm(2, 1)
    gd[0].g0()
    for k in (-3, 3):
        for p in range(2):
            norm(k, p)
    tok(4, 0)
    norm(4, 0)
    tok(4, 1)
    norm(4, 1)

    def hidden(img):
        h = nn(N[img, 0], U[0].reshape(BLK, BLK))
        for b in range(1, NZ):
            h = h + nn(N[img, b], U[b].reshape(BLK, BLK))
        HP[img] = h

        def act_rows(i, carry):
            rows = pl.ds(pl.multiple_of(i * 32, 32), 32)
            ACT[img, rows] = gelu(HP[img, rows]).astype(BF)
            return carry

        lax.fori_loop(0, SEQ // 32, act_rows, 0)

    def slopes(img):
        def rows_of_slope(i, carry):
            rows = pl.ds(pl.multiple_of(i * 32, 32), 32)
            SL[img, rows] = gelu_slope(HP[img, rows])
            return carry

        lax.fori_loop(0, SEQ // 32, rows_of_slope, 0)

    act_out = []

    def send_act(img):
        @pl.when(student)
        def _():
            act_out.append(copy(lambda: ACT.at[img()], lambda: ACTG.at[img()], S, 1))

    m_out, zs = {}, {}
    z_sems = used[0]
    used[0] += 4 * R

    def ring(r, q, k):
        return z_sems + 4 * r + 2 * q + k % 2


    def mixed(r):
        w = D[r].reshape(NZ * 2 * ROWS, BLK)
        PS[r] = nt(w, ACT[oc]).astype(BF)
        m_out[r] = copy(lambda: PS.at[r], lambda: PR.at[r], C)
        PO[r] = nt(w, ACT[c])

    def val(r, b):
        rows = pl.ds(pl.multiple_of(b * 2 * ROWS, 32), 2 * ROWS)
        return PO[r, rows] + PR[r, rows].astype(F32)

    def zstage(r, k):
        h0, h1 = pl.ds(0, ROWS), pl.ds(ROWS, ROWS)
        if k == 0:
            m_out[r].wait_recv()
            v = val(r, zz(4)).astype(BF)
            ZS[r, 0, 0] = v
            zs[r, 0, 0] = copy(lambda: ZS.at[r, 0, 0, h0], lambda: ZR.at[r, 0, 0, h0], ZP, None, ring(r, 0, 0))
            zs[r, 1, 0] = copy(lambda: ZS.at[r, 0, 0, h1], lambda: ZR.at[r, 1, 0, h1], ZM, None, ring(r, 1, 0))
            return
        for q in range(2):
            zs[r, q, k - 1].wait_recv()
        for q in range(2):
            v = val(r, zz((4 - k) if q == 0 else (k - 4)))
            if k == 1:
                h = slice(0, ROWS) if q == 0 else slice(ROWS, 2 * ROWS)
                g = slice(ROWS, 2 * ROWS) if q == 0 else slice(0, ROWS)
                ZS[r, q, k, h] = (v[h] + ZR[r, q, 0, h].astype(F32)).astype(BF)
                ZS[r, q, k, g] = v[g].astype(BF)
            else:
                ZS[r, q, k] = (v + ZR[r, q, k - 1].astype(F32)).astype(BF)
            at = functools.partial(lambda ref, q: ref.at[r, q, k], q=q)
            to = ZP if q == 0 else ZM
            zs[r, q, k] = copy(functools.partial(at, ZS), functools.partial(at, ZR), to, None, ring(r, q, k))

    sw = {}

    def rows_of(r, h):
        return slice(192 * h + ROWS * r, 192 * h + ROWS * (r + 1))

    def output(r):
        zs[r, 0, 3].wait_recv()
        zs[r, 1, 3].wait_recv()
        m = val(r, z) + ZR[r, 0, 3].astype(F32) + ZR[r, 1, 3].astype(F32)
        for h in range(2):
            w = rows_of(r, h)
            o = (TOKT[w] + GATE[w] * m[ROWS * h:ROWS * (h + 1)]).astype(BF)
            OTA[r, h] = o
            TOKT[w] = o.astype(F32)

        sw[r] = copy(lambda: OTA.at[r], lambda: OTB.at[r], S)

    ag, fw = {}, {}
    for r in range(R):
        fw[r] = used[0]
        used[0] += 1

    def gslice(r, img, b, h):
        n = ROWS if h is not None else 2 * ROWS
        return GT.at[r, img, pl.ds(pl.multiple_of(b * 2 * ROWS + (h or 0) * ROWS, 16), n)]

    def astage(r, k):
        def push(kk, dev, h=None, at=None):
            return copy_same(lambda: gslice(r, c, zz(kk), h), dev, None, fw[r] if at is None else at)

        if k == 0:
            sw[r].wait_recv()
            total = counts_ref[0]
            for i in range(1, 16):
                total = total + counts_ref[i]
            norm = jnp.sqrt(jnp.full((1, SEQ), total, jnp.int32).astype(F32))
            at = lax.broadcasted_iota(jnp.int32, (1, SEQ), 1)
            vrow = jnp.where(at < counts_ref[dp], (2 * s - 1).astype(F32), 0.0) / norm
            for h in range(2):
                w = rows_of(r, h)
                diff = OTA[r, h].astype(F32) - OTB[r, h].astype(F32)
                rows = pl.ds(pl.multiple_of(z * 2 * ROWS + h * ROWS, 16), ROWS)
                GT[r, c, rows] = (GATEG[w] * diff * vrow).astype(BF)
            ag[r, 0, 0] = push(0, ZP, at=ring(r, 0, 4))
            ag[r, 1, 0] = push(0, ZM, at=ring(r, 1, 4))
            push(0, C)
            return
        ag[r, 0, k - 1].wait_recv()
        ag[r, 1, k - 1].wait_recv()
        if k < 4:
            ag[r, 0, k] = push(-k, ZP, 0 if k > 2 else None, ring(r, 0, 4 + k))
        push(-k, C, None if k < 4 else 0)
        if k < 4:
            ag[r, 1, k] = push(k, ZM, 1 if k > 2 else None, ring(r, 1, 4 + k))
        push(k, C, None if k < 4 else 1)

    class Reduce:
        def __init__(self, i):
            self.i, self.a, self.b = i, slice(0, RA[i]), slice(RA[i], ROWS)
            self.ra, self.rb = pl.ds(0, RA[i]), pl.ds(0, ROWS - RA[i])
            self.r = lax.rem(i + 2 * (1 - s), R)

        def both(self, src, dst):
            at = used[0]
            used[0] += 1
            for h in range(2):
                copy(lambda: src().at[h], lambda: dst().at[h], (YP, YM)[h], None, at)
            return Whole(at, dst)

        def q(self, j, rows):
            return QV[self.r, j, :, rows]

        def r0(self):
            i, ra, rb = self.i, self.ra, self.rb
            for h in range(2):
                for x in range(2):
                    A2S[i, h, x, ra] = QV[self.r, jj(x, y2), h, self.a].astype(BF)
            self.a2 = self.both(lambda: A2S.at[i, :, :, ra], lambda: A2R.at[i, :, :, ra])
            for k in range(4):
                XBS[i, k, :, rb] = self.q(jj(xo, k), self.b).astype(BF)
            self.xb = copy(lambda: XBS.at[i, :, :, rb], lambda: XBR.at[i, :, :, rb], X)

        def r1(self):
            i, ra = self.i, self.ra
            self.a2.wait_recv()
            for h in range(2):
                for x in range(2):
                    v = self.q(jj(x, (yp, ym)[h]), self.a)
                    A1S[i, h, x, h, ra] = (v[h] + A2R[i, h, x, ra].astype(F32)).astype(BF)
                    A1S[i, h, x, 1 - h, ra] = v[1 - h].astype(BF)
            self.a1 = self.both(lambda: A1S.at[i, :, :, :, ra], lambda: A1R.at[i, :, :, :, ra])

        def r2(self):
            i, rb = self.i, self.rb
            self.xb.wait_recv()
            v = self.q(jj(xl, y2), self.b) + XBR[i, y2, :, rb].astype(F32)
            B2S[i, :, rb] = v.astype(BF)
            self.b2 = self.both(lambda: B2S.at[i, :, rb], lambda: B2R.at[i, :, rb])

        def r3(self):
            i, rb = self.i, self.rb
            self.b2.wait_recv()
            for h in range(2):
                yy = (yp, ym)[h]
                v = self.q(jj(xl, yy), self.b) + XBR[i, yy, :, rb].astype(F32)
                B1S[i, h, h, rb] = (v[h] + B2R[i, h, rb].astype(F32)).astype(BF)
                B1S[i, h, 1 - h, rb] = v[1 - h].astype(BF)
            self.b1 = self.both(lambda: B1S.at[i, :, :, rb], lambda: B1R.at[i, :, :, rb])

        def r4(self):
            i, ra = self.i, self.ra
            self.a1.wait_recv()
            v = self.q(jj(xo, y), self.a) + A1R[i, 0, xo, :, ra].astype(F32) + A1R[i, 1, xo, :, ra].astype(F32)
            AXS[i, :, ra] = v.astype(BF)
            self.ax = copy(lambda: AXS.at[i, :, ra], lambda: AXR.at[i, :, ra], X)

        def r5(self):
            i, ra, rb = self.i, self.ra, self.rb
            va = self.q(own, self.a) + A1R[i, 0, xl, :, ra].astype(F32) + A1R[i, 1, xl, :, ra].astype(F32)
            vb = self.q(own, self.b) + XBR[i, y, :, rb].astype(F32)
            self.b1.wait_recv()
            vb = vb + B1R[i, 0, :, rb].astype(F32) + B1R[i, 1, :, rb].astype(F32)
            self.ax.wait_recv()
            FO[i, :, self.a] = va + AXR[i, :, ra].astype(F32)
            FO[i, :, self.b] = vb
            FS[i] = FO[i, oc].astype(BF)
            self.f = copy(lambda: FS.at[i], lambda: FR.at[i], C)

        def r6(self):
            i = self.i
            self.f.wait_recv()
            if i < R // 2:
                HS[i, c] = FO[i, c].astype(BF)
                HS[i, oc] = FR[i]
                self.h = copy(lambda: HS.at[i], lambda: HR.at[i], S)
                return
            FO[i, oc] = FR[i].astype(F32)
            rows = slice(ROWS * (i - R // 2), ROWS * (i - R // 2 + 1))

            def keep(o):
                for h in range(2):
                    o[rows, BLK * h:BLK * (h + 1)] = FO[i, h]

            pl.when(student)(lambda: keep(ug_ref))
            pl.when(s == 0)(lambda: keep(dg_ref))

        def r7(self):
            i = self.i
            self.h.wait_recv()
            rows = slice(ROWS * i, ROWS * (i + 1))

            def keep(o):
                for h in range(2):
                    o[rows, BLK * h:BLK * (h + 1)] = HR[i, h].astype(F32)

            pl.when(student)(lambda: keep(dg_ref))
            pl.when(s == 0)(lambda: keep(ug_ref))

    red = [Reduce(i) for i in range(R)]

    def down_grads(r):
        g = [GT[r, 0], GT[r, 1]]
        q = nn(g[0], ACTG[0]) + nn(g[1], ACTG[1])
        QV[r] = q.reshape(NZ, 2, ROWS, BLK)

    def grad_act(r, first):
        w = D[r].reshape(NZ * 2 * ROWS, BLK)
        for img in range(2):
            v = tn(GT[r, img], w)
            if first:
                GA[img] = v
            else:
                GA[img] += v

    def arrived(r):
        wait_bytes(fw[r], GT.at[r, 0])

    def transposed(part):
        def one(i, carry):
            img, j = lax.div(i, 8), lax.rem(i, 8)
            t = jnp.transpose(N[img, j].astype(F32)).astype(BF)
            for r in range(R):
                for h in range(2):
                    NTR[r, img, pl.ds(pl.multiple_of(j * 2 * ROWS + h * ROWS, 16), ROWS)] = t[rows_of(r, h)]
            return carry

        lax.fori_loop(4 * part, 4 * part + 4, one, 0)

    def up_grads(r):
        q = nn(NTR[r, 0], GP[0]) + nn(NTR[r, 1], GP[1])
        QV[r] = q.reshape(NZ, 2, ROWS, BLK)

    summed = []

    def stage(n, k):
        if k < 4:
            zstage(n, k)
        elif k == 4:
            output(n)
        elif k < 10:
            astage(n, k - 5)
        else:
            arrived(n)
            first = not summed
            summed.append(n)
            pl.when(student)(lambda: grad_act(n, first))

            @pl.when(s == 0)
            def _():
                if first:
                    for d in act_out:
                        d.wait_recv()
                down_grads(n)

    def begin(n):
        if not begun:
            @pl.when(student)
            def _():
                for img in range(2):
                    GP[img] = (GA[img] * SL[img]).astype(BF)

        begun.append(n)
        pl.when(student)(lambda: up_grads(n))
        red[n].r0()

    u_in.wait()
    out_put = pltpu.make_async_copy(out_ref, out_to, local.at[6])
    begun, mixed_of, swapped, put = [], [], [], []
    gu.g5()
    for what, n in ORDER:
        if what == "hc":
            hidden(c)
        elif what == "ho":
            wait_bytes(n_sem, N.at[oc])
            hidden(oc)
        elif what[0] == "g":
            getattr(gd[n], what)()
        elif what == "m":
            mixed(n)
            mixed_of.append(n)
            if len(mixed_of) == R:
                send_act(lambda: c)
                send_act(lambda: oc)
        elif what == "tr":
            pl.when(student)(functools.partial(transposed, n))
        elif what == "sl":
            pl.when(student)(functools.partial(slopes, n))
        elif what[0] == "s":
            k = int(what[1:])
            if k == 5:
                if not swapped:
                    gate_of_student()
                swapped.append(n)
            stage(n, k)
            if k == 4:
                put.append(n)
                if len(put) == R:
                    out_ref[...] = jnp.transpose(TOKT[...]).astype(BF)
                    out_put.start()
        elif what == "b":
            begin(n)
        else:
            getattr(red[n], what)()

    out_put.wait()
    for d in started[None][-N_SEND[None]:]:
        d.wait_send()

    @pl.when(student)
    def _():
        for d in started[1][-N_SEND[1]:]:
            d.wait_send()


def shards(axes, tokens, up_weight, down_weight, mod_table, timesteps, valid_counts):
    table = mod_table.reshape(mod_table.shape[1], -1, 128)
    downt = down_weight[0].T.reshape(R, ROWS, 2 * BLK)

    v = pltpu.VMEM
    nred = R
    scratch = [
        v((SEQ, BLK), BF),
        v((NZ, SEQ, BLK), BF),
        v((NZ, 8, SEQ), F32),
        v((SEQ, 128), F32),
        v((SEQ, 128), F32),
        v((NZ, 2, 192, BLK), BF),
        v((R, NZ, 2, ROWS, BLK), BF),
        v((2, NZ, SEQ, BLK), BF),
        v((R, 2, NZ * 2 * ROWS, SEQ), BF),
        v((2, SEQ, BLK), F32),
        v((2, SEQ, BLK), F32),
        v((2, SEQ, BLK), BF),
        v((2, SEQ, BLK), BF),
        v((R, NZ * 2 * ROWS, SEQ), F32),
        v((R, NZ * 2 * ROWS, SEQ), BF),
        v((R, NZ * 2 * ROWS, SEQ), BF),
        v((R, 2, 4, 2 * ROWS, SEQ), BF),
        v((R, 2, 4, 2 * ROWS, SEQ), BF),
        v(table.shape, F32),
        pltpu.SMEM(timesteps.shape, jnp.int32),
        pltpu.SMEM(valid_counts.shape, jnp.int32),
        v((3, NZ * BLK), F32),
        v((3, NZ * BLK), F32),
        v((BLK, SEQ), F32),
        v((BLK, SEQ), F32),
        v((BLK, SEQ), F32),
        v((R, 2, ROWS, SEQ), BF),
        v((R, 2, ROWS, SEQ), BF),
        v((R, 2, NZ * 2 * ROWS, SEQ), BF),
        v((2, SEQ, BLK), F32),
        v((2, SEQ, BLK), BF),
        v((nred, NZ, 2, ROWS, BLK), F32),
        v((nred, 4, 2, 32, BLK), BF),
        v((nred, 4, 2, 32, BLK), BF),
        v((nred, 2, 2, 32, BLK), BF),
        v((nred, 2, 2, 32, BLK), BF),
        v((nred, 2, 2, 2, 32, BLK), BF),
        v((nred, 2, 2, 2, 32, BLK), BF),
        v((nred, 2, 32, BLK), BF),
        v((nred, 2, 32, BLK), BF),
        v((nred, 2, 2, 32, BLK), BF),
        v((nred, 2, 2, 32, BLK), BF),
        v((nred, 2, 32, BLK), BF),
        v((nred, 2, 32, BLK), BF),
        v((nred, ROWS, BLK), BF),
        v((nred, 2, ROWS, BLK), F32),
        v((nred, ROWS, BLK), BF),
        v((nred, 2, ROWS, BLK), BF),
        v((nred, 2, ROWS, BLK), BF),
        pltpu.SemaphoreType.DMA((sum(N_SEND.values()),)),
        pltpu.SemaphoreType.DMA((N_RECV,)),
        pltpu.SemaphoreType.DMA((7,)),
    ]
    hbm = pl.BlockSpec(memory_space=pl.ANY)
    vm = pl.BlockSpec(memory_space=pltpu.VMEM)
    out, up, down = pl.pallas_call(
        functools.partial(kernel, axes),
        out_shape=(
            jax.ShapeDtypeStruct((SEQ, BLK), BF),
            jax.ShapeDtypeStruct((96, 2 * BLK), F32),
            jax.ShapeDtypeStruct((96, 2 * BLK), F32),
        ),
        in_specs=[hbm] * 6,
        out_specs=(hbm, vm, vm),
        scratch_shapes=scratch,
        compiler_params=pltpu.CompilerParams(
            collective_id=0, has_side_effects=True, vmem_limit_bytes=67043328
        ),
    )(tokens, up_weight[0], downt, table, timesteps, valid_counts)
    def settle(*refs):
        came, sems = refs[6:9], refs[9]
        into = [pltpu.make_async_copy(refs[i], came[i], sems.at[i]) for i in range(3)]
        outof = [pltpu.make_async_copy(came[i], refs[3 + i], sems.at[3 + i]) for i in range(3)]
        for d in into:
            d.start()
        for d, e in zip(into, outof):
            d.wait()
            e.start()
        for e in outof:
            e.wait()

    shapes = [((SEQ, BLK), BF), ((96, 2 * BLK), F32), ((96, 2 * BLK), F32)]
    out, up, down = pl.pallas_call(
        settle,
        out_shape=tuple(jax.ShapeDtypeStruct(*i) for i in shapes),
        in_specs=[hbm] * 3,
        out_specs=(hbm,) * 3,
        scratch_shapes=[v(*i) for i in shapes] + [pltpu.SemaphoreType.DMA((6,))],
        compiler_params=pltpu.CompilerParams(vmem_limit_bytes=67043328),
    )(out, up, down)
    return out[None], up, down.T


def solution(mesh):
    placed = (
        P("dp", "mp"),
        P("side", "dp", "mp"),
        P("side", "mp", "dp"),
        P("side", None, None, None),
        P("dp"),
        P(),
    )
    return jax.shard_map(
        functools.partial(shards, mesh.axis_names),
        mesh=mesh,
        in_specs=placed,
        out_specs=(P("side", "dp", "mp"), P(("dp", "side"), "mp"), P("mp", ("dp", "side"))),
        check_vma=False,
    )
```

```python
import functools

import jax
import jax.numpy as jnp
from jax import lax
from jax.experimental import pallas as pl
from jax.experimental.pallas import tpu as pltpu
from jax.sharding import PartitionSpec as P

BF = jnp.bfloat16
F32 = jnp.float32
R = 4
ROWS = 192 // R
RA = (32, 32, 32, 16)
RU = 112
ORDER = (
    ("g2", 3), ("g1", 3), ("g0", 2), ("hc", 0), ("ho", 0), ("g1", 0), ("g4", 3), ("g2", 0), ("g3", 3), ("g1", 1),
    ("g2", 1), ("g2", 2), ("g1", 2), ("g3", 0), ("g4", 0), ("g5", 3), ("m", 3), ("g3", 1), ("g4", 1), ("g4", 2),
    ("s0", 3), ("g3", 2), ("g5", 0), ("m", 0), ("g5", 1), ("m", 1), ("s1", 3), ("g5", 2), ("m", 2), ("s0", 0),
    ("s0", 1), ("s0", 2), ("s2", 3), ("s1", 0), ("s1", 1), ("s1", 2), ("s3", 3), ("s2", 0), ("s2", 1), ("s2", 2),
    ("s4", 3), ("tr", 0), ("s3", 0), ("s3", 1), ("s3", 2), ("s4", 0), ("tr", 1), ("s5", 3), ("s4", 1), ("tr", 2),
    ("s4", 2), ("tr", 3), ("s6", 3), ("sl", 0), ("s5", 0), ("s5", 1), ("s5", 2), ("s7", 3), ("s6", 0), ("sl", 1),
    ("s6", 1), ("s6", 2), ("s8", 3), ("s7", 0), ("s7", 1), ("s7", 2), ("s9", 3), ("s8", 0), ("s10", 3), ("s8", 1),
    ("s8", 2), ("s9", 0), ("s9", 1), ("s10", 0), ("s9", 2), ("s10", 1), ("s10", 2), ("b", 1), ("b", 0), ("b", 2),
    ("b", 3), ("r1", 1), ("r2", 1), ("r1", 0), ("r2", 0), ("r1", 2), ("r4", 1), ("r2", 2), ("r3", 1), ("r3", 0),
    ("r4", 0), ("r1", 3), ("r2", 3), ("r4", 2), ("r3", 2), ("r5", 1), ("r5", 0), ("r6", 1), ("r4", 3), ("r3", 3),
    ("r6", 0), ("r5", 2), ("r6", 2), ("r5", 3), ("r7", 1), ("r6", 3), ("r7", 0),
)
NZ = 8
SEQ = 256
BLK = 384
N_RECV = 121
N_SEND = {None: 40, 1: 2}


K = 0.7978845608028654


def gelu(v):
    return v * (0.5 * (1.0 + jnp.tanh(K * v * (1.0 + 0.044715 * (v * v)))))


def gelu_slope(v):
    v2 = v * v
    t = jnp.tanh(K * v * (1.0 + 0.044715 * v2))
    return 0.5 * (1.0 + t) + 0.5 * v * (1.0 - t * t) * (K * (1.0 + 3.0 * 0.044715 * v2))


def nn(a, b):
    return lax.dot_general(a, b, (((1,), (0,)), ((), ())), preferred_element_type=F32)


def nt(a, b):
    return lax.dot_general(a, b, (((1,), (1,)), ((), ())), preferred_element_type=F32)


def tn(a, b):
    return lax.dot_general(a, b, (((0,), (0,)), ((), ())), preferred_element_type=F32)


def kernel(
    axes,
    tok_ref, up_ref, downt_ref, table_ref, step_in, counts_in,
    out_to, ug_ref, dg_ref,
    out_ref, T, ST, MEAN, RSTD, U, D, N, NTR, HP, SL, ACT, ACTG, PO, PS, PR, ZS, ZR, TAB, step_ref, counts_ref, mod_ref, MODO, GATE, GATEG, TOKT, OTA, OTB, GT, GA, GP,
    QV, XBS, XBR, A2S, A2R, A1S, A1R, B2S, B2R, B1S, B1R, AXS, AXR, FS, FO, FR, HS, HR,
    send, recv, local,
):
    dp, z, s = lax.axis_index("dp"), lax.axis_index("mp"), lax.axis_index("side")
    c = lax.rem(dp, 2)
    y = lax.rem(lax.div(dp, 2), 4)
    xl = lax.div(dp, 8)
    xo = 1 - xl
    yp, ym, y2 = lax.rem(y + 1, 4), lax.rem(y + 3, 4), lax.rem(y + 2, 4)
    oc = 1 - c

    def zz(k):
        return lax.rem(z + (k + NZ), NZ)

    def where(dp_=None, mp_=None, side_=None):
        at = {"dp": dp if dp_ is None else dp_, "mp": z if mp_ is None else mp_, "side": s if side_ is None else side_}
        return tuple(at[a] for a in axes)

    def jj(a, b):
        return a * 4 + b

    X = where(dp_=xo * 8 + y * 2 + c)
    YP = where(dp_=xl * 8 + yp * 2 + c)
    YM = where(dp_=xl * 8 + ym * 2 + c)
    ZP = where(mp_=zz(1))
    ZM = where(mp_=zz(-1))
    C = where(dp_=dp + 1 - 2 * c)
    S = where(side_=1 - s)

    table_in = pltpu.make_async_copy(table_ref, TAB, local.at[3])
    table_in.start()
    step_copy = pltpu.make_async_copy(step_in, step_ref, local.at[4])
    step_copy.start()
    counts_copy = pltpu.make_async_copy(counts_in, counts_ref, local.at[5])
    counts_copy.start()
    barrier = pltpu.get_barrier_semaphore()
    peers = (X, YP, YM, ZP, ZM, C, S)
    for peer in peers:
        pl.semaphore_signal(barrier, inc=1, device_id=peer, device_id_type=pl.DeviceIdType.MESH)
    pl.semaphore_wait(barrier, len(peers))

    used = [0]
    started = {None: [], 1: []}

    class Copy:
        def __init__(self, refs, dev, side, at=None):
            self.refs, self.dev = refs, dev
            if at is None:
                at = used[0]
                used[0] += 1
            self.i = at
            mine = started[side]
            pool = N_SEND[side]
            self.j = len(mine) % pool + {None: 0, 1: N_SEND[None]}[side]
            if len(mine) >= pool:
                mine[-pool].wait_send()
            self.made().start()
            mine.append(self)

        def made(self):
            src, dst = self.refs()
            return pltpu.make_async_remote_copy(
                src_ref=src, dst_ref=dst, send_sem=send.at[self.j], recv_sem=recv.at[self.i],
                device_id=self.dev, device_id_type=pl.DeviceIdType.MESH,
            )

        def wait_recv(self):
            self.made().wait_recv()

        def wait_send(self):
            self.made().wait_send()

    def copy(src, dst, dev, side=None, at=None):
        return Copy(lambda: (src(), dst()), dev, side, at)

    def copy_same(ref, dev, side=None, at=None):
        return Copy(lambda: (ref(),) * 2, dev, side, at)

    def wait_bytes(i, ref):
        pltpu.make_async_copy(ref, ref, recv.at[i]).wait()

    student = s == 1

    class Whole:
        def __init__(self, i, ref):
            self.wait_recv = lambda: wait_bytes(i, ref())

    class Gather:
        def __init__(self, buf, ra, two, four):
            self.buf, self.ra, self.two, self.four = buf, ra, two, four

        def g0(self):
            self.bx = used[0]
            used[0] += 1
            self.xa = copy_same(lambda: self.apart(xl, y), X)
            self.yp = copy_same(lambda: self.buf(own), YP)
            self.ym = copy_same(lambda: self.buf(own), YM)
            self.xb = copy_same(lambda: self.bpart(xl, y), X, at=self.bx)

        def direct(self, mine):
            if mine:
                self.xi, self.yi, self.wi, self.bx = range(used[0], used[0] + 4)
                used[0] += 4
            h, ra = (c if mine else oc), self.ra
            cols = pl.ds(pl.multiple_of(c * BLK, 128), BLK)

            def send(dev, rows, at):
                copy(
                    lambda: up_ref.at[rows, cols] if mine else self.buf(own).at[h, rows],
                    lambda: self.buf(own).at[h, rows], dev, None, at,
                )

            send(X, pl.ds(0, ra), self.xi)
            send(YP, pl.ds(0, 192), self.yi)
            send(YM, pl.ds(0, 192), self.wi)
            send(X, pl.ds(ra, 192 - ra), self.bx)
            self.xa = Whole(self.xi, lambda: self.apart(xo, y))
            self.yp = Whole(self.yi, lambda: self.buf(jj(xl, ym)))
            self.ym = Whole(self.wi, lambda: self.buf(jj(xl, yp)))

        def g1(self):
            self.xa.wait_recv()
            self.xap = copy_same(lambda: self.apart(xo, y), YP)
            self.xam = copy_same(lambda: self.apart(xo, y), YM)

        def apart(self, xx, yy):
            return self.buf(jj(xx, yy)).at[:, pl.ds(0, self.ra)]

        def bpart(self, xx, yy):
            b = self.buf(jj(xx, yy))
            return b.at[:, pl.ds(self.ra, b.shape[1] - self.ra)]

        def g2(self):
            self.yp.wait_recv()
            late = self.late = used[0]
            used[0] += 1
            self.rp = copy_same(lambda: self.bpart(xl, ym).at[0], YP)
            self.bxm = copy_same(lambda: self.bpart(xl, ym), X, at=self.bx)
            copy_same(lambda: self.apart(xl, ym).at[0], YP, None, late)
            self.ym.wait_recv()
            self.rm = copy_same(lambda: self.bpart(xl, yp).at[1], YM)
            self.bxp = copy_same(lambda: self.bpart(xl, yp), X, at=self.bx)
            copy_same(lambda: self.apart(xl, yp).at[1], YM, None, late)

        def g3(self):
            self.xap.wait_recv()
            copy_same(lambda: self.buf(jj(xo, ym)).at[0, pl.ds(0, self.ra)], YP, None, self.late)
            self.xam.wait_recv()
            copy_same(lambda: self.buf(jj(xo, yp)).at[1, pl.ds(0, self.ra)], YM, None, self.late)

        def g4(self):
            self.rp.wait_recv()
            self.rm.wait_recv()
            self.bx2 = copy_same(lambda: self.bpart(xl, y2), X, at=self.bx)

        def g5(self):
            wait_bytes(self.late, self.two())
            wait_bytes(self.bx, self.four())

    own = jj(xl, y)
    u_out = copy(lambda: up_ref.at[:, pl.ds(pl.multiple_of(oc * BLK, 128), BLK)], lambda: U.at[own, c], C)
    gu = Gather(lambda j: U.at[j], RU, lambda: U.at[0:2, :, 0:RU], lambda: U.at[0:4, :, RU:192])
    gu.direct(True)
    tok_in = pltpu.make_async_copy(tok_ref, T.at[z], local.at[0])
    tok_in.start()
    u_in = pltpu.make_async_copy(up_ref.at[:, pl.ds(pl.multiple_of(c * BLK, 128), BLK)], U.at[own, c], local.at[1])
    u_in.start()
    d_in = pltpu.make_async_copy(
        downt_ref.at[:, :, pl.ds(pl.multiple_of(c * BLK, 128), BLK)], D.at[:, own, c], local.at[2]
    )
    d_in.start()

    tk = {}
    t_sems = used[0]
    used[0] += 12

    def tok(hop, p):
        rows = pl.ds(128 * p, 128)
        for q in range(2):
            if (q, hop - 1, p) in tk:
                tk[q, hop - 1, p].wait_recv()
        for q, sign, dev in ((0, -1, ZP), (1, 1, ZM)):
            if hop < 3 or hop == 3 and p == q:
                at = functools.partial(lambda k, rows: tok_ref.at[rows] if k is None else T.at[zz(k), rows], rows=rows)
                src = functools.partial(at, None if hop == 0 else sign * hop)
                tk[q, hop, p] = copy(src, functools.partial(at, sign * hop), dev, None, t_sems + 4 * p + 2 * q + hop % 2)

    st = {}

    def stats(hop):
        for q in range(2):
            if (q, hop - 1) in st:
                st[q, hop - 1].wait_recv()
        for q, sign, dev in ((0, -1, ZP), (1, 1, ZM)):
            if hop < 3 or hop == 3 and q == 0:
                st[q, hop] = copy_same(
                    functools.partial(lambda k: ST.at[zz(k)], sign * hop), dev, None, t_sems + 8 + 2 * q + hop % 2
                )

    def own_stats():
        x = T[z].astype(F32)
        m = jnp.sum(x, axis=-1, keepdims=True) * (1.0 / BLK)
        x = x - m
        sq = jnp.sum(x * x, axis=-1, keepdims=True)
        lane = lax.broadcasted_iota(jnp.int32, (SEQ, 128), 1)
        ST[z] = jnp.transpose(jnp.where(lane == 0, m, sq))[0:8]

    def all_stats():
        ms = [ST[b, 0:1] for b in range(NZ)]
        mean = ms[0]
        sq = ST[0, 1:2]
        for b in range(1, NZ):
            mean = mean + ms[b]
            sq = sq + ST[b, 1:2]
        mean = mean * (1.0 / NZ)
        apart = (ms[0] - mean) * (ms[0] - mean)
        for b in range(1, NZ):
            apart = apart + (ms[b] - mean) * (ms[b] - mean)
        rs = lax.rsqrt((sq + BLK * apart) * (1.0 / (NZ * BLK)) + 1e-06)
        MEAN[...] = jnp.transpose(jnp.broadcast_to(mean, (128, SEQ)))
        RSTD[...] = jnp.transpose(jnp.broadcast_to(rs, (128, SEQ)))

    n_sem = used[0]
    used[0] += 1

    def norm(k, p):
        b = zz(k)
        at = pl.ds(pl.multiple_of(b * BLK, 128), BLK)
        scale, shift = 1.0 + mod_ref[1:2, at], mod_ref[0:1, at]

        def tile(i, carry):
            rows = pl.ds(pl.multiple_of(128 * p + i * 32, 32), 32)
            m, rs = MEAN[rows], RSTD[rows]
            m, rs = jnp.concatenate([m] * 3, axis=1), jnp.concatenate([rs] * 3, axis=1)
            N[c, b, rows] = ((T[b, rows].astype(F32) - m) * rs * scale + shift).astype(BF)
            return carry

        lax.fori_loop(0, 4, tile, 0)
        copy_same(lambda: N.at[c, zz(k), pl.ds(128 * p, 128)], C, at=n_sem)

    gd = [
        Gather(
            functools.partial(lambda r, j: D.at[r, j], r), RA[r],
            functools.partial(lambda r: D.at[r, 0:2, :, 0:RA[r]], r),
            functools.partial(lambda r: D.at[r, 0:4, :, RA[r]:ROWS], r),
        )
        for r in range(R)
    ]

    tok(0, 0)
    u_out.wait_recv()
    gu.direct(False)
    tok_in.wait()
    own_stats()
    stats(0)
    tok(0, 1)
    d_out = copy(lambda: downt_ref.at[:, :, pl.ds(pl.multiple_of(oc * BLK, 128), BLK)], lambda: D.at[:, own, c], C)
    table_in.wait()
    step_copy.wait()
    counts_copy.wait()
    n = 3 * NZ * BLK // 128
    plan = TAB[step_ref[0]]
    for i in range(n):
        k, at = divmod(128 * i, NZ * BLK)
        mod_ref[k:k + 1, at:at + 128] = plan[i:i + 1]
    mod_out = copy(lambda: mod_ref, lambda: MODO, S)
    gate = mod_ref[2:3, pl.ds(pl.multiple_of(z * BLK, 128), BLK)]
    gate = jnp.transpose(jnp.broadcast_to(gate, (128, BLK)))
    GATE[:, 0:128] = gate
    GATE[:, 128:256] = gate

    def gate_of_student():
        mod_out.wait_recv()
        at = pl.ds(pl.multiple_of(z * BLK, 128), BLK)
        g = jnp.where(jnp.full((1, BLK), s) == 1, mod_ref[2:3, at], MODO[2:3, at])
        g = jnp.transpose(jnp.broadcast_to(g, (128, BLK)))
        GATEG[:, 0:128] = g
        GATEG[:, 128:256] = g

    tt = jnp.transpose(T[z].astype(F32))
    TOKT[...] = tt
    stats(1)
    tok(1, 0)
    gu.g1()
    tok(1, 1)
    stats(2)
    gu.g2()
    tok(2, 0)
    stats(3)
    tok(2, 1)
    d_in.wait()
    d_out.wait_recv()
    gu.g3()
    gd[3].g0()
    st[0, 3].wait_recv()
    all_stats()
    for k in (0, -1, 1):
        for p in range(2):
            norm(k, p)
    gu.g4()
    gd[1].g0()
    tok(3, 0)
    norm(-2, 0)
    norm(2, 0)
    tok(3, 1)
    norm(-2, 1)
    norm(2, 1)
    gd[0].g0()
    for k in (-3, 3):
        for p in range(2):
            norm(k, p)
    tok(4, 0)
    norm(4, 0)
    tok(4, 1)
    norm(4, 1)

    def hidden(img):
        h = nn(N[img, 0], U[0].reshape(BLK, BLK))
        for b in range(1, NZ):
            h = h + nn(N[img, b], U[b].reshape(BLK, BLK))
        HP[img] = h

        def act_rows(i, carry):
            rows = pl.ds(pl.multiple_of(i * 32, 32), 32)
            ACT[img, rows] = gelu(HP[img, rows]).astype(BF)
            return carry

        lax.fori_loop(0, SEQ // 32, act_rows, 0)

    def slopes(img):
        def rows_of_slope(i, carry):
            rows = pl.ds(pl.multiple_of(i * 32, 32), 32)
            SL[img, rows] = gelu_slope(HP[img, rows])
            return carry

        lax.fori_loop(0, SEQ // 32, rows_of_slope, 0)

    act_out = []

    def send_act(img):
        @pl.when(student)
        def _():
            act_out.append(copy(lambda: ACT.at[img()], lambda: ACTG.at[img()], S, 1))

    m_out, zs = {}, {}
    z_sems = used[0]
    used[0] += 4 * R

    def ring(r, q, k):
        return z_sems + 4 * r + 2 * q + k % 2


    def mixed(r):
        w = D[r].reshape(NZ * 2 * ROWS, BLK)
        PS[r] = nt(w, ACT[oc]).astype(BF)
        m_out[r] = copy(lambda: PS.at[r], lambda: PR.at[r], C)
        PO[r] = nt(w, ACT[c])

    def val(r, b):
        rows = pl.ds(pl.multiple_of(b * 2 * ROWS, 32), 2 * ROWS)
        return PO[r, rows] + PR[r, rows].astype(F32)

    def zstage(r, k):
        h0, h1 = pl.ds(0, ROWS), pl.ds(ROWS, ROWS)
        if k == 0:
            m_out[r].wait_recv()
            v = val(r, zz(4)).astype(BF)
            ZS[r, 0, 0] = v
            zs[r, 0, 0] = copy(lambda: ZS.at[r, 0, 0, h0], lambda: ZR.at[r, 0, 0, h0], ZP, None, ring(r, 0, 0))
            zs[r, 1, 0] = copy(lambda: ZS.at[r, 0, 0, h1], lambda: ZR.at[r, 1, 0, h1], ZM, None, ring(r, 1, 0))
            return
        for q in range(2):
            zs[r, q, k - 1].wait_recv()
        for q in range(2):
            v = val(r, zz((4 - k) if q == 0 else (k - 4)))
            if k == 1:
                h = slice(0, ROWS) if q == 0 else slice(ROWS, 2 * ROWS)
                g = slice(ROWS, 2 * ROWS) if q == 0 else slice(0, ROWS)
                ZS[r, q, k, h] = (v[h] + ZR[r, q, 0, h].astype(F32)).astype(BF)
                ZS[r, q, k, g] = v[g].astype(BF)
            else:
                ZS[r, q, k] = (v + ZR[r, q, k - 1].astype(F32)).astype(BF)
            at = functools.partial(lambda ref, q: ref.at[r, q, k], q=q)
            to = ZP if q == 0 else ZM
            zs[r, q, k] = copy(functools.partial(at, ZS), functools.partial(at, ZR), to, None, ring(r, q, k))

    sw = {}

    def rows_of(r, h):
        return slice(192 * h + ROWS * r, 192 * h + ROWS * (r + 1))

    def output(r):
        zs[r, 0, 3].wait_recv()
        zs[r, 1, 3].wait_recv()
        m = val(r, z) + ZR[r, 0, 3].astype(F32) + ZR[r, 1, 3].astype(F32)
        for h in range(2):
            w = rows_of(r, h)
            o = (TOKT[w] + GATE[w] * m[ROWS * h:ROWS * (h + 1)]).astype(BF)
            OTA[r, h] = o
            TOKT[w] = o.astype(F32)

        sw[r] = copy(lambda: OTA.at[r], lambda: OTB.at[r], S)

    ag, fw = {}, {}
    for r in range(R):
        fw[r] = used[0]
        used[0] += 1

    def gslice(r, img, b, h):
        n = ROWS if h is not None else 2 * ROWS
        return GT.at[r, img, pl.ds(pl.multiple_of(b * 2 * ROWS + (h or 0) * ROWS, 16), n)]

    def astage(r, k):
        def push(kk, dev, h=None, at=None):
            return copy_same(lambda: gslice(r, c, zz(kk), h), dev, None, fw[r] if at is None else at)

        if k == 0:
            sw[r].wait_recv()
            total = counts_ref[0]
            for i in range(1, 16):
                total = total + counts_ref[i]
            norm = jnp.sqrt(jnp.full((1, SEQ), total, jnp.int32).astype(F32))
            at = lax.broadcasted_iota(jnp.int32, (1, SEQ), 1)
            vrow = jnp.where(at < counts_ref[dp], (2 * s - 1).astype(F32), 0.0) / norm
            for h in range(2):
                w = rows_of(r, h)
                diff = OTA[r, h].astype(F32) - OTB[r, h].astype(F32)
                rows = pl.ds(pl.multiple_of(z * 2 * ROWS + h * ROWS, 16), ROWS)
                GT[r, c, rows] = (GATEG[w] * diff * vrow).astype(BF)
            ag[r, 0, 0] = push(0, ZP, at=ring(r, 0, 4))
            ag[r, 1, 0] = push(0, ZM, at=ring(r, 1, 4))
            push(0, C)
            return
        ag[r, 0, k - 1].wait_recv()
        ag[r, 1, k - 1].wait_recv()
        if k < 4:
            ag[r, 0, k] = push(-k, ZP, 0 if k > 2 else None, ring(r, 0, 4 + k))
        push(-k, C, None if k < 4 else 0)
        if k < 4:
            ag[r, 1, k] = push(k, ZM, 1 if k > 2 else None, ring(r, 1, 4 + k))
        push(k, C, None if k < 4 else 1)

    class Reduce:
        def __init__(self, i):
            self.i, self.a, self.b = i, slice(0, RA[i]), slice(RA[i], ROWS)
            self.ra, self.rb = pl.ds(0, RA[i]), pl.ds(0, ROWS - RA[i])
            self.r = lax.rem(i + 2 * (1 - s), R)

        def both(self, src, dst):
            at = used[0]
            used[0] += 1
            for h in range(2):
                copy(lambda: src().at[h], lambda: dst().at[h], (YP, YM)[h], None, at)
            return Whole(at, dst)

        def q(self, j, rows):
            return QV[self.r, j, :, rows]

        def r0(self):
            i, ra, rb = self.i, self.ra, self.rb
            for h in range(2):
                for x in range(2):
                    A2S[i, h, x, ra] = QV[self.r, jj(x, y2), h, self.a].astype(BF)
            self.a2 = self.both(lambda: A2S.at[i, :, :, ra], lambda: A2R.at[i, :, :, ra])
            for k in range(4):
                XBS[i, k, :, rb] = self.q(jj(xo, k), self.b).astype(BF)
            self.xb = copy(lambda: XBS.at[i, :, :, rb], lambda: XBR.at[i, :, :, rb], X)

        def r1(self):
            i, ra = self.i, self.ra
            self.a2.wait_recv()
            for h in range(2):
                for x in range(2):
                    v = self.q(jj(x, (yp, ym)[h]), self.a)
                    A1S[i, h, x, h, ra] = (v[h] + A2R[i, h, x, ra].astype(F32)).astype(BF)
                    A1S[i, h, x, 1 - h, ra] = v[1 - h].astype(BF)
            self.a1 = self.both(lambda: A1S.at[i, :, :, :, ra], lambda: A1R.at[i, :, :, :, ra])

        def r2(self):
            i, rb = self.i, self.rb
            self.xb.wait_recv()
            v = self.q(jj(xl, y2), self.b) + XBR[i, y2, :, rb].astype(F32)
            B2S[i, :, rb] = v.astype(BF)
            self.b2 = self.both(lambda: B2S.at[i, :, rb], lambda: B2R.at[i, :, rb])

        def r3(self):
            i, rb = self.i, self.rb
            self.b2.wait_recv()
            for h in range(2):
                yy = (yp, ym)[h]
                v = self.q(jj(xl, yy), self.b) + XBR[i, yy, :, rb].astype(F32)
                B1S[i, h, h, rb] = (v[h] + B2R[i, h, rb].astype(F32)).astype(BF)
                B1S[i, h, 1 - h, rb] = v[1 - h].astype(BF)
            self.b1 = self.both(lambda: B1S.at[i, :, :, rb], lambda: B1R.at[i, :, :, rb])

        def r4(self):
            i, ra = self.i, self.ra
            self.a1.wait_recv()
            v = self.q(jj(xo, y), self.a) + A1R[i, 0, xo, :, ra].astype(F32) + A1R[i, 1, xo, :, ra].astype(F32)
            AXS[i, :, ra] = v.astype(BF)
            self.ax = copy(lambda: AXS.at[i, :, ra], lambda: AXR.at[i, :, ra], X)

        def r5(self):
            i, ra, rb = self.i, self.ra, self.rb
            va = self.q(own, self.a) + A1R[i, 0, xl, :, ra].astype(F32) + A1R[i, 1, xl, :, ra].astype(F32)
            vb = self.q(own, self.b) + XBR[i, y, :, rb].astype(F32)
            self.b1.wait_recv()
            vb = vb + B1R[i, 0, :, rb].astype(F32) + B1R[i, 1, :, rb].astype(F32)
            self.ax.wait_recv()
            FO[i, :, self.a] = va + AXR[i, :, ra].astype(F32)
            FO[i, :, self.b] = vb
            FS[i] = FO[i, oc].astype(BF)
            self.f = copy(lambda: FS.at[i], lambda: FR.at[i], C)

        def r6(self):
            i = self.i
            self.f.wait_recv()
            if i < R // 2:
                HS[i, c] = FO[i, c].astype(BF)
                HS[i, oc] = FR[i]
                self.h = copy(lambda: HS.at[i], lambda: HR.at[i], S)
                return
            FO[i, oc] = FR[i].astype(F32)
            rows = slice(ROWS * (i - R // 2), ROWS * (i - R // 2 + 1))

            def keep(o):
                for h in range(2):
                    o[rows, BLK * h:BLK * (h + 1)] = FO[i, h]

            pl.when(student)(lambda: keep(ug_ref))
            pl.when(s == 0)(lambda: keep(dg_ref))

        def r7(self):
            i = self.i
            self.h.wait_recv()
            rows = slice(ROWS * i, ROWS * (i + 1))

            def keep(o):
                for h in range(2):
                    o[rows, BLK * h:BLK * (h + 1)] = HR[i, h].astype(F32)

            pl.when(student)(lambda: keep(dg_ref))
            pl.when(s == 0)(lambda: keep(ug_ref))

    red = [Reduce(i) for i in range(R)]

    def down_grads(r):
        g = [GT[r, 0], GT[r, 1]]
        q = nn(g[0], ACTG[0]) + nn(g[1], ACTG[1])
        QV[r] = q.reshape(NZ, 2, ROWS, BLK)

    def grad_act(r, first):
        w = D[r].reshape(NZ * 2 * ROWS, BLK)
        for img in range(2):
            v = tn(GT[r, img], w)
            if first:
                GA[img] = v
            else:
                GA[img] += v

    def arrived(r):
        wait_bytes(fw[r], GT.at[r, 0])

    def transposed(part):
        def one(i, carry):
            img, j = lax.div(i, 8), lax.rem(i, 8)
            t = jnp.transpose(N[img, j].astype(F32)).astype(BF)
            for r in range(R):
                for h in range(2):
                    NTR[r, img, pl.ds(pl.multiple_of(j * 2 * ROWS + h * ROWS, 16), ROWS)] = t[rows_of(r, h)]
            return carry

        lax.fori_loop(4 * part, 4 * part + 4, one, 0)

    def up_grads(r):
        q = nn(NTR[r, 0], GP[0]) + nn(NTR[r, 1], GP[1])
        QV[r] = q.reshape(NZ, 2, ROWS, BLK)

    summed = []

    def stage(n, k):
        if k < 4:
            zstage(n, k)
        elif k == 4:
            output(n)
        elif k < 10:
            astage(n, k - 5)
        else:
            arrived(n)
            first = not summed
            summed.append(n)
            pl.when(student)(lambda: grad_act(n, first))

            @pl.when(s == 0)
            def _():
                if first:
                    for d in act_out:
                        d.wait_recv()
                down_grads(n)

    def begin(n):
        if not begun:
            @pl.when(student)
            def _():
                for img in range(2):
                    GP[img] = (GA[img] * SL[img]).astype(BF)

        begun.append(n)
        pl.when(student)(lambda: up_grads(n))
        red[n].r0()

    u_in.wait()
    out_put = pltpu.make_async_copy(out_ref, out_to, local.at[6])
    begun, mixed_of, swapped, put = [], [], [], []
    gu.g5()
    for what, n in ORDER:
        if what == "hc":
            hidden(c)
        elif what == "ho":
            wait_bytes(n_sem, N.at[oc])
            hidden(oc)
        elif what[0] == "g":
            getattr(gd[n], what)()
        elif what == "m":
            mixed(n)
            mixed_of.append(n)
            if len(mixed_of) == R:
                send_act(lambda: c)
                send_act(lambda: oc)
        elif what == "tr":
            pl.when(student)(functools.partial(transposed, n))
        elif what == "sl":
            pl.when(student)(functools.partial(slopes, n))
        elif what[0] == "s":
            k = int(what[1:])
            if k == 5:
                if not swapped:
                    gate_of_student()
                swapped.append(n)
            stage(n, k)
            if k == 4:
                put.append(n)
                if len(put) == R:
                    out_ref[...] = jnp.transpose(TOKT[...]).astype(BF)
                    out_put.start()
        elif what == "b":
            begin(n)
        else:
            getattr(red[n], what)()

    out_put.wait()
    for d in started[None][-N_SEND[None]:]:
        d.wait_send()

    @pl.when(student)
    def _():
        for d in started[1][-N_SEND[1]:]:
            d.wait_send()


def shards(axes, tokens, up_weight, down_weight, mod_table, timesteps, valid_counts):
    table = mod_table.reshape(mod_table.shape[1], -1, 128)
    downt = down_weight[0].T.reshape(R, ROWS, 2 * BLK)

    v = pltpu.VMEM
    nred = R
    scratch = [
        v((SEQ, BLK), BF),
        v((NZ, SEQ, BLK), BF),
        v((NZ, 8, SEQ), F32),
        v((SEQ, 128), F32),
        v((SEQ, 128), F32),
        v((NZ, 2, 192, BLK), BF),
        v((R, NZ, 2, ROWS, BLK), BF),
        v((2, NZ, SEQ, BLK), BF),
        v((R, 2, NZ * 2 * ROWS, SEQ), BF),
        v((2, SEQ, BLK), F32),
        v((2, SEQ, BLK), F32),
        v((2, SEQ, BLK), BF),
        v((2, SEQ, BLK), BF),
        v((R, NZ * 2 * ROWS, SEQ), F32),
        v((R, NZ * 2 * ROWS, SEQ), BF),
        v((R, NZ * 2 * ROWS, SEQ), BF),
        v((R, 2, 4, 2 * ROWS, SEQ), BF),
        v((R, 2, 4, 2 * ROWS, SEQ), BF),
        v(table.shape, F32),
        pltpu.SMEM(timesteps.shape, jnp.int32),
        pltpu.SMEM(valid_counts.shape, jnp.int32),
        v((3, NZ * BLK), F32),
        v((3, NZ * BLK), F32),
        v((BLK, SEQ), F32),
        v((BLK, SEQ), F32),
        v((BLK, SEQ), F32),
        v((R, 2, ROWS, SEQ), BF),
        v((R, 2, ROWS, SEQ), BF),
        v((R, 2, NZ * 2 * ROWS, SEQ), BF),
        v((2, SEQ, BLK), F32),
        v((2, SEQ, BLK), BF),
        v((nred, NZ, 2, ROWS, BLK), F32),
        v((nred, 4, 2, 32, BLK), BF),
        v((nred, 4, 2, 32, BLK), BF),
        v((nred, 2, 2, 32, BLK), BF),
        v((nred, 2, 2, 32, BLK), BF),
        v((nred, 2, 2, 2, 32, BLK), BF),
        v((nred, 2, 2, 2, 32, BLK), BF),
        v((nred, 2, 32, BLK), BF),
        v((nred, 2, 32, BLK), BF),
        v((nred, 2, 2, 32, BLK), BF),
        v((nred, 2, 2, 32, BLK), BF),
        v((nred, 2, 32, BLK), BF),
        v((nred, 2, 32, BLK), BF),
        v((nred, ROWS, BLK), BF),
        v((nred, 2, ROWS, BLK), F32),
        v((nred, ROWS, BLK), BF),
        v((nred, 2, ROWS, BLK), BF),
        v((nred, 2, ROWS, BLK), BF),
        pltpu.SemaphoreType.DMA((sum(N_SEND.values()),)),
        pltpu.SemaphoreType.DMA((N_RECV,)),
        pltpu.SemaphoreType.DMA((7,)),
    ]
    hbm = pl.BlockSpec(memory_space=pl.ANY)
    vm = pl.BlockSpec(memory_space=pltpu.VMEM)
    out, up, down = pl.pallas_call(
        functools.partial(kernel, axes),
        out_shape=(
            jax.ShapeDtypeStruct((SEQ, BLK), BF),
            jax.ShapeDtypeStruct((96, 2 * BLK), F32),
            jax.ShapeDtypeStruct((96, 2 * BLK), F32),
        ),
        in_specs=[hbm] * 6,
        out_specs=(hbm, vm, vm),
        scratch_shapes=scratch,
        compiler_params=pltpu.CompilerParams(
            collective_id=0, has_side_effects=True, vmem_limit_bytes=67043328
        ),
    )(tokens, up_weight[0], downt, table, timesteps, valid_counts)
    def settle(*refs):
        came, sems = refs[6:9], refs[9]
        into = [pltpu.make_async_copy(refs[i], came[i], sems.at[i]) for i in range(3)]
        outof = [pltpu.make_async_copy(came[i], refs[3 + i], sems.at[3 + i]) for i in range(3)]
        for d in into:
            d.start()
        for d, e in zip(into, outof):
            d.wait()
            e.start()
        for e in outof:
            e.wait()

    shapes = [((SEQ, BLK), BF), ((96, 2 * BLK), F32), ((96, 2 * BLK), F32)]
    out, up, down = pl.pallas_call(
        settle,
        out_shape=tuple(jax.ShapeDtypeStruct(*i) for i in shapes),
        in_specs=[hbm] * 3,
        out_specs=(hbm,) * 3,
        scratch_shapes=[v(*i) for i in shapes] + [pltpu.SemaphoreType.DMA((6,))],
        compiler_params=pltpu.CompilerParams(vmem_limit_bytes=67043328),
    )(out, up, down)
    return out[None], up, down.T


def solution(mesh):
    placed = (
        P("dp", "mp"),
        P("side", "dp", "mp"),
        P("side", "mp", "dp"),
        P("side", None, None, None),
        P("dp"),
        P(),
    )
    return jax.shard_map(
        functools.partial(shards, mesh.axis_names),
        mesh=mesh,
        in_specs=placed,
        out_specs=(P("side", "dp", "mp"), P(("dp", "side"), "mp"), P("mp", ("dp", "side"))),
        check_vma=False,
    )
```
